32 devices in a mesh: dp: 4 (over y, x), row: 2 (over core), col: 4 (over z).
Axes of the slice: x: 2, y: 2, z: 4, core: 2. Of those that a mesh axis runs over, the one named last changes fastest.
Arguments:
- tokens: bfloat16 [16384, 1024], P(('dp', 'row'), 'col'), may hold values from -6 to 6
- segment_ids: int32 [16, 1024], P(('dp', 'row')), may hold values from 0 to 3, never falling along the last dimension, each value on 1 to 768 neighbouring positions
- w_qkv: bfloat16 [1024, 3, 1024], P('row', None, 'col'), may hold values from -0.25 to 0.25
- b_qv: bfloat16 [2, 1024], P(None, 'col'), may hold values from -3 to 3
- w_out: bfloat16 [1024, 1024], P('col', 'row'), may hold values from -0.75 to 0.75
- b_out: bfloat16 [1024], P('col'), may hold values from -3 to 3
- norm1_gain: bfloat16 [1024], P('col'), may hold values from 0.25 to 1.75
- norm1_shift: bfloat16 [1024], P('col'), may hold values from -3 to 3
- w_up: bfloat16 [1024, 4096], P('row', 'col'), may hold values from -0.1875 to 0.1875
- b_up: bfloat16 [4096], P('col'), may hold values from -3 to 3
- w_down: bfloat16 [4096, 1024], P('col', 'row'), may hold values from -0.09375 to 0.09375
- b_down: bfloat16 [1024], P('col'), may hold values from -3 to 3
- norm2_gain: bfloat16 [1024], P('col'), may hold values from 0.25 to 1.75
- norm2_shift: bfloat16 [1024], P('col'), may hold values from -3 to 3
- out_grad: bfloat16 [16384, 1024], P(('dp', 'row'), 'col'), may hold values from -6 to 6
Outputs:
- output: bfloat16 [16384, 1024], P(('dp', 'row'), 'col')
- in_grad: float32 [16384, 1024], P(('dp', 'row'), 'col')
- grad_w_qkv: float32 [1024, 3, 1024], P(('dp', 'row'), None, 'col')
- grad_b_qv: float32 [2, 1024], P(None, 'col')
- grad_w_out: float32 [1024, 1024], P('col', ('dp', 'row'))
- grad_b_out: float32 [1024], P('col')
- grad_norm1_gain: float32 [1024], P('col')
- grad_norm1_shift: float32 [1024], P('col')
- grad_w_up: float32 [1024, 4096], P(('dp', 'row'), 'col')
- grad_b_up: float32 [4096], P('col')
- grad_w_down: float32 [4096, 1024], P('col', ('dp', 'row'))
- grad_b_down: float32 [1024], P('col')
- grad_norm2_gain: float32 [1024], P('col')
- grad_norm2_shift: float32 [1024], P('col')
The draws below stay inside these ranges and needn't reach their ends.
Inputs may be any that keep to these rules, and one draw needn't show every extreme that they name: `segment_ids`: document numbers never fall along a sequence; a document holds at most 768 positions, and some document holds exactly that many.
All inputs are finite; a program needn't handle non-finite values.
Results may differ from the reference program's by a relative error of at most 0.013.
Values may be sent and summed in bfloat16 or wider, within the bound.
A program may use at most 128 MiB of HBM per device.

```python
import math
import jax
import jax.numpy as jnp
import numpy as np
from jax import lax

D = 1024
HEADS = 16
HEAD_DIM = 64
FF = 4096
SEQ = 1024
SEQUENCES = 16
TOKENS = 16384


def shard_levels(own_key, shape, cuts, least, largest):
    factor_of = 1.0
    for position, parts in cuts:
        heights = jax.random.uniform(jax.random.fold_in(jax.random.fold_in(own_key, 6), position), (parts,), jnp.float32, least / len(cuts), largest / len(cuts))
        factor_of = factor_of * jnp.repeat(jnp.exp(heights), shape[position] // parts).reshape((-1,) + (1,) * (len(shape) - 1 - position))
    return factor_of


def length_profile(count, total, limit, slope):
    weights = [(1 << 20) // math.isqrt(grade ** slope) + 1 for grade in range(2, count + 1)]
    surplus, holding = total - limit - (count - 1), [1] * (count - 1)
    while surplus > 0:
        movable = [i for i in range(count - 1) if holding[i] < limit]
        whole, remaining = sum([weights[i] for i in movable]), surplus
        for i in movable:
            addition = min(limit - holding[i], max(1, remaining * weights[i] // whole), surplus)
            holding[i] = holding[i] + addition
            surplus = surplus - addition
    return np.array([limit] + holding)


def uneven(key, amount, total, most, lean):
    if amount == 2:
        one = jax.random.randint(key, (), max(1, total - most), min(most, total - 1) + 1)
        return jnp.stack([one, total - one])
    sizes = jnp.asarray(length_profile(amount, total, most, lean), jnp.int32)
    pairs = (amount - 1) // 2
    donor, taker = sizes[1:1 + 2 * pairs:2], sizes[2:2 + 2 * pairs:2]
    slack = jnp.minimum(donor - 1, most - taker)
    passed = jax.random.randint(jax.random.fold_in(key, 1), (pairs,), 0, 1 << 20) % (slack + 1)
    sizes = sizes.at[1:1 + 2 * pairs:2].set(donor - passed).at[2:2 + 2 * pairs:2].set(taker + passed)
    return sizes[jax.random.permutation(jax.random.fold_in(key, 2), amount)]


def bell_draw(stream_key, extent, spread, limit, pieces=(), kind=jnp.bfloat16):
    result = spread * jax.random.normal(stream_key, extent, jnp.float32)
    if pieces:
        result = result * shard_levels(stream_key, extent, pieces, -0.22, 0.18)
    return jnp.clip(result, -limit, limit).astype(kind)


def setup_inputs(seed: int = 0) -> dict:
    streams_of = jax.random.split(jax.random.key(seed), 16)
    tokens = bell_draw(streams_of[0], (TOKENS, D), 1.0, 6.0, ((0, 8), (1, 4)))
    segment_ids = jax.vmap(lambda own: jnp.searchsorted(jnp.cumsum(uneven(own, 4, SEQ, SEQ * 3 // 4, 2)), jnp.arange(SEQ), side="right"))(jax.random.split(streams_of[1], SEQUENCES)).reshape((SEQUENCES, SEQ)).astype(jnp.int32)
    w_qkv = bell_draw(streams_of[2], (D, 3, D), (D // 2) ** -0.5, 0.25, ((0, 2), (2, 4)))
    b_qv = bell_draw(streams_of[3], (2, D), 0.5, 3.0, ((1, 4),))
    w_out = bell_draw(streams_of[4], (D, D), (D // 16) ** -0.5, 0.75, ((0, 4), (1, 2)))
    b_out = bell_draw(streams_of[5], (D,), 0.5, 3.0, ((0, 4),))
    norm1_gain = jnp.clip(1.0 + 0.15 * jax.random.normal(streams_of[6], (D,), jnp.float32), 0.25, 1.75).astype(jnp.bfloat16)
    norm1_shift = bell_draw(streams_of[7], (D,), 0.5, 3.0, ((0, 4),))
    w_up = bell_draw(streams_of[8], (D, FF), D ** -0.5, 0.1875, ((0, 2), (1, 4)))
    b_up = bell_draw(streams_of[9], (FF,), 0.5, 3.0, ((0, 4),))
    w_down = bell_draw(streams_of[10], (FF, D), FF ** -0.5, 0.09375, ((0, 4), (1, 2)))
    b_down = bell_draw(streams_of[11], (D,), 0.5, 3.0, ((0, 4),))
    norm2_gain = jnp.clip(1.0 + 0.15 * jax.random.normal(streams_of[12], (D,), jnp.float32), 0.25, 1.75).astype(jnp.bfloat16)
    norm2_shift = bell_draw(streams_of[13], (D,), 0.5, 3.0, ((0, 4),))
    out_grad = bell_draw(streams_of[14], (TOKENS, D), 1.0, 6.0, ((0, 8), (1, 4)))
    return dict(tokens=tokens, segment_ids=segment_ids, w_qkv=w_qkv, b_qv=b_qv, w_out=w_out, b_out=b_out, norm1_gain=norm1_gain, norm1_shift=norm1_shift, w_up=w_up, b_up=b_up, w_down=w_down, b_down=b_down, norm2_gain=norm2_gain, norm2_shift=norm2_shift, out_grad=out_grad)


@jax.custom_vjp
def low(v):
    return lax.optimization_barrier(v.astype(jnp.bfloat16)).astype(jnp.float32)

@jax.custom_vjp
def low_back(v):
    return v

def low_keep(v):
    return (low(v), None)

def low_pass(kept, grad):
    return (grad,)

def back_keep(v):
    return (v, None)

def back_low(kept, grad):
    return (low(grad),)
low.defvjp(low_keep, low_pass)
low_back.defvjp(back_keep, back_low)
NORM_EPSILON = 1e-05
HIGHEST_MODE = lax.Precision.HIGHEST

def normalize(residual, norm_gain, norm_shift):
    row_mean = lax.optimization_barrier(jnp.mean(residual, axis=-1, keepdims=True))
    centered = residual - row_mean
    row_var = lax.optimization_barrier(jnp.mean(centered * centered, axis=-1, keepdims=True))
    return centered * lax.rsqrt(row_var + NORM_EPSILON) * norm_gain + norm_shift

def attend_one(packed):
    queries, key_rows, value_rows, segments = packed
    score_scale = 1.0 / math.sqrt(HEAD_DIM)
    scores = jnp.einsum('qhd,khd->hqk', queries, key_rows, precision=HIGHEST_MODE) * score_scale
    scores = low_back(scores)
    same_doc = segments[:, None] == segments[None, :]
    scores = jnp.where(same_doc[None], scores, -1000000000.0)
    row_max = lax.optimization_barrier(jnp.max(scores, axis=-1, keepdims=True))
    exp_terms = jnp.exp(scores - row_max)
    attn_prob = exp_terms / lax.optimization_barrier(jnp.sum(exp_terms, axis=-1, keepdims=True))
    return jnp.einsum('hqk,khd->qhd', low(attn_prob), value_rows, precision=HIGHEST_MODE)

def encoder_layer(token_block, segments, w_qkv, b_qv, w_out, b_out, gain_one, shift_one, w_up, b_up, w_down, b_down, gain_two, shift_two):
    token_rows = token_block.shape[0]
    projected = jnp.einsum('td,dje->tje', token_block, w_qkv, precision=HIGHEST_MODE)
    queries = low(low_back(projected[:, 0]) + b_qv[0])
    key_rows = low(low_back(projected[:, 1]))
    value_rows = low(low_back(projected[:, 2]) + b_qv[1])
    split_shape = (token_rows // SEQ, SEQ, HEADS, HEAD_DIM)
    context = lax.map(jax.checkpoint(attend_one), (queries.reshape(split_shape), key_rows.reshape(split_shape), value_rows.reshape(split_shape), segments))
    context = low(low_back(context.reshape(token_rows, D)))
    residual_one = token_block + low_back(jnp.dot(context, w_out, precision=HIGHEST_MODE)) + b_out
    hidden_one = normalize(residual_one, gain_one, shift_one)
    up_proj = low_back(jnp.dot(low(hidden_one), w_up, precision=HIGHEST_MODE)) + b_up
    activated = low(jax.nn.gelu(up_proj, approximate=False))
    residual_two = hidden_one + low_back(jnp.dot(activated, w_down, precision=HIGHEST_MODE)) + b_down
    return normalize(residual_two, gain_two, shift_two)

def reference(tokens, segment_ids, w_qkv, b_qv, w_out, b_out, norm1_gain, norm1_shift, w_up, b_up, w_down, b_down, norm2_gain, norm2_shift, out_grad):
    group_size = 4
    group_count = SEQUENCES // group_size
    token_groups = tokens.astype(jnp.float32).reshape(group_count, group_size * SEQ, D)
    segment_groups = segment_ids.reshape(group_count, group_size, SEQ)
    parameters = tuple((weight.astype(jnp.float32) for weight in (w_qkv, b_qv, w_out, b_out, norm1_gain, norm1_shift, w_up, b_up, w_down, b_down, norm2_gain, norm2_shift)))
    checked_layer = jax.checkpoint(encoder_layer)

    def forward(token_blocks, *weights):

        def one_group(packed):
            return checked_layer(packed[0], packed[1], *weights)
        return lax.map(one_group, (token_blocks, segment_groups))
    outputs, pull_back = jax.vjp(forward, token_groups, *parameters)
    gradients = pull_back(out_grad.astype(jnp.float32).reshape(group_count, group_size * SEQ, D))
    output = outputs.reshape(TOKENS, D).astype(jnp.bfloat16)
    in_grad = gradients[0].reshape(TOKENS, D)
    return (output, in_grad, gradients[1], gradients[2], gradients[3], gradients[4], gradients[5], gradients[6], gradients[7], gradients[8], gradients[9], gradients[10], gradients[11], gradients[12])
```

```python
from functools import partial
import math

import jax
import jax.numpy as jnp
from jax import lax
from jax.experimental import pallas as pl
from jax.experimental.pallas import tpu as pltpu
from jax.sharding import Mesh, PartitionSpec as P

HEAD_DIM = 64
NORM_EPSILON = 1e-05
MESH = pl.DeviceIdType.MESH
LOG2E = math.log2(math.e)
BF = jnp.bfloat16
F32 = jnp.float32
CONTRACT_LAST = (((1,), (1,)), ((), ()))
CONTRACT_FIRST = (((0,), (0,)), ((), ()))
VMEM_LIMIT = 62 * 2**20


def wait_for(ref, sem):
    pltpu.make_async_copy(ref, ref, sem).wait()


def ds(start, size, multiple=128):
    return pl.ds(pl.multiple_of(start, multiple), size)


def gather_kernel(
    tok, og, par, wq, wo, wu, wd,
    xf, ogh, parf, wqf, wof, wuf, wdf,
    send_a, recv_a, send_b, recv_b, recv_l, send_l, send_t, recv_t, send_m, recv_m, send_g, recv_g, send_p, recv_p,
):
    d, r, c = lax.axis_index("dp"), lax.axis_index("core"), lax.axis_index("col")
    owner, j0 = c // 2, lax.rem(c, 2)
    half = tok.shape[0] // 4
    barrier = pltpu.get_barrier_semaphore()
    for s in range(4):
        for o in range(2):
            if s or o:
                target = {"core": lax.rem(r + o, 2), "col": lax.rem(c + s, 4)}
                pl.semaphore_signal(barrier, inc=1, device_id=target, device_id_type=MESH)
    peers = [lax.bitwise_xor(d, p) for p in (1, 2, 3)]
    for p in peers:
        pl.semaphore_signal(barrier, inc=1, device_id={"dp": p}, device_id_type=MESH)
    pl.semaphore_wait(barrier, 10)

    source, dest = (wq, wo, wu, wd), (wqf, wof, wuf, wdf)

    def whole(w, rr, j):
        rows, cols = source[w].shape
        if w in (0, 2):
            return dest[w].at[ds(rr * rows, rows), ds(j * cols, cols)]
        return dest[w].at[ds(j * rows, rows), ds(rr * cols, cols)]

    def piece(w, rr, dd, j):
        rows, cols = source[w].shape
        part = rows // 4
        if w in (0, 2):
            return dest[w].at[ds(rr * rows + dd * part, part, 64), ds(j * cols, cols)]
        return dest[w].at[ds(j * rows + dd * part, part, 64), ds(rr * cols, cols)]

    def a_copy(w, s):
        part = source[w].shape[0] // 4
        return pltpu.make_async_remote_copy(
            source[w].at[ds(d * part, part, 64)], piece(w, r, d, j0), send_a.at[w, s - 1], recv_a.at[w, j0 * 2 + r],
            device_id={"core": owner, "col": lax.rem(c + s, 4)}, device_id_type=MESH)

    def mate_part(w):
        return pltpu.make_async_remote_copy(
            source[w], whole(w, r, j0), send_l.at[w], recv_l.at[w], device_id={"core": 1 - r}, device_id_type=MESH)

    def start_a(w):
        for s in (2, 1, 3):
            a_copy(w, s).start()

        @pl.when(r == owner)
        def _():
            pltpu.make_async_copy(source[w], whole(w, r, j0), send_l.at[w]).start()

        @pl.when(r != owner)
        def _():
            mate_part(w).start()

    def token_copy(which, k, h, wait):
        src, dst = ((tok, xf), (og, ogh))[which]
        ssem = (send_t, send_g)[which].at[k * 2 + h]
        rsem = (recv_t, recv_g)[which].at[c]
        sref = src.at[pl.ds(k * 2 * half + h * half, half)]
        dref = dst.at[pl.ds(0, half), ds(c * 256, 256)]
        z = 2 * r + k
        me = jnp.logical_and(z == c, r == h)
        remote = pltpu.make_async_remote_copy(
            sref, dref, ssem, rsem, device_id={"core": h, "col": z}, device_id_type=MESH)
        if not wait:
            @pl.when(me)
            def _():
                pltpu.make_async_copy(sref, dref, rsem).start()

        @pl.when(jnp.logical_not(me))
        def _():
            remote.wait_send() if wait else remote.start()

    def mate_copy(q):
        src = xf.at[pl.ds(0, half), pl.ds(q * 256, 256)]
        dst = xf.at[pl.ds(half, half), pl.ds(q * 256, 256)]
        return pltpu.make_async_remote_copy(
            src, dst, send_m.at[q], recv_m.at[q], device_id={"core": 1 - r}, device_id_type=MESH)

    def par_copy(s):
        return pltpu.make_async_remote_copy(
            par, parf.at[:, ds(c * 256, 256)], send_p.at[s], recv_p.at[c],
            device_id={"col": lax.rem(c + s, 4)}, device_id_type=MESH)

    def b_copy(w, j, rr, p):
        ref = piece(w, rr, d, j)
        return pltpu.make_async_remote_copy(
            ref, ref, send_b.at[w, j * 2 + rr, p], recv_b.at[w, j * 2 + rr, p],
            device_id={"dp": peers[p]}, device_id_type=MESH)

    def b_step(w, j, rr):
        @pl.when(2 * r + j != c)
        def _():
            wait_for(piece(w, rr, d, j), recv_a.at[w, j * 2 + rr])
            for p in (2, 0, 1):
                b_copy(w, j, rr, p).start()

    start_a(0)
    for s in range(1, 4):
        par_copy(s).start()
    pltpu.make_async_copy(par, parf.at[:, ds(c * 256, 256)], recv_p.at[c]).start()
    for k in range(2):
        for h in range(2):
            token_copy(0, k, h, False)
    for j in range(2):
        for rr in range(2):
            b_step(0, j, rr)
    start_a(1)
    start_a(2)
    for q in range(4):
        wait_for(xf.at[pl.ds(0, half), pl.ds(q * 256, 256)], recv_t.at[q])
        mate_copy(q).start()
    start_a(3)
    for k in range(2):
        for h in range(2):
            token_copy(1, k, h, False)
    for w in (1, 2, 3):
        for j in range(2):
            for rr in range(2):
                b_step(w, j, rr)
    for s in range(1, 4):
        par_copy(s).wait_send()
    for q in range(4):
        wait_for(parf.at[:, pl.ds(q * 256, 256)], recv_p.at[q])
        mate_copy(q).wait_send()
        wait_for(xf.at[pl.ds(half, half), pl.ds(q * 256, 256)], recv_m.at[q])
        wait_for(ogh.at[:, pl.ds(q * 256, 256)], recv_g.at[q])
    for which in range(2):
        for k in range(2):
            for h in range(2):
                token_copy(which, k, h, True)
    for w in range(4):
        for s in (1, 2, 3):
            a_copy(w, s).wait_send()

        @pl.when(r == owner)
        def _():
            pltpu.make_async_copy(source[w], whole(w, r, j0), send_l.at[w]).wait()
            wait_for(whole(w, 1 - r, j0), recv_l.at[w])

        @pl.when(r != owner)
        def _():
            mate_part(w).wait_send()

        for j in range(2):
            @pl.when(2 * r + j != c)
            def _():
                for rr in range(2):
                    for p in range(3):
                        b_copy(w, j, rr, p).wait_send()
                        wait_for(piece(w, rr, peers[p], j), recv_b.at[w, j * 2 + rr, p])


def gather(tok, og, par, weights):
    dma = pltpu.SemaphoreType.DMA
    vmem, anywhere = pl.BlockSpec(memory_space=pltpu.VMEM), pl.BlockSpec(memory_space=pl.ANY)
    half, width = tok.shape[0] // 4, tok.shape[1] * 4
    out = [(2 * half, width), (half, width), (par.shape[0], width)]
    for w, weight in enumerate(weights):
        out.append((weight.shape[0] * 2, weight.shape[1] * 2))
    return pl.pallas_call(
        gather_kernel,
        out_shape=[jax.ShapeDtypeStruct(s, BF) for s in out],
        in_specs=[vmem] * 7,
        out_specs=[anywhere] * 7,
        scratch_shapes=[
            dma((4, 3)), dma((4, 4)), dma((4, 4, 3)), dma((4, 4, 3)), dma((4,)), dma((4,)), dma((4,)), dma((4,)),
            dma((4,)), dma((4,)), dma((4,)), dma((4,)), dma((4,)), dma((4,)),
        ],
        compiler_params=pltpu.CompilerParams(collective_id=0, has_side_effects=True, vmem_limit_bytes=VMEM_LIMIT),
        name="gather",
    )(tok, og, par, *weights)


def attend_kernel(q_ref, k_ref, v_ref, segq_ref, segk_ref, ctx_ref, lse_ref, *, scale):
    rows = 256
    length = q_ref.shape[0]
    seg_k = segk_ref[0:1, :]
    for h in range(2):
        lanes = slice(h * HEAD_DIM, (h + 1) * HEAD_DIM)
        k, v = k_ref[:, lanes], v_ref[:, lanes]
        for start in range(0, length, rows):
            q = q_ref[start : start + rows, lanes]
            s = lax.dot_general(q, k, CONTRACT_LAST, preferred_element_type=F32) * (scale * LOG2E)
            s = jnp.where(segq_ref[start : start + rows, 0:1] == seg_k, s, -1e9 * LOG2E)
            top = jnp.max(s, axis=1, keepdims=True)
            e = jnp.exp2(s - top)
            total = jnp.sum(e, axis=1, keepdims=True)
            ctx = jnp.dot(e.astype(BF), v, preferred_element_type=F32) / total
            ctx_ref[start : start + rows, lanes] = ctx.astype(BF)
            lse = top + jnp.log2(total)
            lse_ref[0, h : h + 1, start : start + rows] = jnp.transpose(jnp.broadcast_to(lse, (rows, 128)))[0:1, :]


def attend(qkv, seg_col, seg_row, scale):
    length = qkv.shape[0]
    pairs = qkv.shape[1] // 3 // 128
    per = pairs // 2

    def block(kind):
        return pl.BlockSpec((length, 128), lambda i: (0, (i // per) * 3 * per + kind * per + i % per))

    return pl.pallas_call(
        partial(attend_kernel, scale=scale),
        grid=(pairs,),
        out_shape=[jax.ShapeDtypeStruct((length, pairs * 128), BF), jax.ShapeDtypeStruct((pairs, 2, length), F32)],
        in_specs=[block(0), block(1), block(2), pl.BlockSpec((length, 128), lambda i: (0, 0)), pl.BlockSpec((8, length), lambda i: (0, 0))],
        out_specs=[pl.BlockSpec((length, 128), lambda i: (0, i)), pl.BlockSpec((1, 2, length), lambda i: (i, 0, 0))],
        compiler_params=pltpu.CompilerParams(vmem_limit_bytes=VMEM_LIMIT),
        name="attend",
    )(qkv, qkv, qkv, seg_col, seg_row)


def attend_back_kernel(q_ref, k_ref, v_ref, do_ref, ctx_ref, lse_ref, segk_ref, segq_ref, dq_ref, dk_ref, dv_ref, bq_ref, bv_ref, *, scale):
    rows = 256
    length = q_ref.shape[0]
    seg_q = segq_ref[0:1, :]
    prod = jnp.transpose(do_ref[...].astype(F32) * ctx_ref[...].astype(F32))
    for h in range(2):
        lanes = slice(h * HEAD_DIM, (h + 1) * HEAD_DIM)
        q, do = q_ref[:, lanes], do_ref[:, lanes]
        delta = jnp.sum(prod[h * HEAD_DIM : (h + 1) * HEAD_DIM], axis=0, keepdims=True)
        lse = lse_ref[0, h : h + 1, :]
        dqt = jnp.zeros((HEAD_DIM, length), F32)
        vsum = jnp.zeros((1, HEAD_DIM), F32)
        for start in range(0, length, rows):
            k = k_ref[start : start + rows, lanes]
            v = v_ref[start : start + rows, lanes]
            s = lax.dot_general(k, q, CONTRACT_LAST, preferred_element_type=F32) * (scale * LOG2E)
            s = jnp.where(segk_ref[start : start + rows, 0:1] == seg_q, s, -1e9 * LOG2E)
            p = jnp.exp2(s - lse)
            dp = lax.dot_general(v, do, CONTRACT_LAST, preferred_element_type=F32)
            g = (p * (dp - delta)).astype(BF)
            dk = jnp.dot(g, q, preferred_element_type=F32) * scale
            dk_ref[start : start + rows, lanes] = dk.astype(BF)
            dv = jnp.dot(p.astype(BF), do, preferred_element_type=F32)
            dv_ref[start : start + rows, lanes] = dv.astype(BF)
            vsum += jnp.sum(dv, axis=0, keepdims=True)
            dqt += jnp.dot(jnp.transpose(k), g, preferred_element_type=F32)
        dq = jnp.transpose(dqt) * scale
        dq_ref[:, lanes] = dq.astype(BF)
        bq_ref[0, :, lanes] = jnp.broadcast_to(jnp.sum(dq, axis=0, keepdims=True), (8, HEAD_DIM))
        bv_ref[0, :, lanes] = jnp.broadcast_to(vsum, (8, HEAD_DIM))


def attend_back(qkv, do, ctx, lse, seg_col, seg_row, scale):
    length = qkv.shape[0]
    pairs = qkv.shape[1] // 3 // 128
    per = pairs // 2

    def block(kind):
        return pl.BlockSpec((length, 128), lambda i: (0, (i // per) * 3 * per + kind * per + i % per))

    one = pl.BlockSpec((length, 128), lambda i: (0, i))
    small = pl.BlockSpec((1, 8, 128), lambda i: (i, 0, 0))
    return pl.pallas_call(
        partial(attend_back_kernel, scale=scale),
        grid=(pairs,),
        out_shape=[jax.ShapeDtypeStruct((length, pairs * 128), BF)] * 3 + [jax.ShapeDtypeStruct((pairs, 8, 128), F32)] * 2,
        in_specs=[
            block(0), block(1), block(2), one, one, pl.BlockSpec((1, 2, length), lambda i: (i, 0, 0)),
            pl.BlockSpec((length, 128), lambda i: (0, 0)), pl.BlockSpec((8, length), lambda i: (0, 0)),
        ],
        out_specs=[one, one, one, small, small],
        compiler_params=pltpu.CompilerParams(vmem_limit_bytes=VMEM_LIMIT),
        name="attend_back",
    )(qkv, qkv, qkv, do, ctx, lse, seg_col, seg_row)


def scatter_kernel(
    out_half, in_half, gq, go, gu, gd,
    outp, inp, rq, ro, ru, rd,
    r1q, r1o, r1u, r1d, s2q, s2o, s2u, s2d, r2q, r2o, r2u, r2d, s3q, s3o, s3u, s3d, r3q, r3o, r3u, r3d,
    send1, recv1, send2, recv2, send3, recv3, send_y, recv_y, send_i, recv_i,
):
    d, r, c = lax.axis_index("dp"), lax.axis_index("core"), lax.axis_index("col")
    a, b = d // 2, lax.rem(d, 2)
    barrier = pltpu.get_barrier_semaphore()
    for s in range(4):
        for o in range(2):
            if s or o:
                target = {"core": lax.rem(r + o, 2), "col": lax.rem(c + s, 4)}
                pl.semaphore_signal(barrier, inc=1, device_id=target, device_id_type=MESH)
    x_peer, y_peer = lax.bitwise_xor(d, 1), lax.bitwise_xor(d, 2)
    for p in (x_peer, y_peer):
        pl.semaphore_signal(barrier, inc=1, device_id={"dp": p}, device_id_type=MESH)
    pl.semaphore_wait(barrier, 9)

    grads = (gq, go, gu, gd)
    first, second = (r1q, r1o, r1u, r1d), (r2q, r2o, r2u, r2d)
    out2, out3 = (s2q, s2o, s2u, s2d), (s3q, s3o, s3u, s3d)
    third, result = (r3q, r3o, r3u, r3d), (rq, ro, ru, rd)
    by_rows = (True, False, True, False)

    def local(w, j, slab):
        rows, cols = grads[w].shape
        if by_rows[w]:
            return grads[w].at[ds(slab * (rows // 4), rows // 4), pl.ds(j * (cols // 2), cols // 2)]
        return grads[w].at[pl.ds(j * (rows // 2), rows // 2), ds(slab * (cols // 4), cols // 4)]

    def slab_of(j, i, mine):
        if j == 0:
            return i * 2 + (b if mine else 1 - b)
        return (a if mine else 1 - a) * 2 + i

    def copy1(w, j, i):
        return pltpu.make_async_remote_copy(
            local(w, j, slab_of(j, i, False)), first[w].at[j, i], send1.at[w, j, i], recv1.at[w, j, i],
            device_id={"dp": x_peer if j == 0 else y_peer}, device_id_type=MESH)

    def copy2(w, j):
        return pltpu.make_async_remote_copy(
            out2[w].at[j], second[w].at[j], send2.at[w, j], recv2.at[w, j],
            device_id={"dp": y_peer if j == 0 else x_peer}, device_id_type=MESH)

    def part3(w, j, rr):
        if by_rows[w]:
            return out3[w].at[j, pl.ds(rr * 128, 128), :]
        return out3[w].at[j, :, pl.ds(rr * 128, 128)]

    def copy3(w, j, rr, wait):
        dst = third[w].at[c]
        z = 2 * r + j
        me = jnp.logical_and(z == c, r == rr)
        remote = pltpu.make_async_remote_copy(
            part3(w, j, rr), dst, send3.at[w, j, rr], recv3.at[w, c],
            device_id={"core": rr, "col": z}, device_id_type=MESH)
        if not wait:
            @pl.when(me)
            def _():
                pltpu.make_async_copy(part3(w, j, rr), dst, recv3.at[w, c]).start()

        @pl.when(jnp.logical_not(me))
        def _():
            remote.wait_send() if wait else remote.start()

    def keep(j):
        return a if j == 0 else b

    def step2(w, j):
        give = 1 - keep(j)
        for i in range(2):
            wait_for(first[w].at[j, i], recv1.at[w, j, i])
        n = first[w].shape[2]
        src = local(w, j, slab_of(j, give, True))

        def body(t, carry):
            rows = ds(t * 64, 64, 64)
            out2[w][j, rows, :] = (src[rows, :].astype(F32) + first[w][j, give, rows, :].astype(F32)).astype(BF)
            return carry
        lax.fori_loop(0, n // 64, body, 0)
        copy2(w, j).start()

    def step3(w, j):
        wait_for(second[w].at[j], recv2.at[w, j])
        n = first[w].shape[2]
        src = local(w, j, slab_of(j, keep(j), True))

        def body(t, carry):
            rows = ds(t * 64, 64, 64)
            value = src[rows, :].astype(F32) + first[w][j, keep(j), rows, :].astype(F32) + second[w][j, rows, :].astype(F32)
            out3[w][j, rows, :] = value.astype(BF)
            return carry
        lax.fori_loop(0, n // 64, body, 0)
        for rr in range(2):
            copy3(w, j, rr, False)

    def finish(w):
        for z in range(4):
            wait_for(third[w].at[z], recv3.at[w, z])
        n = third[w].shape[1]

        def body(t, carry):
            rows = ds(t * 64, 64, 64)
            value = (third[w][0, rows, :].astype(F32) + third[w][1, rows, :].astype(F32)) + (
                third[w][2, rows, :].astype(F32) + third[w][3, rows, :].astype(F32))
            result[w][rows, :] = value
            return carry
        lax.fori_loop(0, n // 64, body, 0)

    half = out_half.shape[0]

    def token_copy(which, q, wait):
        src, dst = ((out_half, outp), (in_half, inp))[which]
        ssem, rsem = ((send_y, recv_y), (send_i, recv_i))[which]
        rr, k = c // 2, lax.rem(c, 2)
        sref = src.at[:, pl.ds(q * 256, 256)]
        dref = dst.at[ds(k * 2 * half + r * half, half)]
        sem = rsem.at[k * 2 + r]
        me = jnp.logical_and(rr == r, q == c)
        remote = pltpu.make_async_remote_copy(
            sref, dref, ssem.at[q], sem, device_id={"core": rr, "col": q}, device_id_type=MESH)
        if not wait:
            @pl.when(me)
            def _():
                pltpu.make_async_copy(sref, dref, sem).start()

        @pl.when(jnp.logical_not(me))
        def _():
            remote.wait_send() if wait else remote.start()

    order = (3, 2, 1, 0)
    for w in order:
        for i in range(2):
            for j in range(2):
                copy1(w, j, i).start()
    for q in range(4):
        token_copy(0, q, False)
        token_copy(1, q, False)
    for w in order:
        for j in range(2):
            step2(w, j)
        if w < 3:
            for j in range(2):
                step3(w + 1, j)
    for j in range(2):
        step3(0, j)
    for w in order:
        finish(w)
    for w in order:
        for j in range(2):
            for i in range(2):
                copy1(w, j, i).wait_send()
                copy3(w, j, i, True)
            copy2(w, j).wait_send()
    for which in range(2):
        for q in range(4):
            token_copy(which, q, True)
            dst, rsem = ((outp, recv_y), (inp, recv_i))[which]
            wait_for(dst.at[pl.ds(q * half, half)], rsem.at[q])


def scatter(out_half, in_half, grads):
    dma = pltpu.SemaphoreType.DMA
    vmem = pl.BlockSpec(memory_space=pltpu.VMEM)
    half, width = out_half.shape
    out, r1, r2, r3 = [((4 * half, width // 4), BF)] * 2, [], [], []
    for w, g in enumerate(grads):
        rows, cols = g.shape
        if w in (0, 2):
            out.append(((rows // 8, cols // 2), F32))
            r1.append((2, 2, rows // 4, cols // 2))
            r2.append((2, rows // 4, cols // 2))
            r3.append((4, rows // 8, cols // 2))
        else:
            out.append(((rows // 2, cols // 8), F32))
            r1.append((2, 2, rows // 2, cols // 4))
            r2.append((2, rows // 2, cols // 4))
            r3.append((4, rows // 2, cols // 8))
    return pl.pallas_call(
        scatter_kernel,
        out_shape=[jax.ShapeDtypeStruct(s, t) for s, t in out],
        in_specs=[vmem] * 6,
        out_specs=[vmem] * 6,
        scratch_shapes=[pltpu.VMEM(s, BF) for s in r1 + r2 + r2 + r2 + r3]
        + [dma((4, 2, 2)), dma((4, 2, 2)), dma((4, 2)), dma((4, 2)), dma((4, 2, 2)), dma((4, 4)), dma((4,)), dma((4,)), dma((4,)), dma((4,))],
        compiler_params=pltpu.CompilerParams(collective_id=1, has_side_effects=True, vmem_limit_bytes=VMEM_LIMIT),
        name="scatter",
    )(out_half, in_half, *grads)


def swap(values):
    return lax.ppermute(values, "core", [(0, 1), (1, 0)])


def both(own):
    return jnp.concatenate([own, swap(own)], axis=0)


def normalize(residual, gain, shift):
    mean = jnp.mean(residual, axis=1, keepdims=True)
    centered = residual - mean
    inverse = lax.rsqrt(jnp.mean(centered * centered, axis=1, keepdims=True) + NORM_EPSILON)
    normed = centered * inverse
    return normed * gain + shift, normed, inverse


def normalize_back(incoming, normed, inverse, gain):
    scaled = incoming * gain
    first = jnp.mean(scaled, axis=1, keepdims=True)
    second = jnp.mean(scaled * normed, axis=1, keepdims=True)
    grad = inverse * (scaled - first - normed * second)
    return grad, jnp.sum(incoming * normed, axis=0), jnp.sum(incoming, axis=0)


def mm(left, right, dims=(((1,), (0,)), ((), ()))):
    return lax.dot_general(left, right, dims, preferred_element_type=F32)


def join_rows(values, groups):
    if groups == 1:
        return values
    rows, cols = values.shape
    return values.reshape(2, groups, rows // (2 * groups), cols).transpose(1, 0, 2, 3).reshape(rows, cols)


def part_rows(values, groups):
    if groups == 1:
        return values
    rows, cols = values.shape
    return values.reshape(4, groups, 2, rows // (8 * groups), cols).transpose(0, 2, 1, 3, 4).reshape(rows, cols)


def on_device(
    tokens, segment_ids, w_qkv, b_qv, w_out, b_out, norm1_gain, norm1_shift,
    w_up, b_up, w_down, b_down, norm2_gain, norm2_shift, out_grad,
):
    groups = lax.axis_size("rh")
    core, col = lax.axis_index("core"), lax.axis_index("col")
    part = tokens.shape[1]
    length = segment_ids.shape[1]
    half = length // 2
    scale = 1.0 / math.sqrt(HEAD_DIM)
    wq, wo, wu, wd = w_qkv.reshape(w_qkv.shape[0], 3 * part), w_out, w_up, w_down
    if groups > 1:
        wq, wu = (lax.all_gather(w, "rh", axis=0, tiled=True) for w in (wq, wu))
        wo, wd = (lax.all_gather(w, "rh", axis=1, tiled=True) for w in (wo, wd))
    par = jnp.concatenate(
        [b_qv, b_out[None], norm1_gain[None], norm1_shift[None], b_down[None], norm2_gain[None], norm2_shift[None],
         b_up.reshape(4, part), jnp.zeros((4, part), BF)], axis=0)
    x, og, params, wq, wo, wu, wd = gather(tokens, out_grad, par, (wq, wo, wu, wd))
    wq, wu = join_rows(wq, groups), join_rows(wu, groups)
    wo, wd = join_rows(wo.T, groups).T if groups > 1 else wo, join_rows(wd.T, groups).T if groups > 1 else wd
    wo_mate = swap(wo)
    params = params.astype(F32)
    mine = lax.dynamic_slice_in_dim(params, core * 2 * part, 2 * part, 1)
    zeros = jnp.zeros((part,), F32)
    bias_qkv = jnp.concatenate([mine[0, :part], zeros, mine[1, :part], mine[0, part:], zeros, mine[1, part:]])
    bias_up = mine[8:12].reshape(4, 2, part).transpose(1, 0, 2).reshape(-1)
    bias_out, gain1, shift1, bias_down, gain2, shift2 = (params[i] for i in range(2, 8))

    seqs = lax.all_gather(segment_ids, "core", axis=0, tiled=True)
    seg = lax.dynamic_index_in_dim(seqs, col, 0, False)
    seg = jnp.concatenate([lax.dynamic_slice_in_dim(seg, core * half, half), lax.dynamic_slice_in_dim(seg, (1 - core) * half, half)])
    seg_col = jnp.broadcast_to(seg[:, None], (length, 128))
    seg_row = jnp.broadcast_to(seg[None], (8, length))

    qkv = (mm(x, wq) + bias_qkv).astype(BF)
    ctx, lse = attend(qkv, seg_col, seg_row, scale)
    ctx_mate = swap(ctx[half:])
    residual_one = x[:half].astype(F32) + (mm(ctx[:half], wo) + mm(ctx_mate, wo_mate)) + bias_out
    hidden_one, normed_one, inverse_one = normalize(residual_one, gain1, shift1)
    hidden = both(hidden_one.astype(BF))
    up_proj = mm(hidden, wu) + bias_up
    gate = 0.5 * (1.0 + lax.erf(up_proj * math.sqrt(0.5)))
    activated = (up_proj * gate).astype(BF)
    down = mm(activated, wd)
    residual_two = hidden_one + (down[:half] + swap(down[half:])) + bias_down
    output, normed_two, inverse_two = normalize(residual_two, gain2, shift2)
    two_grad, gain2_grad, shift2_grad = normalize_back(og.astype(F32), normed_two, inverse_two, gain2)
    mix = both(two_grad.astype(BF))
    down_wgrad = mm(activated, mix, CONTRACT_FIRST).astype(BF)
    slope = gate + up_proj * (math.sqrt(0.5 / math.pi) * jnp.exp(-0.5 * up_proj * up_proj))
    up_grad = mm(mix, wd, CONTRACT_LAST) * slope
    up_low = up_grad.astype(BF)
    up_bias_grad = jnp.sum(up_grad, axis=0)
    up_wgrad = mm(hidden, up_low, CONTRACT_FIRST).astype(BF)
    hidden_grad = mm(up_low, wu, CONTRACT_LAST)
    hidden_grad = hidden_grad[:half] + swap(hidden_grad[half:]) + two_grad
    one_grad, gain1_grad, shift1_grad = normalize_back(hidden_grad, normed_one, inverse_one, gain1)
    attn = both(one_grad.astype(BF))
    out_wgrad = mm(ctx, attn, CONTRACT_FIRST).astype(BF)
    ctx_grad = mm(attn, wo, CONTRACT_LAST).astype(BF)
    dq, dk, dv, bq, bv = attend_back(qkv, ctx_grad, ctx, lse, seg_col, seg_row, scale)
    low = jnp.concatenate([dq[:, :part], dk[:, :part], dv[:, :part], dq[:, part:], dk[:, part:], dv[:, part:]], axis=1)
    qkv_wgrad = mm(x, low, CONTRACT_FIRST).astype(BF)
    in_part = mm(low, wq, CONTRACT_LAST)
    in_half = (in_part[:half] + swap(in_part[half:]) + one_grad).astype(BF)

    qkv_wgrad, up_wgrad = part_rows(qkv_wgrad, groups), part_rows(up_wgrad, groups)
    if groups > 1:
        out_wgrad, down_wgrad = part_rows(out_wgrad.T, groups).T, part_rows(down_wgrad.T, groups).T
    output, in_grad, qkv_share, out_share, up_share, down_share = scatter(
        output.astype(BF), in_half, (qkv_wgrad, out_wgrad, up_wgrad, down_wgrad))
    if groups > 1:
        qkv_share, up_share = (lax.psum_scatter(g, "rh", scatter_dimension=0, tiled=True) for g in (qkv_share, up_share))
        out_share, down_share = (lax.psum_scatter(g, "rh", scatter_dimension=1, tiled=True) for g in (out_share, down_share))

    full = jnp.stack([jnp.sum(one_grad, axis=0), gain1_grad, shift1_grad, jnp.sum(two_grad, axis=0), gain2_grad, shift2_grad])
    owned = jnp.concatenate([bq[:, 0].reshape(1, -1), bv[:, 0].reshape(1, -1), up_bias_grad.reshape(2, 4, part).transpose(1, 0, 2).reshape(4, -1)], axis=0)
    owned = lax.dynamic_update_slice_in_dim(jnp.zeros((6, 4 * part), F32), owned, core * 2 * part, 1)
    sums = lax.psum(jnp.concatenate([full, owned], axis=0), ("dp", "rh", "core", "col"))
    sums = lax.dynamic_slice_in_dim(sums, col * part, part, 1)
    return (
        output,
        in_grad.astype(F32),
        qkv_share.reshape(qkv_share.shape[0], 3, part),
        sums[6:8],
        out_share,
        sums[0],
        sums[1],
        sums[2],
        up_share,
        sums[8:12].reshape(-1),
        down_share,
        sums[3],
        sums[4],
        sums[5],
    )


def solution(mesh):
    dp, row, col = (mesh.shape[name] for name in ("dp", "row", "col"))
    fine = Mesh(mesh.devices.reshape(dp, row // 2, 2, col), ("dp", "rh", "core", "col"))
    row, every = ("rh", "core"), ("dp", "rh", "core")
    return jax.shard_map(
        on_device,
        mesh=fine,
        in_specs=(
            P(every, "col"), P(every, None), P(row, None, "col"), P(None, "col"), P("col", row), P("col"), P("col"), P("col"),
            P(row, "col"), P("col"), P("col", row), P("col"), P("col"), P("col"), P(every, "col"),
        ),
        out_specs=(
            P(every, "col"), P(every, "col"), P(every, None, "col"), P(None, "col"), P("col", every), P("col"), P("col"),
            P("col"), P(every, "col"), P("col"), P("col", every), P("col"), P("col"), P("col"),
        ),
        check_vma=False,
    )
```

```python
from functools import partial
import math

import jax
import jax.numpy as jnp
from jax import lax
from jax.experimental import pallas as pl
from jax.experimental.pallas import tpu as pltpu
from jax.sharding import Mesh, PartitionSpec as P

HEAD_DIM = 64
NORM_EPSILON = 1e-05
MESH = pl.DeviceIdType.MESH
LOG2E = math.log2(math.e)
BF = jnp.bfloat16
F32 = jnp.float32
CONTRACT_LAST = (((1,), (1,)), ((), ()))
CONTRACT_FIRST = (((0,), (0,)), ((), ()))
VMEM_LIMIT = 62 * 2**20


def wait_for(ref, sem):
    pltpu.make_async_copy(ref, ref, sem).wait()


def ds(start, size, multiple=128):
    return pl.ds(pl.multiple_of(start, multiple), size)


def normalize(residual, gain, shift):
    mean = jnp.mean(residual, axis=1, keepdims=True)
    centered = residual - mean
    inverse = lax.rsqrt(jnp.mean(centered * centered, axis=1, keepdims=True) + NORM_EPSILON)
    normed = centered * inverse
    return normed * gain + shift, normed, inverse


def gather_kernel(
    tok, og, par, seg, wq, wo, wu, wd,
    parf, lse, segc, segr, inverse, vec,
    x_out, wq_out, wo_out, wu_out, wd_out, qkv_out, ctx_out, normed_out, hidden_out, act_out, slope_out, out_half, two_out, mix_out,
    xf, wqf, wof, wuf, wdf, qkv, ctx, normed, hidden, act, slope, outh, two, mix,
    ogh, wom, ctxm, hidden_one, mate_out, mate_in, segs, tq, tk, tv, tc,
    send_a, recv_a, send_f, send_b, recv_b, send_c, recv_c, recv_l, send_l, send_t, recv_t, send_g, recv_g, send_m, recv_m, send_p, recv_p,
    send_s, recv_s, send_x, recv_x, store,
    *, scale,
):
    d, r, c = lax.axis_index("dp"), lax.axis_index("core"), lax.axis_index("col")
    owner, j0 = c // 2, lax.rem(c, 2)
    half = tok.shape[0] // 4
    barrier = pltpu.get_barrier_semaphore()
    for s in range(4):
        for o in range(2):
            if s or o:
                target = {"core": lax.rem(r + o, 2), "col": lax.rem(c + s, 4)}
                pl.semaphore_signal(barrier, inc=1, device_id=target, device_id_type=MESH)
    x_peer, y_peer, far = (lax.bitwise_xor(d, p) for p in (1, 2, 3))
    peers = (x_peer, y_peer)
    for p in peers:
        pl.semaphore_signal(barrier, inc=1, device_id={"dp": p}, device_id_type=MESH)
    pl.semaphore_wait(barrier, 9)

    source, dest = (wq, wo, wu, wd), (wqf, wof, wuf, wdf)

    def whole(w, rr, j):
        rows, cols = source[w].shape
        if w in (0, 2):
            return dest[w].at[ds(rr * rows, rows), ds(j * cols, cols)]
        return dest[w].at[ds(j * rows, rows), ds(rr * cols, cols)]

    def piece(w, rr, dd, j, part=None):
        rows, cols = source[w].shape
        size = rows // 4
        base = (rr if w in (0, 2) else j) * rows + dd * size
        if part is not None:
            size = size // 2
            base = base + part * size
        return dest[w].at[ds(base, size, 32), ds((j if w in (0, 2) else rr) * cols, cols)]

    def a_copy(w, up):
        size = source[w].shape[0] // 4
        return pltpu.make_async_remote_copy(
            source[w].at[ds(d * size, size, 64)], piece(w, r, d, j0), send_a.at[w, up], recv_a.at[w, j0 * 2 + r],
            device_id={"core": owner, "col": lax.rem(c + (1 if up else 3), 4)}, device_id_type=MESH)

    def outer(up):
        return c < 3 if up else c > 0

    def mate_part(w):
        return pltpu.make_async_remote_copy(
            source[w], whole(w, r, j0), send_l.at[w], recv_l.at[w], device_id={"core": 1 - r}, device_id_type=MESH)

    def start_a(w):
        for up in (0, 1):
            @pl.when(outer(up))
            def _():
                a_copy(w, up).start()

        @pl.when(r == owner)
        def _():
            pltpu.make_async_copy(source[w], whole(w, r, j0), send_l.at[w]).start()

        @pl.when(r != owner)
        def _():
            mate_part(w).start()

    def token_copy(which, k, h, wait):
        src, dst = ((tok, xf), (og, ogh))[which]
        ssem = (send_t, send_g)[which].at[k * 2 + h]
        rsem = (recv_t, recv_g)[which].at[c]
        sref = src.at[pl.ds(k * 2 * half + h * half, half)]
        dref = dst.at[pl.ds(0, half), ds(c * 256, 256)]
        z = 2 * r + k
        me = jnp.logical_and(z == c, r == h)
        remote = pltpu.make_async_remote_copy(
            sref, dref, ssem, rsem, device_id={"core": h, "col": z}, device_id_type=MESH)
        if not wait:
            @pl.when(me)
            def _():
                pltpu.make_async_copy(sref, dref, rsem).start()

        @pl.when(jnp.logical_not(me))
        def _():
            remote.wait_send() if wait else remote.start()

    def mate_copy(q):
        src = xf.at[pl.ds(0, half), pl.ds(q * 256, 256)]
        dst = xf.at[pl.ds(half, half), pl.ds(q * 256, 256)]
        return pltpu.make_async_remote_copy(
            src, dst, send_m.at[q], recv_m.at[q], device_id={"core": 1 - r}, device_id_type=MESH)

    def par_copy(s):
        return pltpu.make_async_remote_copy(
            par, parf.at[:, ds(c * 256, 256)], send_p.at[s], recv_p.at[c],
            device_id={"col": lax.rem(c + s, 4)}, device_id_type=MESH)

    def forward(w, j, rr, up, wait):
        origin = 2 * r + j
        ref = piece(w, rr, d, j)
        copy = pltpu.make_async_remote_copy(
            ref, ref, send_f.at[w, j * 2 + rr], recv_a.at[w, j * 2 + rr],
            device_id={"col": lax.rem(c + (1 if up else 3), 4)}, device_id_type=MESH)

        @pl.when(jnp.logical_and(origin < c if up else origin > c, outer(up)))
        def _():
            copy.wait_send() if wait else copy.start()

    def b_copy(w, j, rr, p):
        ref = piece(w, rr, d, j)
        return pltpu.make_async_remote_copy(
            ref, ref, send_b.at[w, j * 2 + rr, p], recv_b.at[w, j * 2 + rr, p],
            device_id={"dp": peers[p]}, device_id_type=MESH)

    def c_copy(w, j, rr, p):
        ref = piece(w, rr, peers[p], j, p)
        return pltpu.make_async_remote_copy(
            ref, ref, send_c.at[w, j * 2 + rr, p], recv_c.at[w, j * 2 + rr, p],
            device_id={"dp": peers[1 - p]}, device_id_type=MESH)

    def b_step(w, near, rr):
        j = 1 - r if near else r

        @pl.when(2 * r + j != c)
        def _():
            wait_for(piece(w, rr, d, j), recv_a.at[w, j * 2 + rr])
            for up in (0, 1):
                forward(w, j, rr, up, False)
            for p in range(2):
                b_copy(w, j, rr, p).start()

    def c_step(w, near, rr):
        j = 1 - r if near else r

        @pl.when(2 * r + j != c)
        def _():
            for p in range(2):
                wait_for(piece(w, rr, peers[p], j), recv_b.at[w, j * 2 + rr, p])
                c_copy(w, j, rr, p).start()

    def finish_weight(w):
        @pl.when(r == owner)
        def _():
            wait_for(whole(w, r, j0), send_l.at[w])
            wait_for(whole(w, 1 - r, j0), recv_l.at[w])

        for j in range(2):
            @pl.when(2 * r + j != c)
            def _():
                for rr in range(2):
                    for p in range(2):
                        wait_for(piece(w, rr, far, j, p), recv_c.at[w, j * 2 + rr, p])

    seg_send = pltpu.make_async_remote_copy(
        seg, segs.at[r], send_s.at[0], recv_s.at[r], device_id={"core": 1 - r}, device_id_type=MESH)
    seg_own = pltpu.make_async_copy(seg, segs.at[r], recv_s.at[r])
    start_a(0)
    for s in range(1, 4):
        par_copy(s).start()
    pltpu.make_async_copy(par, parf.at[:, ds(c * 256, 256)], recv_p.at[c]).start()
    seg_send.start()
    seg_own.start()
    steps = [(w, near, rr) for w in range(4) for near in (1, 0) for rr in range(2)]
    lag = 3

    def advance(i):
        b_step(*steps[i])
        if i >= lag:
            c_step(*steps[i - lag])
        if i == 1:
            start_a(1)
        if i == 3:
            for k in range(2):
                for h in range(2):
                    token_copy(0, k, h, False)
            start_a(2)
        if i == 7:
            start_a(3)
        if i == 15:
            for k in range(2):
                for h in range(2):
                    token_copy(1, k, h, False)

    for i in range(8):
        advance(i)
    for q in range(4):
        wait_for(xf.at[pl.ds(0, half), pl.ds(q * 256, 256)], recv_t.at[q])
        mate_copy(q).start()
    for rr in range(2):
        wait_for(segs.at[rr], recv_s.at[rr])
    length, part = xf.shape[0], wqf.shape[1] // 6
    segr[:, 0:half] = jnp.broadcast_to(segs[owner, pl.ds(j0, 1), ds(r * half, half)], (8, half))
    segr[:, half:] = jnp.broadcast_to(segs[owner, pl.ds(j0, 1), ds((1 - r) * half, half)], (8, half))
    segc[...] = jnp.transpose(jnp.broadcast_to(segr[0:1, :], (128, length)))
    finish_weight(0)
    for q in range(4):
        wait_for(parf.at[:, pl.ds(q * 256, 256)], recv_p.at[q])
        wait_for(xf.at[pl.ds(half, half), pl.ds(q * 256, 256)], recv_m.at[q])

    def project(t, carry):
        place = ds(t * 256, 256)
        for j in range(2):
            lanes = slice(j * 3 * part, (j + 1) * 3 * part)
            value = jnp.dot(xf[place, :], wqf[:, lanes], preferred_element_type=F32)
            bias = parf[:, ds(r * 2 * part + j * part, part)].astype(F32)
            low = j * 3 * part
            qkv[place, low : low + part] = (value[:, :part] + bias[0:1]).astype(BF)
            qkv[place, low + part : low + 2 * part] = value[:, part : 2 * part].astype(BF)
            qkv[place, low + 2 * part : low + 3 * part] = (value[:, 2 * part :] + bias[1:2]).astype(BF)
        for k, i in ((0, 8), (2, 9)):
            @pl.when(t == k)
            def _():
                advance(i)
        return carry
    lax.fori_loop(0, length // 256, project, 0)
    pairs = (
        (xf, x_out), (wqf, wq_out), (wof, wo_out), (wuf, wu_out), (wdf, wd_out), (qkv, qkv_out), (ctx, ctx_out), (normed, normed_out),
        (hidden, hidden_out), (act, act_out), (slope, slope_out), (outh, out_half), (two, two_out), (mix, mix_out))
    stores = [pltpu.make_async_copy(near, out, store.at[i]) for i, (near, out) in enumerate(pairs)]
    for i in (0, 1, 5):
        stores[i].start()

    def to_mate(src, dst, i):
        return pltpu.make_async_remote_copy(
            src, dst, send_x.at[i], recv_x.at[i], device_id={"core": 1 - r}, device_id_type=MESH)

    top_half, low_half = pl.ds(0, half), pl.ds(half, half)
    swaps = [
        to_mate(wof, wom, 0), to_mate(ctx.at[low_half], ctxm, 1), to_mate(hidden.at[top_half], hidden.at[low_half], 2),
        to_mate(mate_out.at[pl.ds(0, 256)], mate_in.at[pl.ds(0, 256)], 3),
        to_mate(mate_out.at[pl.ds(256, 256)], mate_in.at[pl.ds(256, 256)], 4), to_mate(mix.at[top_half], mix.at[low_half], 5)]

    rows = 256

    def pair(i, carry):
        base = (i // 2) * 3 * part + lax.rem(i, 2) * 128
        tq[...] = qkv[:, ds(base, 128)]
        tk[...] = qkv[:, ds(base + part, 128)]
        tv[...] = qkv[:, ds(base + 2 * part, 128)]
        seg_k = segr[0:1, :]
        for h in range(2):
            lanes = slice(h * HEAD_DIM, (h + 1) * HEAD_DIM)
            k, v = tk[:, lanes], tv[:, lanes]
            for start in range(0, length, rows):
                q = tq[start : start + rows, lanes]
                s = lax.dot_general(q, k, CONTRACT_LAST, preferred_element_type=F32) * (scale * LOG2E)
                s = jnp.where(segc[start : start + rows, 0:1] == seg_k, s, -1e9 * LOG2E)
                top = jnp.max(s, axis=1, keepdims=True)
                e = jnp.exp2(s - top)
                total = jnp.sum(e, axis=1, keepdims=True)
                out = jnp.dot(e.astype(BF), v, preferred_element_type=F32) / total
                tc[start : start + rows, lanes] = out.astype(BF)
                log_total = top + jnp.log2(total)
                lse[i, h : h + 1, start : start + rows] = jnp.transpose(jnp.broadcast_to(log_total, (rows, 128)))[0:1, :]
            for at, n in ATTEND_STEPS:
                if at[1] == h:
                    @pl.when(i == at[0])
                    def _():
                        advance(n)
        ctx[:, ds(i * 128, 128)] = tc[...]

        @pl.when(i == 2)
        def _():
            finish_weight(1)
            swaps[0].start()
            stores[2].start()
        return carry
    lax.fori_loop(0, ctx.shape[1] // 128, pair, 0)

    swaps[1].start()
    stores[6].start()
    for i in range(10 + len(ATTEND_STEPS), 16):
        advance(i)
    c_step(*steps[13])
    rowsf = parf[...].astype(F32)
    swaps[0].wait_recv()
    swaps[1].wait_recv()

    def out_rows(t, carry):
        place = ds(t * 256, 256)
        value = jnp.dot(ctx[place, :], wof[...], preferred_element_type=F32) + jnp.dot(ctxm[place, :], wom[...], preferred_element_type=F32)
        value = xf[place, :].astype(F32) + value + rowsf[2:3]
        out, norm, inv = normalize(value, rowsf[3:4], rowsf[4:5])
        hidden_one[place, :] = out
        normed[place, :] = norm
        inverse[place, :] = inv
        hidden[place, :] = out.astype(BF)
        return carry
    lax.fori_loop(0, half // 256, out_rows, 0)
    swaps[2].start()
    stores[7].start()
    c_step(*steps[14])
    c_step(*steps[15])
    finish_weight(2)
    stores[3].start()
    n = act.shape[1] // 2
    bias = []
    for j in range(2):
        block = parf[:, ds(r * 2 * part + j * part, part)].astype(F32)
        bias.append(jnp.concatenate([block[8 + k : 9 + k] for k in range(4)], axis=1))

    def up_rows(t, carry):
        place = ds(t * 256, 256)
        for j in range(2):
            lanes = slice(j * n, (j + 1) * n)
            value = jnp.dot(hidden[place, :], wuf[:, lanes], preferred_element_type=F32) + bias[j]
            gate = 0.5 * (1.0 + lax.erf(value * math.sqrt(0.5)))
            act[place, lanes] = (value * gate).astype(BF)
            slope[place, lanes] = (gate + value * (math.sqrt(0.5 / math.pi) * jnp.exp(-0.5 * value * value))).astype(BF)
        return carry
    lax.fori_loop(0, half // 256, up_rows, 0)
    swaps[2].wait_recv()
    stores[8].start()
    lax.fori_loop(half // 256, length // 256, up_rows, 0)
    stores[9].start()
    stores[10].start()
    finish_weight(3)
    stores[4].start()
    vec[...] = jnp.zeros(vec.shape, F32)
    for t in range(2):
        mate_out[t * 256 : (t + 1) * 256, :] = jnp.dot(
            act[half + t * 256 : half + (t + 1) * 256, :], wdf[...], preferred_element_type=F32)
        swaps[3 + t].start()
    for q in range(4):
        wait_for(ogh.at[:, pl.ds(q * 256, 256)], recv_g.at[q])
    for t in range(2):
        place = slice(t * 256, (t + 1) * 256)
        value = jnp.dot(act[place, :], wdf[...], preferred_element_type=F32)
        swaps[3 + t].wait_recv()
        value = hidden_one[place, :] + (value + mate_in[place, :]) + rowsf[5:6]
        out, norm, inv = normalize(value, rowsf[6:7], rowsf[7:8])
        outh[place, :] = out.astype(BF)
        dy = ogh[place, :].astype(F32)
        scaled = dy * rowsf[6:7]
        mean = jnp.mean(scaled, axis=1, keepdims=True)
        slant = jnp.mean(scaled * norm, axis=1, keepdims=True)
        grad = inv * (scaled - mean - norm * slant)
        two[place, :] = grad
        mix[place, :] = grad.astype(BF)
        vec[3:4, :] += jnp.sum(grad, axis=0, keepdims=True)
        vec[4:5, :] += jnp.sum(dy * norm, axis=0, keepdims=True)
        vec[5:6, :] += jnp.sum(dy, axis=0, keepdims=True)
    swaps[5].start()
    stores[11].start()
    stores[12].start()
    for s in range(1, 4):
        par_copy(s).wait_send()
    seg_send.wait_send()
    swaps[5].wait_recv()
    stores[13].start()
    for copy in swaps:
        copy.wait_send()
    for q in range(4):
        mate_copy(q).wait_send()
    for which in range(2):
        for k in range(2):
            for h in range(2):
                token_copy(which, k, h, True)
    for w in range(4):
        for up in (0, 1):
            @pl.when(outer(up))
            def _():
                a_copy(w, up).wait_send()

        @pl.when(r != owner)
        def _():
            mate_part(w).wait_send()

        for j in range(2):
            @pl.when(2 * r + j != c)
            def _():
                for rr in range(2):
                    for up in (0, 1):
                        forward(w, j, rr, up, True)
                    for p in range(2):
                        b_copy(w, j, rr, p).wait_send()
                        c_copy(w, j, rr, p).wait_send()
    for copy in stores:
        copy.wait()


ATTEND_STEPS = (((0, 0), 10), ((0, 1), 11), ((1, 1), 12), ((2, 1), 13), ((3, 0), 14))


def gather(tok, og, par, seg, weights, scale):
    dma = pltpu.SemaphoreType.DMA
    vmem, anywhere = pl.BlockSpec(memory_space=pltpu.VMEM), pl.BlockSpec(memory_space=pl.ANY)
    half, width = tok.shape[0] // 4, tok.shape[1] * 4
    length, heads, units = 2 * half, weights[1].shape[0] * 2, weights[2].shape[1] * 2
    rows = (half, width)
    out = [((16, width), BF), ((heads // 128, 2, length), F32), ((length, 128), jnp.int32), ((8, length), jnp.int32), ((half, 1), F32), ((16, width), F32)]
    large = [((length, width), BF)] + [((w.shape[0] * 2, w.shape[1] * 2), BF) for w in weights]
    large += [((length, 3 * heads), BF), ((length, heads), BF), (rows, F32), ((length, width), BF), ((length, units), BF), ((length, units), BF)]
    large += [(rows, BF), (rows, F32), ((length, width), BF)]
    scratch = large + [(rows, BF), ((heads, width), BF), ((half, heads), BF)] + [(rows, F32)] * 3 + [((2,) + seg.shape, jnp.int32)]
    scratch += [((length, 128), BF)] * 4
    sems = [(4, 2), (4, 4), (4, 4)] + [(4, 4, 2)] * 4 + [(4,)] * 10 + [(1,), (2,), (6,), (6,), (14,)]
    return pl.pallas_call(
        partial(gather_kernel, scale=scale),
        out_shape=[jax.ShapeDtypeStruct(s, t) for s, t in out + large],
        in_specs=[vmem] * 8,
        out_specs=[vmem] * 6 + [anywhere] * 14,
        scratch_shapes=[pltpu.VMEM(s, t) for s, t in scratch] + [dma(s) for s in sems],
        compiler_params=pltpu.CompilerParams(collective_id=0, has_side_effects=True, vmem_limit_bytes=VMEM_LIMIT),
        name="gather",
    )(tok, og, par, seg, *weights)


def mid_kernel(
    inverse, gain, vec_in, out_half, act_far, cols_far, mix_far, slope_far, wd_far, two_far, normed_far, hidden_far, wu_far, wo_far, ctx_far,
    outp, gu_out, go, do, one_grad, vec, gsum,
    act, attn, mix, slope, wd, two_grad, normed, hidden, wu, wo, ctx, gd, gu, up_low, ub, mate_out, mate_in, first, second,
    send1, recv1, send2, recv2, send_y, recv_y, send_m, recv_m, load, store,
):
    d, r, c = lax.axis_index("dp"), lax.axis_index("core"), lax.axis_index("col")
    a, b = d // 2, lax.rem(d, 2)
    barrier = pltpu.get_barrier_semaphore()
    for s in range(4):
        for o in range(2):
            if s or o:
                target = {"core": lax.rem(r + o, 2), "col": lax.rem(c + s, 4)}
                pl.semaphore_signal(barrier, inc=1, device_id=target, device_id_type=MESH)
    x_peer, y_peer = lax.bitwise_xor(d, 1), lax.bitwise_xor(d, 2)
    for p in (x_peer, y_peer):
        pl.semaphore_signal(barrier, inc=1, device_id={"dp": p}, device_id_type=MESH)
    pl.semaphore_wait(barrier, 9)

    half, n = out_half.shape[0], gd.shape[1] // 2
    size = gd.shape[0] // 4

    def local(j, slab):
        return gd.at[ds(slab * size, size), pl.ds(j * n, n)]

    def slab_of(j, i, mine):
        if j == 0:
            return i * 2 + (b if mine else 1 - b)
        return (a if mine else 1 - a) * 2 + i

    def turn(j, kept):
        own = a if j == 0 else b
        return own if kept else 1 - own

    def copy1(j, kept):
        i = turn(j, kept)
        return pltpu.make_async_remote_copy(
            local(j, slab_of(j, i, False)), first.at[j, i], send1.at[j, i], recv1.at[j, i],
            device_id={"dp": x_peer if j == 0 else y_peer}, device_id_type=MESH)

    def copy2(j):
        return pltpu.make_async_remote_copy(
            first.at[j, turn(j, False)], second.at[j], send2.at[j], recv2.at[j],
            device_id={"dp": y_peer if j == 0 else x_peer}, device_id_type=MESH)

    def token_copy(q, wait):
        rr, k = c // 2, lax.rem(c, 2)
        sref = out_half.at[:, pl.ds(q * 256, 256)]
        dref = outp.at[ds(k * 2 * half + r * half, half)]
        sem = recv_y.at[k * 2 + r]
        me = jnp.logical_and(rr == r, q == c)
        remote = pltpu.make_async_remote_copy(
            sref, dref, send_y.at[q], sem, device_id={"core": rr, "col": q}, device_id_type=MESH)
        if not wait:
            @pl.when(me)
            def _():
                pltpu.make_async_copy(sref, dref, sem).start()

        @pl.when(jnp.logical_not(me))
        def _():
            remote.wait_send() if wait else remote.start()

    for q in range(4):
        token_copy(q, False)
    far_near = (
        (cols_far, attn), (act_far, act), (mix_far, mix), (wd_far, wd), (slope_far, slope), (wu_far, wu), (two_far, two_grad),
        (normed_far, normed), (hidden_far, hidden), (wo_far, wo), (ctx_far, ctx))
    loads = [pltpu.make_async_copy(far, near, load.at[i]) for i, (far, near) in enumerate(far_near)]
    for copy in loads:
        copy.start()
    vec[...] = vec_in[...]
    ub[...] = jnp.zeros(ub.shape, F32)
    loads[0].wait()
    loads[1].wait()

    def down_rows(t, carry):
        slab = lax.bitwise_xor(d, 3 - t)
        xt = jnp.transpose(attn[:, ds(slab * size, size)])
        for j in range(2):
            lanes = slice(j * n, (j + 1) * n)
            gd[ds(slab * size, size), lanes] = jnp.dot(xt, act[:, lanes], preferred_element_type=F32).astype(BF)
        for k, sends in ((0, ((0, False), (1, False))), (1, ((1, True),)), (2, ((0, True),))):
            @pl.when(t == k)
            def _():
                for j, kept in sends:
                    copy1(j, kept).start()
        return carry
    lax.fori_loop(0, 4, down_rows, 0)
    for copy in loads[2:5]:
        copy.wait()

    def up_rows(t, carry):
        place = ds(t * 256, 256)
        for j in range(2):
            lanes = slice(j * n, (j + 1) * n)
            value = lax.dot_general(mix[place, :], wd[lanes, :], CONTRACT_LAST, preferred_element_type=F32) * slope[place, lanes].astype(F32)
            up_low[place, lanes] = value.astype(BF)
            ub[0:1, lanes] += jnp.sum(value, axis=0, keepdims=True)
        return carry
    lax.fori_loop(0, 2 * half // 256, up_rows, 0)

    loads[5].wait()

    def mate_rows(t, carry):
        mate_out[ds(t * 256, 256), :] = lax.dot_general(
            up_low[ds(half + t * 256, 256), :], wu[...], CONTRACT_LAST, preferred_element_type=F32)
        return carry
    lax.fori_loop(0, half // 256, mate_rows, 0)
    mate = pltpu.make_async_remote_copy(
        mate_out, mate_in, send_m.at[0], recv_m.at[0], device_id={"core": 1 - r}, device_id_type=MESH)
    mate.start()
    for copy in loads[6:]:
        copy.wait()

    for j in range(2):
        give = turn(j, False)
        wait_for(first.at[j, give], recv1.at[j, give])
        src, dst = local(j, slab_of(j, give, True)), first.at[j, give]

        def add_two(t, carry):
            rows = ds(t * 64, 64, 64)
            dst[rows, :] = (src[rows, :].astype(F32) + dst[rows, :].astype(F32)).astype(BF)
            return carry
        lax.fori_loop(0, size // 64, add_two, 0)
        copy2(j).start()

    mate.wait_recv()
    width = mate_in.shape[1]
    vec[0:3, :] = jnp.zeros((3, width), F32)

    def own_rows(t, carry):
        place = ds(t * 256, 256)
        value = lax.dot_general(up_low[place, :], wu[...], CONTRACT_LAST, preferred_element_type=F32)
        value = value + mate_in[place, :] + two_grad[place, :]
        norm = normed[place, :]
        scaled = value * gain[...]
        mean = jnp.mean(scaled, axis=1, keepdims=True)
        slant = jnp.mean(scaled * norm, axis=1, keepdims=True)
        grad = inverse[place, :] * (scaled - mean - norm * slant)
        one_grad[place, :] = grad
        attn[place, :] = grad.astype(BF)
        vec[0:1, :] += jnp.sum(grad, axis=0, keepdims=True)
        vec[1:2, :] += jnp.sum(value * norm, axis=0, keepdims=True)
        vec[2:3, :] += jnp.sum(value, axis=0, keepdims=True)
        return carry
    lax.fori_loop(0, half // 256, own_rows, 0)
    pair = pltpu.make_async_remote_copy(
        attn.at[pl.ds(0, half)], attn.at[pl.ds(half, half)], send_m.at[1], recv_m.at[1],
        device_id={"core": 1 - r}, device_id_type=MESH)
    pair.start()

    def weight_rows(t, carry):
        xt = jnp.transpose(hidden[:, ds(t * 256, 256)])
        for j in range(2):
            lanes = slice(j * n, (j + 1) * n)
            gu[ds(t * 256, 256), lanes] = jnp.dot(xt, up_low[:, lanes], preferred_element_type=F32).astype(BF)
        return carry
    lax.fori_loop(0, hidden.shape[1] // 256, weight_rows, 0)
    gu_store = pltpu.make_async_copy(gu, gu_out, store.at[0])
    gu_store.start()
    part = n // 4
    for k in range(4):
        for j in range(2):
            vec[8 + k : 9 + k, ds(r * 2 * part + j * part, part)] = ub[0:1, j * n + k * part : j * n + (k + 1) * part]
    pair.wait_recv()

    def ctx_rows(t, carry):
        place = ds(t * 256, 256)
        do[place, :] = lax.dot_general(attn[place, :], wo[...], CONTRACT_LAST, preferred_element_type=F32).astype(BF)
        return carry
    lax.fori_loop(0, 2 * half // 256, ctx_rows, 0)

    def out_rows(t, carry):
        xt = jnp.transpose(ctx[:, ds(t * 256, 256)])
        go[ds(t * 256, 256), :] = jnp.dot(xt, attn[...], preferred_element_type=F32).astype(BF)
        return carry
    lax.fori_loop(0, ctx.shape[1] // 256, out_rows, 0)

    for j in range(2):
        kept = turn(j, True)
        wait_for(first.at[j, kept], recv1.at[j, kept])
        wait_for(second.at[j], recv2.at[j])
        src, more = local(j, slab_of(j, kept, True)), first.at[j, kept]

        def add_three(t, carry):
            rows = ds(t * 64, 64, 64)
            value = src[rows, :].astype(F32) + more[rows, :].astype(F32) + second[j, rows, :].astype(F32)
            gsum[j, rows, :] = value.astype(BF)
            return carry
        lax.fori_loop(0, size // 64, add_three, 0)
    for j in range(2):
        for kept in (False, True):
            copy1(j, kept).wait_send()
        copy2(j).wait_send()
    mate.wait_send()
    pair.wait_send()
    gu_store.wait()
    for q in range(4):
        token_copy(q, True)
        wait_for(outp.at[pl.ds(q * half, half)], recv_y.at[q])


def middle(out_half, act, cols, mix, slope, wd, two_grad, normed, inverse, gain, vec, hidden, wu, wo, ctx):
    dma = pltpu.SemaphoreType.DMA
    vmem, anywhere = pl.BlockSpec(memory_space=pltpu.VMEM), pl.BlockSpec(memory_space=pl.ANY)
    half, width = out_half.shape
    slab = (width // 4, act.shape[1] // 2)
    out = [((4 * half, width // 4), BF), (wu.shape, BF), (wo.shape, BF), (ctx.shape, BF), ((half, width), F32), (vec.shape, F32), ((2,) + slab, BF)]
    scratch = [(v.shape, v.dtype) for v in (act, cols, mix, slope, wd, two_grad, normed, hidden, wu, wo, ctx)]
    scratch += [(wu.shape, BF), (wu.shape, BF), (slope.shape, BF)]
    scratch += [((8, slope.shape[1]), F32), ((half, width), F32), ((half, width), F32), ((2, 2) + slab, BF), ((2,) + slab, BF)]
    sems = [(2, 2), (2, 2), (2,), (2,), (4,), (4,), (2,), (2,), (11,), (1,)]
    return pl.pallas_call(
        mid_kernel,
        out_shape=[jax.ShapeDtypeStruct(s, t) for s, t in out],
        in_specs=[vmem] * 3 + [anywhere] * 12,
        out_specs=[anywhere] * 2 + [vmem] * 5,
        scratch_shapes=[pltpu.VMEM(s, t) for s, t in scratch] + [dma(s) for s in sems],
        compiler_params=pltpu.CompilerParams(collective_id=2, has_side_effects=True, vmem_limit_bytes=VMEM_LIMIT),
        name="mid",
    )(inverse, gain, vec, out_half, act, cols, mix, slope, wd, two_grad, normed, hidden, wu, wo, ctx)


def back_kernel(
    lse, segk, segq, vec, qkv_far, do_far, ctx_far, gu_far, go_far, x_far, wq_far, one_far, gsum,
    inp, total, rq, ro, ru, rd,
    qkv, do, ctx, gu, go, x, wq, one_grad, gq, low, tq, tk, tv, tg, vbuf, mate_out, mate_in, in_half,
    r1q, r1o, r1u, r2q, r2o, r2u, r3q, r3o, r3u, r3d, tall, v1, s4, v2,
    send1, recv1, send2, recv2, send3, recv3, send_i, recv_i, send_v, recv_v, send_w, recv_w, send_m, recv_m, load,
    *, scale,
):
    d, r, c = lax.axis_index("dp"), lax.axis_index("core"), lax.axis_index("col")
    a, b = d // 2, lax.rem(d, 2)
    barrier = pltpu.get_barrier_semaphore()
    for s in range(4):
        for o in range(2):
            if s or o:
                target = {"core": lax.rem(r + o, 2), "col": lax.rem(c + s, 4)}
                pl.semaphore_signal(barrier, inc=1, device_id=target, device_id_type=MESH)
    x_peer, y_peer = lax.bitwise_xor(d, 1), lax.bitwise_xor(d, 2)
    plane = [(p, o) for p in range(4) for o in range(2) if p or o]
    for p, o in plane:
        if p:
            target = {"dp": lax.bitwise_xor(d, p), "core": lax.rem(r + o, 2)}
            pl.semaphore_signal(barrier, inc=1, device_id=target, device_id_type=MESH)
    pl.semaphore_wait(barrier, 13)

    grads, sources = (None, go, gu), (None, go_far, gu_far)
    first, second = (r1q, r1o, r1u), (r2q, r2o, r2u)
    third, result = (r3q, r3o, r3u, r3d), (rq, ro, ru, rd)
    by_rows = (True, False, True, True)
    length, part3q = low.shape[0], low.shape[1] // 2
    part = part3q // 3

    def local(w, j, slab, far=False):
        if w == 0:
            return gq.at[j, slab]
        ref = (sources if far else grads)[w]
        rows, cols = ref.shape
        if by_rows[w]:
            return ref.at[ds(slab * (rows // 4), rows // 4), pl.ds(j * (cols // 2), cols // 2)]
        return ref.at[pl.ds(j * (rows // 2), rows // 2), ds(slab * (cols // 4), cols // 4)]

    def slab_of(j, i, mine):
        if j == 0:
            return i * 2 + (b if mine else 1 - b)
        return (a if mine else 1 - a) * 2 + i

    def turn(j, kept):
        own = a if j == 0 else b
        return own if kept else 1 - own

    def copy1(w, j, kept):
        i = turn(j, kept)
        return pltpu.make_async_remote_copy(
            local(w, j, slab_of(j, i, False), True), first[w].at[j, i], send1.at[w, j, i], recv1.at[w, j, i],
            device_id={"dp": x_peer if j == 0 else y_peer}, device_id_type=MESH)

    def copy2(w, j):
        return pltpu.make_async_remote_copy(
            first[w].at[j, turn(j, False)], second[w].at[j], send2.at[w, j], recv2.at[w, j],
            device_id={"dp": y_peer if j == 0 else x_peer}, device_id_type=MESH)

    def copy3(w, j, rr, wait):
        src = gsum.at[j] if w == 3 else first[w].at[j, turn(j, True)]
        src = src.at[pl.ds(rr * 128, 128), :] if by_rows[w] else src.at[:, pl.ds(rr * 128, 128)]
        dst = third[w].at[c]
        z = 2 * r + j
        me = jnp.logical_and(z == c, r == rr)
        remote = pltpu.make_async_remote_copy(
            src, dst, send3.at[w, j, rr], recv3.at[w, c], device_id={"core": rr, "col": z}, device_id_type=MESH)
        if not wait:
            @pl.when(me)
            def _():
                pltpu.make_async_copy(src, dst, recv3.at[w, c]).start()

        @pl.when(jnp.logical_not(me))
        def _():
            remote.wait_send() if wait else remote.start()

    def send_first(w, kept):
        for j in range(2):
            copy1(w, j, kept).start()

    def step2(w):
        for j in range(2):
            give = turn(j, False)
            wait_for(first[w].at[j, give], recv1.at[w, j, give])
            src, dst = local(w, j, slab_of(j, give, True)), first[w].at[j, give]

            def body(t, carry):
                rows = ds(t * 64, 64, 64)
                dst[rows, :] = (src[rows, :].astype(F32) + dst[rows, :].astype(F32)).astype(BF)
                return carry
            lax.fori_loop(0, dst.shape[0] // 64, body, 0)
            copy2(w, j).start()

    def step3(w):
        for j in range(2):
            kept = turn(j, True)
            wait_for(first[w].at[j, kept], recv1.at[w, j, kept])
            wait_for(second[w].at[j], recv2.at[w, j])
            src, dst, more = local(w, j, slab_of(j, kept, True)), first[w].at[j, kept], second[w].at[j]

            def body(t, carry):
                rows = ds(t * 64, 64, 64)
                dst[rows, :] = (src[rows, :].astype(F32) + dst[rows, :].astype(F32) + more[rows, :].astype(F32)).astype(BF)
                return carry
            lax.fori_loop(0, dst.shape[0] // 64, body, 0)
            for rr in range(2):
                copy3(w, j, rr, False)

    def finish(w):
        for z in range(4):
            wait_for(third[w].at[z], recv3.at[w, z])

        def body(t, carry):
            rows = ds(t * 64, 64, 64)
            value = (third[w][0, rows, :].astype(F32) + third[w][1, rows, :].astype(F32)) + (
                third[w][2, rows, :].astype(F32) + third[w][3, rows, :].astype(F32))
            if w == 3:
                tall[rows, :] = value
            else:
                result[w][rows, :] = value
            return carry
        lax.fori_loop(0, third[w].shape[1] // 64, body, 0)
        if w == 3:
            rd[...] = jnp.transpose(tall[...])

    half = in_half.shape[0]

    def token_copy(q, wait):
        rr, k = c // 2, lax.rem(c, 2)
        sref = in_half.at[:, pl.ds(q * 256, 256)]
        dref = inp.at[ds(k * 2 * half + r * half, half)]
        sem = recv_i.at[k * 2 + r]
        me = jnp.logical_and(rr == r, q == c)
        remote = pltpu.make_async_remote_copy(
            sref, dref, send_i.at[q], sem, device_id={"core": rr, "col": q}, device_id_type=MESH)
        if not wait:
            @pl.when(me)
            def _():
                pltpu.make_async_copy(sref, dref, sem).start()

        @pl.when(jnp.logical_not(me))
        def _():
            remote.wait_send() if wait else remote.start()

    def vec_z(s):
        z = lax.rem(c + s, 4)
        return pltpu.make_async_remote_copy(
            vbuf.at[:, ds(z * 256, 256)], v1.at[s], send_v.at[s], recv_v.at[s], device_id={"col": z}, device_id_type=MESH)

    def vec_plane(i):
        p, o = plane[i]
        return pltpu.make_async_remote_copy(
            s4, v2.at[i], send_w.at[i], recv_w.at[i],
            device_id={"dp": lax.bitwise_xor(d, p), "core": lax.rem(r + o, 2)}, device_id_type=MESH)

    mate = pltpu.make_async_remote_copy(
        mate_out, mate_in, send_m.at[0], recv_m.at[0], device_id={"core": 1 - r}, device_id_type=MESH)

    send_first(2, False)
    send_first(2, True)
    for j in range(2):
        for rr in range(2):
            copy3(3, j, rr, False)
    far_near = (
        (qkv_far, qkv), (do_far, do), (ctx_far, ctx), (gu_far, gu), (go_far, go), (x_far, x), (wq_far, wq), (one_far, one_grad))
    loads = [pltpu.make_async_copy(far, near, load.at[i]) for i, (far, near) in enumerate(far_near)]
    for copy in loads:
        copy.start()
    vbuf[...] = vec[...]
    for copy in loads[:3]:
        copy.wait()

    rows = 256

    def pair(i, carry):
        base = (i // 2) * part3q + lax.rem(i, 2) * 128
        tq[...] = qkv[:, ds(base, 128)]
        tg[...] = do[:, ds(i * 128, 128)]
        prod = jnp.transpose(tg[...].astype(F32) * ctx[:, ds(i * 128, 128)].astype(F32))
        tk[...] = qkv[:, ds(base + part, 128)]
        tv[...] = qkv[:, ds(base + 2 * part, 128)]
        seg_q = segq[0:1, :]
        for h in range(2):
            lanes = slice(h * HEAD_DIM, (h + 1) * HEAD_DIM)
            qh, doh = tq[:, lanes], tg[:, lanes]
            delta = jnp.sum(prod[h * HEAD_DIM : (h + 1) * HEAD_DIM], axis=0, keepdims=True)
            top = lse[i, h : h + 1, :]
            dqt = jnp.zeros((HEAD_DIM, length), F32)
            vsum = jnp.zeros((1, HEAD_DIM), F32)
            for start in range(0, length, rows):
                kh = tk[start : start + rows, lanes]
                vh = tv[start : start + rows, lanes]
                s = lax.dot_general(kh, qh, CONTRACT_LAST, preferred_element_type=F32) * (scale * LOG2E)
                s = jnp.where(segk[start : start + rows, 0:1] == seg_q, s, -1e9 * LOG2E)
                p = jnp.exp2(s - top)
                dp = lax.dot_general(vh, doh, CONTRACT_LAST, preferred_element_type=F32)
                g = (p * (dp - delta)).astype(BF)
                dk = jnp.dot(g, qh, preferred_element_type=F32) * scale
                tk[start : start + rows, lanes] = dk.astype(BF)
                dv = jnp.dot(p.astype(BF), doh, preferred_element_type=F32)
                tv[start : start + rows, lanes] = dv.astype(BF)
                vsum += jnp.sum(dv, axis=0, keepdims=True)
                dqt += jnp.dot(jnp.transpose(kh), g, preferred_element_type=F32)
            dq = jnp.transpose(dqt) * scale
            tq[:, lanes] = dq.astype(BF)
            v1[0, h : h + 1, 0:HEAD_DIM] = jnp.sum(dq, axis=0, keepdims=True)
            v1[0, h : h + 1, 128 : 128 + HEAD_DIM] = vsum
        low[:, ds(base, 128)] = tq[...]
        low[:, ds(base + part, 128)] = tk[...]
        low[:, ds(base + 2 * part, 128)] = tv[...]
        place = ds(r * 2 * part + i * 128, 128)
        vbuf[6:7, place] = jnp.concatenate([v1[0, 0:1, 0:HEAD_DIM], v1[0, 1:2, 0:HEAD_DIM]], axis=1)
        vbuf[7:8, place] = jnp.concatenate([v1[0, 0:1, 128 : 128 + HEAD_DIM], v1[0, 1:2, 128 : 128 + HEAD_DIM]], axis=1)

        @pl.when(i == 1)
        def _():
            for copy in loads[3:]:
                copy.wait()
            step2(2)
            send_first(1, False)
            send_first(1, True)
        return carry
    lax.fori_loop(0, do.shape[1] // 128, pair, 0)

    for s in range(1, 4):
        vec_z(s).start()

    def weight_rows(t, carry):
        xt = jnp.transpose(x[:, ds(t * 256, 256)])
        for j in range(2):
            gq[j, t] = jnp.dot(xt, low[:, j * part3q : (j + 1) * part3q], preferred_element_type=F32).astype(BF)
        return carry
    lax.fori_loop(0, 4, weight_rows, 0)
    send_first(0, False)
    send_first(0, True)

    def mate_rows(t, carry):
        mate_out[ds(t * 256, 256), :] = lax.dot_general(
            low[ds(half + t * 256, 256), :], wq[...], CONTRACT_LAST, preferred_element_type=F32)
        return carry
    lax.fori_loop(0, half // 256, mate_rows, 0)
    mate.start()
    step3(2)
    for s in range(1, 4):
        vec_z(s).wait()
    s4[...] = (vbuf[:, ds(c * 256, 256)] + v1[1]) + (v1[2] + v1[3])
    for i in range(7):
        vec_plane(i).start()
    mate.wait_recv()

    def own_rows(t, carry):
        place = ds(t * 256, 256)
        value = lax.dot_general(low[place, :], wq[...], CONTRACT_LAST, preferred_element_type=F32)
        in_half[place, :] = (value + mate_in[place, :] + one_grad[place, :]).astype(BF)
        return carry
    lax.fori_loop(0, half // 256, own_rows, 0)
    for q in range(4):
        token_copy(q, False)
    step2(1)
    step2(0)
    step3(1)
    finish(3)
    for i in range(7):
        vec_plane(i).wait()
    total[...] = ((s4[...] + v2[0]) + (v2[1] + v2[2])) + ((v2[3] + v2[4]) + (v2[5] + v2[6]))
    step3(0)
    for w in (2, 1, 0):
        finish(w)
    for w in range(4):
        for j in range(2):
            for i in range(2):
                if w < 3:
                    copy1(w, j, i).wait_send()
                copy3(w, j, i, True)
            if w < 3:
                copy2(w, j).wait_send()
    mate.wait_send()
    for q in range(4):
        token_copy(q, True)
        wait_for(inp.at[pl.ds(q * half, half)], recv_i.at[q])


def back(x, wq, qkv, do, ctx, lse, segk, segq, one_grad, vec, grads, scale):
    dma = pltpu.SemaphoreType.DMA
    vmem, anywhere = pl.BlockSpec(memory_space=pltpu.VMEM), pl.BlockSpec(memory_space=pl.ANY)
    half, width = one_grad.shape
    far = (qkv, do, ctx, grads[1], grads[0], x, wq, one_grad)
    length, part = 2 * half, width // 4
    out, r1, r2, r3 = [((4 * half, part), BF)] + [((vec.shape[0], part), F32)], [], [], []
    for w, (rows, cols) in enumerate([wq.shape] + [g.shape for g in grads[:2]] + [(4 * grads[2].shape[1], 2 * grads[2].shape[2])]):
        if w in (0, 2, 3):
            out.append(((cols // 2, rows // 8) if w == 3 else (rows // 8, cols // 2), F32))
            slab, piece = (rows // 4, cols // 2), (rows // 8, cols // 2)
        else:
            out.append(((rows // 2, cols // 8), F32))
            slab, piece = (rows // 2, cols // 4), (rows // 2, cols // 8)
        if w < 3:
            r1.append((2, 2) + slab)
            r2.append((2,) + slab)
        r3.append((4,) + piece)
    scratch = [(v.shape, v.dtype) for v in far] + [((2, 4, width // 4, wq.shape[1] // 2), BF), (qkv.shape, BF)] + [((length, 128), BF)] * 4
    scratch += [(vec.shape, F32), ((half, width), F32), ((half, width), F32), ((half, width), BF)]
    scratch += [(s, BF) for s in r1 + r2 + r3] + [(r3[3][1:], F32)]
    scratch += [((4, vec.shape[0], part), F32), ((vec.shape[0], part), F32), ((7, vec.shape[0], part), F32)]
    sems = [(3, 2, 2), (3, 2, 2), (3, 2), (3, 2), (4, 2, 2), (4, 4), (4,), (4,), (4,), (4,), (7,), (7,), (1,), (1,), (8,)]
    return pl.pallas_call(
        partial(back_kernel, scale=scale),
        out_shape=[jax.ShapeDtypeStruct(s, t) for s, t in out],
        in_specs=[vmem] * 4 + [anywhere] * 9,
        out_specs=[anywhere] + [vmem] * 5,
        scratch_shapes=[pltpu.VMEM(s, t) for s, t in scratch] + [dma(s) for s in sems],
        compiler_params=pltpu.CompilerParams(collective_id=1, has_side_effects=True, vmem_limit_bytes=VMEM_LIMIT),
        name="back",
    )(lse, segk, segq, vec, *far, grads[2])


def part_rows(values, groups):
    if groups == 1:
        return values
    rows, cols = values.shape
    return values.reshape(4, groups, 2, rows // (8 * groups), cols).transpose(0, 2, 1, 3, 4).reshape(rows, cols)


def on_device(
    tokens, segment_ids, w_qkv, b_qv, w_out, b_out, norm1_gain, norm1_shift,
    w_up, b_up, w_down, b_down, norm2_gain, norm2_shift, out_grad,
):
    groups = lax.axis_size("rh")
    core, col = lax.axis_index("core"), lax.axis_index("col")
    part = tokens.shape[1]
    scale = 1.0 / math.sqrt(HEAD_DIM)
    wq, wo, wu, wd = w_qkv.reshape(w_qkv.shape[0], 3 * part), w_out, w_up, w_down
    if groups > 1:
        both_rows = ("rh", "core")
        wq, wu = (lax.all_gather(w, both_rows, axis=0, tiled=True) for w in (wq, wu))
        wo, wd = (lax.all_gather(w, both_rows, axis=1, tiled=True) for w in (wo, wd))
        wq, wu = (lax.dynamic_slice_in_dim(w, core * (w.shape[0] // 2), w.shape[0] // 2, 0) for w in (wq, wu))
        wo, wd = (lax.dynamic_slice_in_dim(w, core * (w.shape[1] // 2), w.shape[1] // 2, 1) for w in (wo, wd))
    vectors = [b_qv[0], b_qv[1], b_out, norm1_gain, norm1_shift, b_down, norm2_gain, norm2_shift] + [b_up[k * part : (k + 1) * part] for k in range(4)]
    index = lax.broadcasted_iota(jnp.int32, (16, part), 0)
    par = jnp.zeros((16, part), BF)
    for k, vector in enumerate(vectors):
        par = jnp.where(index == k, vector[None], par)
    (params, lse, seg_col, seg_row, inverse_one, vec, x, wq, wo, wu, wd, qkv, ctx, normed_one, hidden, activated, slope, output, two_grad,
     mix) = gather(tokens, out_grad, par, segment_ids, (wq, wo, wu, wd), scale)
    gain1 = params[3:4].astype(F32)
    x_cols, hidden_cols, mix_cols = x, hidden, mix
    if groups > 1:
        x_cols, hidden_cols, mix_cols = (part_rows(v.T, groups).T for v in (x, hidden, mix))
    output, up_wgrad, out_wgrad, ctx_grad, one_grad, vec, down_sum = middle(
        output, activated, mix_cols, mix, slope, wd, two_grad, normed_one, inverse_one, gain1, vec, hidden_cols, wu, wo, ctx)
    if groups > 1:
        out_wgrad = part_rows(out_wgrad.T, groups).T
    in_grad, sums, qkv_share, out_share, up_share, down_share = back(
        x_cols, wq, qkv, ctx_grad, ctx, lse, seg_col, seg_row, one_grad, vec, (out_wgrad, up_wgrad, down_sum), scale)
    if groups > 1:
        sums = lax.psum(sums, "rh")
        qkv_share, up_share = (lax.psum_scatter(g, "rh", scatter_dimension=0, tiled=True) for g in (qkv_share, up_share))
        out_share, down_share = (lax.psum_scatter(g, "rh", scatter_dimension=1, tiled=True) for g in (out_share, down_share))
    return (
        output,
        in_grad.astype(F32),
        qkv_share.reshape(qkv_share.shape[0], 3, part),
        sums[6:8],
        out_share,
        sums[0],
        sums[1],
        sums[2],
        up_share,
        sums[8:12].reshape(-1),
        down_share,
        sums[3],
        sums[4],
        sums[5],
    )


def solution(mesh):
    dp, row, col = (mesh.shape[name] for name in ("dp", "row", "col"))
    fine = Mesh(mesh.devices.reshape(dp, row // 2, 2, col), ("dp", "rh", "core", "col"))
    row, every = ("rh", "core"), ("dp", "rh", "core")
    return jax.shard_map(
        on_device,
        mesh=fine,
        in_specs=(
            P(every, "col"), P(every, None), P(row, None, "col"), P(None, "col"), P("col", row), P("col"), P("col"), P("col"),
            P(row, "col"), P("col"), P("col", row), P("col"), P("col"), P("col"), P(every, "col"),
        ),
        out_specs=(
            P(every, "col"), P(every, "col"), P(every, None, "col"), P(None, "col"), P("col", every), P("col"), P("col"),
            P("col"), P(every, "col"), P("col"), P("col", every), P("col"), P("col"), P("col"),
        ),
        check_vma=False,
    )
```

```python
from functools import partial
import math

import jax
import jax.numpy as jnp
from jax import lax
from jax.experimental import pallas as pl
from jax.experimental.pallas import tpu as pltpu
from jax.sharding import Mesh, PartitionSpec as P

HEAD_DIM = 64
NORM_EPSILON = 1e-05
MESH = pl.DeviceIdType.MESH
LOG2E = math.log2(math.e)
BF = jnp.bfloat16
F32 = jnp.float32
CONTRACT_LAST = (((1,), (1,)), ((), ()))
CONTRACT_FIRST = (((0,), (0,)), ((), ()))
VMEM_LIMIT = 62 * 2**20


def wait_for(ref, sem):
    pltpu.make_async_copy(ref, ref, sem).wait()


def ds(start, size, multiple=128):
    return pl.ds(pl.multiple_of(start, multiple), size)


def normalize(residual, gain, shift):
    mean = jnp.mean(residual, axis=1, keepdims=True)
    centered = residual - mean
    inverse = lax.rsqrt(jnp.mean(centered * centered, axis=1, keepdims=True) + NORM_EPSILON)
    normed = centered * inverse
    return normed * gain + shift, normed, inverse


def gather_kernel(
    tok, og, par, seg, wq, wo, wu, wd,
    parf, lse, segc, segr, inverse, vec,
    x_out, wq_out, wo_out, wu_out, wd_out, qkv_out, ctx_out, normed_out, hidden_out, act_out, slope_out, out_half, two_out, mix_out,
    xf, wqf, wof, wuf, wdf, qkv, ctx, normed, hidden, act, slope, outh, two, mix,
    ogh, wom, ctxm, hidden_one, mate_out, mate_in, segs, tq, tk, tv, tc,
    send_a, recv_a, send_f, send_b, recv_b, send_c, recv_c, recv_l, send_l, send_t, recv_t, send_g, recv_g, send_m, recv_m, send_p, recv_p,
    send_s, recv_s, send_x, recv_x, store,
    *, scale,
):
    d, r, c = lax.axis_index("dp"), lax.axis_index("core"), lax.axis_index("col")
    owner, j0 = c // 2, lax.rem(c, 2)
    half = tok.shape[0] // 4
    barrier = pltpu.get_barrier_semaphore()
    for s in range(4):
        for o in range(2):
            if s or o:
                target = {"core": lax.rem(r + o, 2), "col": lax.rem(c + s, 4)}
                pl.semaphore_signal(barrier, inc=1, device_id=target, device_id_type=MESH)
    x_peer, y_peer, far = (lax.bitwise_xor(d, p) for p in (1, 2, 3))
    peers = (x_peer, y_peer)
    for p in peers:
        pl.semaphore_signal(barrier, inc=1, device_id={"dp": p}, device_id_type=MESH)
    pl.semaphore_wait(barrier, 9)

    source, dest = (wq, wo, wu, wd), (wqf, wof, wuf, wdf)

    def whole(w, rr, j):
        rows, cols = source[w].shape
        if w in (0, 2):
            return dest[w].at[ds(rr * rows, rows), ds(j * cols, cols)]
        return dest[w].at[ds(j * rows, rows), ds(rr * cols, cols)]

    def piece(w, rr, dd, j, part=None):
        rows, cols = source[w].shape
        size = rows // 4
        base = (rr if w in (0, 2) else j) * rows + dd * size
        if part is not None:
            size = size // 2
            base = base + part * size
        return dest[w].at[ds(base, size, 32), ds((j if w in (0, 2) else rr) * cols, cols)]

    def a_copy(w, up):
        size = source[w].shape[0] // 4
        return pltpu.make_async_remote_copy(
            source[w].at[ds(d * size, size, 64)], piece(w, r, d, j0), send_a.at[w, up], recv_a.at[w, j0 * 2 + r],
            device_id={"core": owner, "col": lax.rem(c + (1 if up else 3), 4)}, device_id_type=MESH)

    def outer(up):
        return c < 3 if up else c > 0

    def mate_part(w):
        return pltpu.make_async_remote_copy(
            source[w], whole(w, r, j0), send_l.at[w], recv_l.at[w], device_id={"core": 1 - r}, device_id_type=MESH)

    def start_a(w):
        for up in (0, 1):
            @pl.when(outer(up))
            def _():
                a_copy(w, up).start()

        @pl.when(r == owner)
        def _():
            pltpu.make_async_copy(source[w], whole(w, r, j0), send_l.at[w]).start()

        @pl.when(r != owner)
        def _():
            mate_part(w).start()

    def token_copy(which, k, h, wait):
        src, dst = ((tok, xf), (og, ogh))[which]
        ssem = (send_t, send_g)[which].at[k * 2 + h]
        rsem = (recv_t, recv_g)[which].at[c]
        sref = src.at[pl.ds(k * 2 * half + h * half, half)]
        dref = dst.at[pl.ds(0, half), ds(c * 256, 256)]
        z = 2 * r + k
        me = jnp.logical_and(z == c, r == h)
        remote = pltpu.make_async_remote_copy(
            sref, dref, ssem, rsem, device_id={"core": h, "col": z}, device_id_type=MESH)
        if not wait:
            @pl.when(me)
            def _():
                pltpu.make_async_copy(sref, dref, rsem).start()

        @pl.when(jnp.logical_not(me))
        def _():
            remote.wait_send() if wait else remote.start()

    def mate_copy(q):
        src = xf.at[pl.ds(0, half), pl.ds(q * 256, 256)]
        dst = xf.at[pl.ds(half, half), pl.ds(q * 256, 256)]
        return pltpu.make_async_remote_copy(
            src, dst, send_m.at[q], recv_m.at[q], device_id={"core": 1 - r}, device_id_type=MESH)

    def par_copy(s):
        return pltpu.make_async_remote_copy(
            par, parf.at[:, ds(c * 256, 256)], send_p.at[s], recv_p.at[c],
            device_id={"col": lax.rem(c + s, 4)}, device_id_type=MESH)

    def forward(w, j, rr, up, wait):
        origin = 2 * r + j
        ref = piece(w, rr, d, j)
        copy = pltpu.make_async_remote_copy(
            ref, ref, send_f.at[w, j * 2 + rr], recv_a.at[w, j * 2 + rr],
            device_id={"col": lax.rem(c + (1 if up else 3), 4)}, device_id_type=MESH)

        @pl.when(jnp.logical_and(origin < c if up else origin > c, outer(up)))
        def _():
            copy.wait_send() if wait else copy.start()

    def b_copy(w, j, rr, p):
        ref = piece(w, rr, d, j)
        return pltpu.make_async_remote_copy(
            ref, ref, send_b.at[w, j * 2 + rr, p], recv_b.at[w, j * 2 + rr, p],
            device_id={"dp": peers[p]}, device_id_type=MESH)

    def c_copy(w, j, rr, p):
        ref = piece(w, rr, peers[p], j, p)
        return pltpu.make_async_remote_copy(
            ref, ref, send_c.at[w, j * 2 + rr, p], recv_c.at[w, j * 2 + rr, p],
            device_id={"dp": peers[1 - p]}, device_id_type=MESH)

    def b_step(w, near, rr):
        j = 1 - r if near else r

        @pl.when(2 * r + j != c)
        def _():
            wait_for(piece(w, rr, d, j), recv_a.at[w, j * 2 + rr])
            for up in (0, 1):
                forward(w, j, rr, up, False)
            for p in range(2):
                b_copy(w, j, rr, p).start()

    def c_step(w, near, rr):
        j = 1 - r if near else r

        @pl.when(2 * r + j != c)
        def _():
            for p in range(2):
                wait_for(piece(w, rr, peers[p], j), recv_b.at[w, j * 2 + rr, p])
                c_copy(w, j, rr, p).start()

    def finish_weight(w):
        @pl.when(r == owner)
        def _():
            wait_for(whole(w, r, j0), send_l.at[w])
            wait_for(whole(w, 1 - r, j0), recv_l.at[w])

        for j in range(2):
            @pl.when(2 * r + j != c)
            def _():
                for rr in range(2):
                    for p in range(2):
                        wait_for(piece(w, rr, far, j, p), recv_c.at[w, j * 2 + rr, p])

    seg_send = pltpu.make_async_remote_copy(
        seg, segs.at[r], send_s.at[0], recv_s.at[r], device_id={"core": 1 - r}, device_id_type=MESH)
    seg_own = pltpu.make_async_copy(seg, segs.at[r], recv_s.at[r])
    start_a(0)
    for s in range(1, 4):
        par_copy(s).start()
    pltpu.make_async_copy(par, parf.at[:, ds(c * 256, 256)], recv_p.at[c]).start()
    seg_send.start()
    seg_own.start()
    steps = [(w, near, rr) for w in range(4) for near in (1, 0) for rr in range(2)]

    def advance(i, lag):
        b_step(*steps[i])
        c_step(*steps[i - lag])

    for i in range(2):
        b_step(*steps[i])
    start_a(1)
    for i in range(2, 4):
        b_step(*steps[i])
    for k in range(2):
        for h in range(2):
            token_copy(0, k, h, False)
    start_a(2)
    start_a(3)
    for i in range(4):
        c_step(*steps[i])
    for q in range(4):
        wait_for(xf.at[pl.ds(0, half), pl.ds(q * 256, 256)], recv_t.at[q])
        mate_copy(q).start()
    for rr in range(2):
        wait_for(segs.at[rr], recv_s.at[rr])
    length, part = xf.shape[0], wqf.shape[1] // 6
    segr[:, 0:half] = jnp.broadcast_to(segs[owner, pl.ds(j0, 1), ds(r * half, half)], (8, half))
    segr[:, half:] = jnp.broadcast_to(segs[owner, pl.ds(j0, 1), ds((1 - r) * half, half)], (8, half))
    segc[...] = jnp.transpose(jnp.broadcast_to(segr[0:1, :], (128, length)))
    finish_weight(0)
    for q in range(4):
        wait_for(parf.at[:, pl.ds(q * 256, 256)], recv_p.at[q])

    def project(t, carry):
        place = ds(t * 256, 256)

        @pl.when(t == half // 256)
        def _():
            for q in range(4):
                wait_for(xf.at[pl.ds(half, half), pl.ds(q * 256, 256)], recv_m.at[q])
        for j in range(2):
            lanes = slice(j * 3 * part, (j + 1) * 3 * part)
            value = jnp.dot(xf[place, :], wqf[:, lanes], preferred_element_type=F32)
            bias = parf[:, ds(r * 2 * part + j * part, part)].astype(F32)
            low = j * 3 * part
            qkv[place, low : low + part] = (value[:, :part] + bias[0:1]).astype(BF)
            qkv[place, low + part : low + 2 * part] = value[:, part : 2 * part].astype(BF)
            qkv[place, low + 2 * part : low + 3 * part] = (value[:, 2 * part :] + bias[1:2]).astype(BF)
        for k in range(4):
            @pl.when(t == k)
            def _():
                b_step(*steps[4 + k])
        return carry
    lax.fori_loop(0, length // 256, project, 0)
    pairs = (
        (xf, x_out), (wqf, wq_out), (wof, wo_out), (wuf, wu_out), (wdf, wd_out), (qkv, qkv_out), (ctx, ctx_out), (normed, normed_out),
        (hidden, hidden_out), (act, act_out), (slope, slope_out), (outh, out_half), (two, two_out), (mix, mix_out))
    stores = [pltpu.make_async_copy(near, out, store.at[i]) for i, (near, out) in enumerate(pairs)]
    for i in (0, 1, 5):
        stores[i].start()

    def to_mate(src, dst, i):
        return pltpu.make_async_remote_copy(
            src, dst, send_x.at[i], recv_x.at[i], device_id={"core": 1 - r}, device_id_type=MESH)

    top_half, low_half = pl.ds(0, half), pl.ds(half, half)
    swaps = [
        to_mate(wof, wom, 0), to_mate(ctx.at[low_half], ctxm, 1), to_mate(hidden.at[top_half], hidden.at[low_half], 2),
        to_mate(mate_out.at[pl.ds(0, 256)], mate_in.at[pl.ds(0, 256)], 3),
        to_mate(mate_out.at[pl.ds(256, 256)], mate_in.at[pl.ds(256, 256)], 4), to_mate(mix.at[top_half], mix.at[low_half], 5)]

    rows = 256

    def pair(i, carry):
        base = (i // 2) * 3 * part + lax.rem(i, 2) * 128
        tq[...] = qkv[:, ds(base, 128)]
        tk[...] = qkv[:, ds(base + part, 128)]
        tv[...] = qkv[:, ds(base + 2 * part, 128)]
        seg_k = segr[0:1, :]
        for h in range(2):
            lanes = slice(h * HEAD_DIM, (h + 1) * HEAD_DIM)
            k, v = tk[:, lanes], tv[:, lanes]
            for start in range(0, length, rows):
                q = tq[start : start + rows, lanes]
                s = lax.dot_general(q, k, CONTRACT_LAST, preferred_element_type=F32) * (scale * LOG2E)
                s = jnp.where(segc[start : start + rows, 0:1] == seg_k, s, -1e9 * LOG2E)
                top = jnp.max(s, axis=1, keepdims=True)
                e = jnp.exp2(s - top)
                total = jnp.sum(e, axis=1, keepdims=True)
                out = jnp.dot(e.astype(BF), v, preferred_element_type=F32) / total
                tc[start : start + rows, lanes] = out.astype(BF)
                log_total = top + jnp.log2(total)
                lse[i, h : h + 1, start : start + rows] = jnp.transpose(jnp.broadcast_to(log_total, (rows, 128)))[0:1, :]
            for k in range(4):
                @pl.when(i == k)
                def _():
                    advance(8 + 2 * k + h, 4)
        ctx[:, ds(i * 128, 128)] = tc[...]

        @pl.when(i == 2)
        def _():
            finish_weight(1)
            swaps[0].start()
            stores[2].start()
        return carry
    lax.fori_loop(0, ctx.shape[1] // 128, pair, 0)

    swaps[1].start()
    stores[6].start()
    for k in range(2):
        for h in range(2):
            token_copy(1, k, h, False)
    c_step(*steps[12])
    c_step(*steps[13])
    rowsf = parf[...].astype(F32)
    swaps[0].wait_recv()
    swaps[1].wait_recv()

    def out_rows(t, carry):
        place = ds(t * 256, 256)
        value = jnp.dot(ctx[place, :], wof[...], preferred_element_type=F32) + jnp.dot(ctxm[place, :], wom[...], preferred_element_type=F32)
        value = xf[place, :].astype(F32) + value + rowsf[2:3]
        out, norm, inv = normalize(value, rowsf[3:4], rowsf[4:5])
        hidden_one[place, :] = out
        normed[place, :] = norm
        inverse[place, :] = inv
        hidden[place, :] = out.astype(BF)
        return carry
    lax.fori_loop(0, half // 256, out_rows, 0)
    swaps[2].start()
    stores[7].start()
    c_step(*steps[14])
    c_step(*steps[15])
    finish_weight(2)
    stores[3].start()
    n = act.shape[1] // 2
    bias = []
    for j in range(2):
        block = parf[:, ds(r * 2 * part + j * part, part)].astype(F32)
        bias.append(jnp.concatenate([block[8 + k : 9 + k] for k in range(4)], axis=1))

    def up_rows(t, carry):
        place = ds(t * 256, 256)

        @pl.when(t == half // 256)
        def _():
            swaps[2].wait_recv()
            stores[8].start()
        for j in range(2):
            lanes = slice(j * n, (j + 1) * n)
            value = jnp.dot(hidden[place, :], wuf[:, lanes], preferred_element_type=F32) + bias[j]
            gate = 0.5 * (1.0 + lax.erf(value * math.sqrt(0.5)))
            act[place, lanes] = (value * gate).astype(BF)
            slope[place, lanes] = (gate + value * (math.sqrt(0.5 / math.pi) * jnp.exp(-0.5 * value * value))).astype(BF)
        return carry
    lax.fori_loop(0, length // 256, up_rows, 0)
    stores[9].start()
    stores[10].start()
    finish_weight(3)
    stores[4].start()
    vec[...] = jnp.zeros(vec.shape, F32)

    def mate_rows(t, carry):
        mate_out[ds(t * 256, 256), :] = jnp.dot(act[ds(half + t * 256, 256), :], wdf[...], preferred_element_type=F32)
        for k in range(2):
            @pl.when(t == k)
            def _():
                swaps[3 + k].start()
        return carry
    lax.fori_loop(0, half // 256, mate_rows, 0)
    for q in range(4):
        wait_for(ogh.at[:, pl.ds(q * 256, 256)], recv_g.at[q])

    def last_rows(t, carry):
        place = ds(t * 256, 256)
        value = jnp.dot(act[place, :], wdf[...], preferred_element_type=F32)
        for k in range(2):
            @pl.when(t == k)
            def _():
                swaps[3 + k].wait_recv()
        value = hidden_one[place, :] + (value + mate_in[place, :]) + rowsf[5:6]
        out, norm, inv = normalize(value, rowsf[6:7], rowsf[7:8])
        outh[place, :] = out.astype(BF)
        dy = ogh[place, :].astype(F32)
        scaled = dy * rowsf[6:7]
        mean = jnp.mean(scaled, axis=1, keepdims=True)
        slant = jnp.mean(scaled * norm, axis=1, keepdims=True)
        grad = inv * (scaled - mean - norm * slant)
        two[place, :] = grad
        mix[place, :] = grad.astype(BF)
        vec[3:4, :] += jnp.sum(grad, axis=0, keepdims=True)
        vec[4:5, :] += jnp.sum(dy * norm, axis=0, keepdims=True)
        vec[5:6, :] += jnp.sum(dy, axis=0, keepdims=True)
        return carry
    lax.fori_loop(0, half // 256, last_rows, 0)
    swaps[5].start()
    stores[11].start()
    stores[12].start()
    for s in range(1, 4):
        par_copy(s).wait_send()
    seg_send.wait_send()
    swaps[5].wait_recv()
    stores[13].start()
    for copy in swaps:
        copy.wait_send()
    for q in range(4):
        mate_copy(q).wait_send()
    for which in range(2):
        for k in range(2):
            for h in range(2):
                token_copy(which, k, h, True)
    for w in range(4):
        for up in (0, 1):
            @pl.when(outer(up))
            def _():
                a_copy(w, up).wait_send()

        @pl.when(r != owner)
        def _():
            mate_part(w).wait_send()

        for j in range(2):
            @pl.when(2 * r + j != c)
            def _():
                for rr in range(2):
                    for up in (0, 1):
                        forward(w, j, rr, up, True)
                    for p in range(2):
                        b_copy(w, j, rr, p).wait_send()
                        c_copy(w, j, rr, p).wait_send()
    for copy in stores:
        copy.wait()


def gather(tok, og, par, seg, weights, scale):
    dma = pltpu.SemaphoreType.DMA
    vmem, anywhere = pl.BlockSpec(memory_space=pltpu.VMEM), pl.BlockSpec(memory_space=pl.ANY)
    half, width = tok.shape[0] // 4, tok.shape[1] * 4
    length, heads, units = 2 * half, weights[1].shape[0] * 2, weights[2].shape[1] * 2
    rows = (half, width)
    out = [((16, width), BF), ((heads // 128, 2, length), F32), ((length, 128), jnp.int32), ((8, length), jnp.int32), ((half, 1), F32), ((16, width), F32)]
    large = [((length, width), BF)] + [((w.shape[0] * 2, w.shape[1] * 2), BF) for w in weights]
    large += [((length, 3 * heads), BF), ((length, heads), BF), (rows, F32), ((length, width), BF), ((length, units), BF), ((length, units), BF)]
    large += [(rows, BF), (rows, F32), ((length, width), BF)]
    scratch = large + [(rows, BF), ((heads, width), BF), ((half, heads), BF)] + [(rows, F32)] * 3 + [((2,) + seg.shape, jnp.int32)]
    scratch += [((length, 128), BF)] * 4
    sems = [(4, 2), (4, 4), (4, 4)] + [(4, 4, 2)] * 4 + [(4,)] * 10 + [(1,), (2,), (6,), (6,), (14,)]
    return pl.pallas_call(
        partial(gather_kernel, scale=scale),
        out_shape=[jax.ShapeDtypeStruct(s, t) for s, t in out + large],
        in_specs=[vmem] * 8,
        out_specs=[vmem] * 6 + [anywhere] * 14,
        scratch_shapes=[pltpu.VMEM(s, t) for s, t in scratch] + [dma(s) for s in sems],
        compiler_params=pltpu.CompilerParams(collective_id=0, has_side_effects=True, vmem_limit_bytes=VMEM_LIMIT),
        name="gather",
    )(tok, og, par, seg, *weights)


def mid_kernel(
    inverse, gain, vec_in, out_half, act_far, cols_far, mix_far, slope_far, wd_far, two_far, normed_far, hidden_far, wu_far, wo_far,
    outp, gu_out, attn_out, do, one_grad, vec, gsum,
    act, attn, mix, slope, wd, two_grad, normed, hidden, wu, wo, gd, gu, up_low, ub, mate_out, mate_in, first, second,
    send1, recv1, send2, recv2, send_y, recv_y, send_m, recv_m, load, store,
):
    d, r, c = lax.axis_index("dp"), lax.axis_index("core"), lax.axis_index("col")
    a, b = d // 2, lax.rem(d, 2)
    barrier = pltpu.get_barrier_semaphore()
    for s in range(4):
        for o in range(2):
            if s or o:
                target = {"core": lax.rem(r + o, 2), "col": lax.rem(c + s, 4)}
                pl.semaphore_signal(barrier, inc=1, device_id=target, device_id_type=MESH)
    x_peer, y_peer = lax.bitwise_xor(d, 1), lax.bitwise_xor(d, 2)
    for p in (x_peer, y_peer):
        pl.semaphore_signal(barrier, inc=1, device_id={"dp": p}, device_id_type=MESH)
    pl.semaphore_wait(barrier, 9)

    half, n = out_half.shape[0], gd.shape[1] // 2
    size = gd.shape[0] // 4

    def local(j, slab):
        return gd.at[ds(slab * size, size), pl.ds(j * n, n)]

    def slab_of(j, i, mine):
        if j == 0:
            return i * 2 + (b if mine else 1 - b)
        return (a if mine else 1 - a) * 2 + i

    def turn(j, kept):
        own = a if j == 0 else b
        return own if kept else 1 - own

    def copy1(j, kept):
        i = turn(j, kept)
        return pltpu.make_async_remote_copy(
            local(j, slab_of(j, i, False)), first.at[j, i], send1.at[j, i], recv1.at[j, i],
            device_id={"dp": x_peer if j == 0 else y_peer}, device_id_type=MESH)

    def copy2(j):
        return pltpu.make_async_remote_copy(
            first.at[j, turn(j, False)], second.at[j], send2.at[j], recv2.at[j],
            device_id={"dp": y_peer if j == 0 else x_peer}, device_id_type=MESH)

    def token_copy(q, wait):
        rr, k = c // 2, lax.rem(c, 2)
        sref = out_half.at[:, pl.ds(q * 256, 256)]
        dref = outp.at[ds(k * 2 * half + r * half, half)]
        sem = recv_y.at[k * 2 + r]
        me = jnp.logical_and(rr == r, q == c)
        remote = pltpu.make_async_remote_copy(
            sref, dref, send_y.at[q], sem, device_id={"core": rr, "col": q}, device_id_type=MESH)
        if not wait:
            @pl.when(me)
            def _():
                pltpu.make_async_copy(sref, dref, sem).start()

        @pl.when(jnp.logical_not(me))
        def _():
            remote.wait_send() if wait else remote.start()

    for q in range(4):
        token_copy(q, False)
    far_near = (
        (cols_far, attn), (act_far, act), (mix_far, mix), (wd_far, wd), (slope_far, slope), (wu_far, wu), (two_far, two_grad),
        (normed_far, normed), (hidden_far, hidden), (wo_far, wo))
    loads = [pltpu.make_async_copy(far, near, load.at[i]) for i, (far, near) in enumerate(far_near)]
    for copy in loads:
        copy.start()
    vec[...] = vec_in[...]
    ub[...] = jnp.zeros(ub.shape, F32)
    loads[0].wait()
    loads[1].wait()

    def down_rows(t, carry):
        slab = lax.bitwise_xor(d, 3 - t)
        xt = jnp.transpose(attn[:, ds(slab * size, size)])
        for j in range(2):
            lanes = slice(j * n, (j + 1) * n)
            gd[ds(slab * size, size), lanes] = jnp.dot(xt, act[:, lanes], preferred_element_type=F32).astype(BF)
        for k, sends in ((0, ((0, False), (1, False))), (1, ((1, True),)), (2, ((0, True),))):
            @pl.when(t == k)
            def _():
                for j, kept in sends:
                    copy1(j, kept).start()
        return carry
    lax.fori_loop(0, 4, down_rows, 0)
    for copy in loads[2:5]:
        copy.wait()

    def up_rows(t, carry):
        place = ds(t * 256, 256)
        for j in range(2):
            lanes = slice(j * n, (j + 1) * n)
            value = lax.dot_general(mix[place, :], wd[lanes, :], CONTRACT_LAST, preferred_element_type=F32) * slope[place, lanes].astype(F32)
            up_low[place, lanes] = value.astype(BF)
            ub[0:1, lanes] += jnp.sum(value, axis=0, keepdims=True)
        return carry
    lax.fori_loop(0, 2 * half // 256, up_rows, 0)

    loads[5].wait()

    def mate_rows(t, carry):
        mate_out[ds(t * 256, 256), :] = lax.dot_general(
            up_low[ds(half + t * 256, 256), :], wu[...], CONTRACT_LAST, preferred_element_type=F32)
        return carry
    lax.fori_loop(0, half // 256, mate_rows, 0)
    mate = pltpu.make_async_remote_copy(
        mate_out, mate_in, send_m.at[0], recv_m.at[0], device_id={"core": 1 - r}, device_id_type=MESH)
    mate.start()
    for copy in loads[6:]:
        copy.wait()

    for j in range(2):
        give = turn(j, False)
        wait_for(first.at[j, give], recv1.at[j, give])
        src, dst = local(j, slab_of(j, give, True)), first.at[j, give]

        def add_two(t, carry):
            rows = ds(t * 64, 64, 64)
            dst[rows, :] = (src[rows, :].astype(F32) + dst[rows, :].astype(F32)).astype(BF)
            return carry
        lax.fori_loop(0, size // 64, add_two, 0)
        copy2(j).start()

    mate.wait_recv()
    width = mate_in.shape[1]
    vec[0:3, :] = jnp.zeros((3, width), F32)

    def own_rows(t, carry):
        place = ds(t * 256, 256)
        value = lax.dot_general(up_low[place, :], wu[...], CONTRACT_LAST, preferred_element_type=F32)
        value = value + mate_in[place, :] + two_grad[place, :]
        norm = normed[place, :]
        scaled = value * gain[...]
        mean = jnp.mean(scaled, axis=1, keepdims=True)
        slant = jnp.mean(scaled * norm, axis=1, keepdims=True)
        grad = inverse[place, :] * (scaled - mean - norm * slant)
        one_grad[place, :] = grad
        attn[place, :] = grad.astype(BF)
        vec[0:1, :] += jnp.sum(grad, axis=0, keepdims=True)
        vec[1:2, :] += jnp.sum(value * norm, axis=0, keepdims=True)
        vec[2:3, :] += jnp.sum(value, axis=0, keepdims=True)
        return carry
    lax.fori_loop(0, half // 256, own_rows, 0)
    pair = pltpu.make_async_remote_copy(
        attn.at[pl.ds(0, half)], attn.at[pl.ds(half, half)], send_m.at[1], recv_m.at[1],
        device_id={"core": 1 - r}, device_id_type=MESH)
    pair.start()

    def weight_rows(t, carry):
        xt = jnp.transpose(hidden[:, ds(t * 256, 256)])
        for j in range(2):
            lanes = slice(j * n, (j + 1) * n)
            gu[ds(t * 256, 256), lanes] = jnp.dot(xt, up_low[:, lanes], preferred_element_type=F32).astype(BF)
        return carry
    lax.fori_loop(0, hidden.shape[1] // 256, weight_rows, 0)
    gu_store = pltpu.make_async_copy(gu, gu_out, store.at[0])
    gu_store.start()
    part = n // 4
    for k in range(4):
        for j in range(2):
            vec[8 + k : 9 + k, ds(r * 2 * part + j * part, part)] = ub[0:1, j * n + k * part : j * n + (k + 1) * part]
    pair.wait_recv()
    attn_store = pltpu.make_async_copy(attn, attn_out, store.at[1])
    attn_store.start()

    def ctx_rows(t, carry):
        place = ds(t * 256, 256)
        do[place, :] = lax.dot_general(attn[place, :], wo[...], CONTRACT_LAST, preferred_element_type=F32).astype(BF)
        return carry
    lax.fori_loop(0, 2 * half // 256, ctx_rows, 0)

    for j in range(2):
        kept = turn(j, True)
        wait_for(first.at[j, kept], recv1.at[j, kept])
        wait_for(second.at[j], recv2.at[j])
        src, more = local(j, slab_of(j, kept, True)), first.at[j, kept]

        def add_three(t, carry):
            rows = ds(t * 64, 64, 64)
            value = src[rows, :].astype(F32) + more[rows, :].astype(F32) + second[j, rows, :].astype(F32)
            gsum[j, rows, :] = value.astype(BF)
            return carry
        lax.fori_loop(0, size // 64, add_three, 0)
    for j in range(2):
        for kept in (False, True):
            copy1(j, kept).wait_send()
        copy2(j).wait_send()
    mate.wait_send()
    pair.wait_send()
    gu_store.wait()
    attn_store.wait()
    for q in range(4):
        token_copy(q, True)
        wait_for(outp.at[pl.ds(q * half, half)], recv_y.at[q])


def middle(out_half, act, cols, mix, slope, wd, two_grad, normed, inverse, gain, vec, hidden, wu, wo):
    dma = pltpu.SemaphoreType.DMA
    vmem, anywhere = pl.BlockSpec(memory_space=pltpu.VMEM), pl.BlockSpec(memory_space=pl.ANY)
    half, width = out_half.shape
    slab = (width // 4, act.shape[1] // 2)
    out = [((4 * half, width // 4), BF), (wu.shape, BF), (cols.shape, BF), ((2 * half, wo.shape[0]), BF), ((half, width), F32), (vec.shape, F32), ((2,) + slab, BF)]
    scratch = [(v.shape, v.dtype) for v in (act, cols, mix, slope, wd, two_grad, normed, hidden, wu, wo)]
    scratch += [(wu.shape, BF), (wu.shape, BF), (slope.shape, BF)]
    scratch += [((8, slope.shape[1]), F32), ((half, width), F32), ((half, width), F32), ((2, 2) + slab, BF), ((2,) + slab, BF)]
    sems = [(2, 2), (2, 2), (2,), (2,), (4,), (4,), (2,), (2,), (10,), (2,)]
    return pl.pallas_call(
        mid_kernel,
        out_shape=[jax.ShapeDtypeStruct(s, t) for s, t in out],
        in_specs=[vmem] * 3 + [anywhere] * 11,
        out_specs=[anywhere] * 3 + [vmem] * 4,
        scratch_shapes=[pltpu.VMEM(s, t) for s, t in scratch] + [dma(s) for s in sems],
        compiler_params=pltpu.CompilerParams(collective_id=2, has_side_effects=True, vmem_limit_bytes=VMEM_LIMIT),
        name="mid",
    )(inverse, gain, vec, out_half, act, cols, mix, slope, wd, two_grad, normed, hidden, wu, wo)


def back_kernel(
    lse, segk, segq, vec, qkv_far, do_far, ctx_far, gu_far, attn_far, x_far, wq_far, one_far, gsum,
    inp, total, rq, ro, ru, rd,
    qkv, do, ctx, gu, attn, x, wq, one_grad, go, inp_low, gq, low, tq, tk, tv, tg, vbuf, mate_out, mate_in, in_half,
    r1q, r1o, r1u, r1v, r2q, r2o, r2u, r2v, r3q, r3o, r3u, r3d, r3v, tall, v1, s4, v2,
    send1, recv1, send2, recv2, send3, recv3, send_i, recv_i, send_v, recv_v, send_w, recv_w, send_m, recv_m, load,
    *, scale,
):
    d, r, c = lax.axis_index("dp"), lax.axis_index("core"), lax.axis_index("col")
    a, b = d // 2, lax.rem(d, 2)
    barrier = pltpu.get_barrier_semaphore()
    for s in range(4):
        for o in range(2):
            if s or o:
                target = {"core": lax.rem(r + o, 2), "col": lax.rem(c + s, 4)}
                pl.semaphore_signal(barrier, inc=1, device_id=target, device_id_type=MESH)
    x_peer, y_peer = lax.bitwise_xor(d, 1), lax.bitwise_xor(d, 2)
    plane = [(p, o) for p in range(4) for o in range(2) if p or o]
    for p, o in plane:
        if p:
            target = {"dp": lax.bitwise_xor(d, p), "core": lax.rem(r + o, 2)}
            pl.semaphore_signal(barrier, inc=1, device_id=target, device_id_type=MESH)
    pl.semaphore_wait(barrier, 13)

    first, second = (r1q, r1o, r1u, None, r1v), (r2q, r2o, r2u, None, r2v)
    third = (r3q, r3o, r3u, r3d, r3v)
    by_rows = (True, False, True, True, True)
    half_up = gu.shape[1] // 4
    result = (rq, ro, ru.at[:, pl.ds(0, half_up)], rd, ru.at[:, pl.ds(half_up, half_up)])
    length, part3q = low.shape[0], low.shape[1] // 2
    part = part3q // 3

    def local(w, j, slab, far=False):
        if w == 0:
            return gq.at[j, slab]
        if w == 1:
            rows, cols = go.shape
            return go.at[pl.ds(j * (rows // 2), rows // 2), ds(slab * (cols // 4), cols // 4)]
        ref, start = gu_far if far else gu, 2 * j * half_up + (half_up if w == 4 else 0)
        return ref.at[ds(slab * (gu.shape[0] // 4), gu.shape[0] // 4), pl.ds(start, half_up)]

    def slab_of(j, i, mine):
        if j == 0:
            return i * 2 + (b if mine else 1 - b)
        return (a if mine else 1 - a) * 2 + i

    def turn(j, kept):
        own = a if j == 0 else b
        return own if kept else 1 - own

    def copy1(w, j, kept):
        i = turn(j, kept)
        return pltpu.make_async_remote_copy(
            local(w, j, slab_of(j, i, False), True), first[w].at[j, i], send1.at[w, j, i], recv1.at[w, j, i],
            device_id={"dp": x_peer if j == 0 else y_peer}, device_id_type=MESH)

    def copy2(w, j):
        return pltpu.make_async_remote_copy(
            first[w].at[j, turn(j, False)], second[w].at[j], send2.at[w, j], recv2.at[w, j],
            device_id={"dp": y_peer if j == 0 else x_peer}, device_id_type=MESH)

    def copy3(w, j, rr, wait):
        src = gsum.at[j] if w == 3 else first[w].at[j, turn(j, True)]
        src = src.at[pl.ds(rr * 128, 128), :] if by_rows[w] else src.at[:, pl.ds(rr * 128, 128)]
        dst = third[w].at[c]
        z = 2 * r + j
        me = jnp.logical_and(z == c, r == rr)
        remote = pltpu.make_async_remote_copy(
            src, dst, send3.at[w, j, rr], recv3.at[w, c], device_id={"core": rr, "col": z}, device_id_type=MESH)
        if not wait:
            @pl.when(me)
            def _():
                pltpu.make_async_copy(src, dst, recv3.at[w, c]).start()

        @pl.when(jnp.logical_not(me))
        def _():
            remote.wait_send() if wait else remote.start()

    def send_first(w, kept):
        for j in range(2):
            copy1(w, j, kept).start()

    def step2(w):
        for j in range(2):
            give = turn(j, False)
            wait_for(first[w].at[j, give], recv1.at[w, j, give])
            src, dst = local(w, j, slab_of(j, give, True)), first[w].at[j, give]

            def body(t, carry):
                rows = ds(t * 64, 64, 64)
                dst[rows, :] = (src[rows, :].astype(F32) + dst[rows, :].astype(F32)).astype(BF)
                return carry
            lax.fori_loop(0, dst.shape[0] // 64, body, 0)
            copy2(w, j).start()

    def step3(w):
        for j in range(2):
            kept = turn(j, True)
            wait_for(first[w].at[j, kept], recv1.at[w, j, kept])
            wait_for(second[w].at[j], recv2.at[w, j])
            src, dst, more = local(w, j, slab_of(j, kept, True)), first[w].at[j, kept], second[w].at[j]

            def body(t, carry):
                rows = ds(t * 64, 64, 64)
                dst[rows, :] = (src[rows, :].astype(F32) + dst[rows, :].astype(F32) + more[rows, :].astype(F32)).astype(BF)
                return carry
            lax.fori_loop(0, dst.shape[0] // 64, body, 0)
            for rr in range(2):
                copy3(w, j, rr, False)

    def finish(w):
        for z in range(4):
            wait_for(third[w].at[z], recv3.at[w, z])

        def body(t, carry):
            rows = ds(t * 64, 64, 64)
            value = (third[w][0, rows, :].astype(F32) + third[w][1, rows, :].astype(F32)) + (
                third[w][2, rows, :].astype(F32) + third[w][3, rows, :].astype(F32))
            if w == 3:
                tall[rows, :] = value
            else:
                result[w][rows, :] = value
            return carry
        lax.fori_loop(0, third[w].shape[1] // 64, body, 0)
        if w == 3:
            rd[...] = jnp.transpose(tall[...])

    half = in_half.shape[0]

    def token_copy(q, wait):
        rr, k = c // 2, lax.rem(c, 2)
        sref = in_half.at[:, pl.ds(q * 256, 256)]
        dref = inp_low.at[ds(k * 2 * half + r * half, half)]
        sem = recv_i.at[k * 2 + r]
        me = jnp.logical_and(rr == r, q == c)
        remote = pltpu.make_async_remote_copy(
            sref, dref, send_i.at[q], sem, device_id={"core": rr, "col": q}, device_id_type=MESH)
        if not wait:
            @pl.when(me)
            def _():
                pltpu.make_async_copy(sref, dref, sem).start()

        @pl.when(jnp.logical_not(me))
        def _():
            remote.wait_send() if wait else remote.start()

    def vec_z(s):
        z = lax.rem(c + s, 4)
        return pltpu.make_async_remote_copy(
            vbuf.at[:, ds(z * 256, 256)], v1.at[s], send_v.at[s], recv_v.at[s], device_id={"col": z}, device_id_type=MESH)

    def vec_plane(i):
        p, o = plane[i]
        return pltpu.make_async_remote_copy(
            s4, v2.at[i], send_w.at[i], recv_w.at[i],
            device_id={"dp": lax.bitwise_xor(d, p), "core": lax.rem(r + o, 2)}, device_id_type=MESH)

    mate = pltpu.make_async_remote_copy(
        mate_out, mate_in, send_m.at[0], recv_m.at[0], device_id={"core": 1 - r}, device_id_type=MESH)

    send_first(2, False)
    send_first(2, True)
    for j in range(2):
        for rr in range(2):
            copy3(3, j, rr, False)
    far_near = (
        (qkv_far, qkv), (do_far, do), (ctx_far, ctx), (gu_far, gu), (attn_far, attn), (x_far, x), (wq_far, wq), (one_far, one_grad))
    loads = [pltpu.make_async_copy(far, near, load.at[i]) for i, (far, near) in enumerate(far_near)]
    for copy in loads:
        copy.start()
    vbuf[...] = vec[...]
    for copy in loads[:3]:
        copy.wait()

    rows = 256

    def pair(i, carry):
        base = (i // 2) * part3q + lax.rem(i, 2) * 128
        tq[...] = qkv[:, ds(base, 128)]
        tg[...] = do[:, ds(i * 128, 128)]
        prod = jnp.transpose(tg[...].astype(F32) * ctx[:, ds(i * 128, 128)].astype(F32))
        tk[...] = qkv[:, ds(base + part, 128)]
        tv[...] = qkv[:, ds(base + 2 * part, 128)]
        seg_q = segq[0:1, :]
        for h in range(2):
            lanes = slice(h * HEAD_DIM, (h + 1) * HEAD_DIM)
            qh, doh = tq[:, lanes], tg[:, lanes]
            delta = jnp.sum(prod[h * HEAD_DIM : (h + 1) * HEAD_DIM], axis=0, keepdims=True)
            top = lse[i, h : h + 1, :]
            dqt = jnp.zeros((HEAD_DIM, length), F32)
            vsum = jnp.zeros((1, HEAD_DIM), F32)
            for start in range(0, length, rows):
                kh = tk[start : start + rows, lanes]
                vh = tv[start : start + rows, lanes]
                s = lax.dot_general(kh, qh, CONTRACT_LAST, preferred_element_type=F32) * (scale * LOG2E)
                s = jnp.where(segk[start : start + rows, 0:1] == seg_q, s, -1e9 * LOG2E)
                p = jnp.exp2(s - top)
                dp = lax.dot_general(vh, doh, CONTRACT_LAST, preferred_element_type=F32)
                g = (p * (dp - delta)).astype(BF)
                dk = jnp.dot(g, qh, preferred_element_type=F32) * scale
                tk[start : start + rows, lanes] = dk.astype(BF)
                dv = jnp.dot(p.astype(BF), doh, preferred_element_type=F32)
                tv[start : start + rows, lanes] = dv.astype(BF)
                vsum += jnp.sum(dv, axis=0, keepdims=True)
                dqt += jnp.dot(jnp.transpose(kh), g, preferred_element_type=F32)
            dq = jnp.transpose(dqt) * scale
            tq[:, lanes] = dq.astype(BF)
            v1[0, h : h + 1, 0:HEAD_DIM] = jnp.sum(dq, axis=0, keepdims=True)
            v1[0, h : h + 1, 128 : 128 + HEAD_DIM] = vsum
        low[:, ds(base, 128)] = tq[...]
        low[:, ds(base + part, 128)] = tk[...]
        low[:, ds(base + 2 * part, 128)] = tv[...]
        place = ds(r * 2 * part + i * 128, 128)
        vbuf[6:7, place] = jnp.concatenate([v1[0, 0:1, 0:HEAD_DIM], v1[0, 1:2, 0:HEAD_DIM]], axis=1)
        vbuf[7:8, place] = jnp.concatenate([v1[0, 0:1, 128 : 128 + HEAD_DIM], v1[0, 1:2, 128 : 128 + HEAD_DIM]], axis=1)

        @pl.when(i == 0)
        def _():
            for copy in loads[3:]:
                copy.wait()
            step2(2)
            send_first(4, False)
            send_first(4, True)

        @pl.when(i == 2)
        def _():
            step3(2)
            step2(4)
        return carry
    lax.fori_loop(0, do.shape[1] // 128, pair, 0)

    for s in range(1, 4):
        vec_z(s).start()

    def out_rows(t, carry):
        xt = jnp.transpose(ctx[:, ds(t * 256, 256)])
        go[ds(t * 256, 256), :] = jnp.dot(xt, attn[...], preferred_element_type=F32).astype(BF)
        return carry
    lax.fori_loop(0, ctx.shape[1] // 256, out_rows, 0)
    send_first(1, False)
    send_first(1, True)

    def weight_rows(t, carry):
        xt = jnp.transpose(x[:, ds(t * 256, 256)])
        for j in range(2):
            gq[j, t] = jnp.dot(xt, low[:, j * part3q : (j + 1) * part3q], preferred_element_type=F32).astype(BF)
        return carry
    lax.fori_loop(0, 4, weight_rows, 0)
    send_first(0, False)
    send_first(0, True)

    def mate_rows(t, carry):
        mate_out[ds(t * 256, 256), :] = lax.dot_general(
            low[ds(half + t * 256, 256), :], wq[...], CONTRACT_LAST, preferred_element_type=F32)
        return carry
    lax.fori_loop(0, half // 256, mate_rows, 0)
    mate.start()
    step3(4)
    for s in range(1, 4):
        vec_z(s).wait()
    s4[...] = (vbuf[:, ds(c * 256, 256)] + v1[1]) + (v1[2] + v1[3])
    for i in range(7):
        vec_plane(i).start()
    mate.wait_recv()

    def own_rows(t, carry):
        place = ds(t * 256, 256)
        value = lax.dot_general(low[place, :], wq[...], CONTRACT_LAST, preferred_element_type=F32)
        in_half[place, :] = (value + mate_in[place, :] + one_grad[place, :]).astype(BF)
        return carry
    lax.fori_loop(0, half // 256, own_rows, 0)
    for q in range(4):
        token_copy(q, False)
    step2(1)
    step2(0)
    step3(1)
    finish(3)
    for i in range(7):
        vec_plane(i).wait()
    total[...] = ((s4[...] + v2[0]) + (v2[1] + v2[2])) + ((v2[3] + v2[4]) + (v2[5] + v2[6]))
    finish(2)
    finish(4)
    for q in range(4):
        place = pl.ds(q * half, half)
        wait_for(inp_low.at[place], recv_i.at[q])
        inp[place, :] = inp_low[place, :].astype(F32)
    step3(0)
    finish(1)
    finish(0)
    for w in range(5):
        for j in range(2):
            for i in range(2):
                if w != 3:
                    copy1(w, j, i).wait_send()
                copy3(w, j, i, True)
            if w != 3:
                copy2(w, j).wait_send()
    mate.wait_send()
    for q in range(4):
        token_copy(q, True)


def back(x, wq, qkv, do, ctx, lse, segk, segq, one_grad, vec, grads, scale):
    dma = pltpu.SemaphoreType.DMA
    vmem, anywhere = pl.BlockSpec(memory_space=pltpu.VMEM), pl.BlockSpec(memory_space=pl.ANY)
    half, width = one_grad.shape
    far = (qkv, do, ctx, grads[1], grads[0], x, wq, one_grad)
    length, part = 2 * half, width // 4
    rows_q, heads, units = wq.shape[1] // 2, do.shape[1], grads[1].shape[1] // 2
    slab, own, cut = width // 4, width // 8, units // 2
    out = [((4 * half, part), F32), ((vec.shape[0], part), F32), ((own, rows_q), F32), ((heads // 2, own), F32), ((own, units), F32), ((units, own), F32)]
    slabs = [(slab, rows_q), (heads // 2, slab), (slab, cut), (slab, cut)]
    r1, r2 = [(2, 2) + v for v in slabs], [(2,) + v for v in slabs]
    r3 = [(4, own, rows_q), (4, heads // 2, own), (4, own, cut), (4, own, units), (4, own, cut)]
    scratch = [(v.shape, v.dtype) for v in far] + [((heads, width), BF), ((4 * half, part), BF), ((2, 4, width // 4, wq.shape[1] // 2), BF), (qkv.shape, BF)] + [((length, 128), BF)] * 4
    scratch += [(vec.shape, F32), ((half, width), F32), ((half, width), F32), ((half, width), BF)]
    scratch += [(s, BF) for s in r1 + r2 + r3] + [(r3[3][1:], F32)]
    scratch += [((4, vec.shape[0], part), F32), ((vec.shape[0], part), F32), ((7, vec.shape[0], part), F32)]
    sems = [(5, 2, 2), (5, 2, 2), (5, 2), (5, 2), (5, 2, 2), (5, 4), (4,), (4,), (4,), (4,), (7,), (7,), (1,), (1,), (8,)]
    return pl.pallas_call(
        partial(back_kernel, scale=scale),
        out_shape=[jax.ShapeDtypeStruct(s, t) for s, t in out],
        in_specs=[vmem] * 4 + [anywhere] * 9,
        out_specs=[vmem] * 6,
        scratch_shapes=[pltpu.VMEM(s, t) for s, t in scratch] + [dma(s) for s in sems],
        compiler_params=pltpu.CompilerParams(collective_id=1, has_side_effects=True, vmem_limit_bytes=VMEM_LIMIT),
        name="back",
    )(lse, segk, segq, vec, *far, grads[2])


def part_rows(values, groups):
    if groups == 1:
        return values
    rows, cols = values.shape
    return values.reshape(4, groups, 2, rows // (8 * groups), cols).transpose(0, 2, 1, 3, 4).reshape(rows, cols)


def on_device(
    tokens, segment_ids, w_qkv, b_qv, w_out, b_out, norm1_gain, norm1_shift,
    w_up, b_up, w_down, b_down, norm2_gain, norm2_shift, out_grad,
):
    groups = lax.axis_size("rh")
    core, col = lax.axis_index("core"), lax.axis_index("col")
    part = tokens.shape[1]
    scale = 1.0 / math.sqrt(HEAD_DIM)
    wq, wo, wu, wd = w_qkv.reshape(w_qkv.shape[0], 3 * part), w_out, w_up, w_down
    if groups > 1:
        both_rows = ("rh", "core")
        wq, wu = (lax.all_gather(w, both_rows, axis=0, tiled=True) for w in (wq, wu))
        wo, wd = (lax.all_gather(w, both_rows, axis=1, tiled=True) for w in (wo, wd))
        wq, wu = (lax.dynamic_slice_in_dim(w, core * (w.shape[0] // 2), w.shape[0] // 2, 0) for w in (wq, wu))
        wo, wd = (lax.dynamic_slice_in_dim(w, core * (w.shape[1] // 2), w.shape[1] // 2, 1) for w in (wo, wd))
    vectors = [b_qv[0], b_qv[1], b_out, norm1_gain, norm1_shift, b_down, norm2_gain, norm2_shift] + [b_up[k * part : (k + 1) * part] for k in range(4)]
    index = lax.broadcasted_iota(jnp.int32, (16, part), 0)
    par = jnp.zeros((16, part), BF)
    for k, vector in enumerate(vectors):
        par = jnp.where(index == k, vector[None], par)
    (params, lse, seg_col, seg_row, inverse_one, vec, x, wq, wo, wu, wd, qkv, ctx, normed_one, hidden, activated, slope, output, two_grad,
     mix) = gather(tokens, out_grad, par, segment_ids, (wq, wo, wu, wd), scale)
    gain1 = params[3:4].astype(F32)
    x_cols, hidden_cols, mix_cols = x, hidden, mix
    if groups > 1:
        x_cols, hidden_cols, mix_cols = (part_rows(v.T, groups).T for v in (x, hidden, mix))
    output, up_wgrad, attn, ctx_grad, one_grad, vec, down_sum = middle(
        output, activated, mix_cols, mix, slope, wd, two_grad, normed_one, inverse_one, gain1, vec, hidden_cols, wu, wo)
    if groups > 1:
        attn = part_rows(attn.T, groups).T
    in_grad, sums, qkv_share, out_share, up_share, down_share = back(
        x_cols, wq, qkv, ctx_grad, ctx, lse, seg_col, seg_row, one_grad, vec, (attn, up_wgrad, down_sum), scale)
    if groups > 1:
        sums = lax.psum(sums, "rh")
        qkv_share, up_share = (lax.psum_scatter(g, "rh", scatter_dimension=0, tiled=True) for g in (qkv_share, up_share))
        out_share, down_share = (lax.psum_scatter(g, "rh", scatter_dimension=1, tiled=True) for g in (out_share, down_share))
    return (
        output,
        in_grad,
        qkv_share.reshape(qkv_share.shape[0], 3, part),
        sums[6:8],
        out_share,
        sums[0],
        sums[1],
        sums[2],
        up_share,
        sums[8:12].reshape(-1),
        down_share,
        sums[3],
        sums[4],
        sums[5],
    )


def solution(mesh):
    dp, row, col = (mesh.shape[name] for name in ("dp", "row", "col"))
    fine = Mesh(mesh.devices.reshape(dp, row // 2, 2, col), ("dp", "rh", "core", "col"))
    row, every = ("rh", "core"), ("dp", "rh", "core")
    return jax.shard_map(
        on_device,
        mesh=fine,
        in_specs=(
            P(every, "col"), P(every, None), P(row, None, "col"), P(None, "col"), P("col", row), P("col"), P("col"), P("col"),
            P(row, "col"), P("col"), P("col", row), P("col"), P("col"), P("col"), P(every, "col"),
        ),
        out_specs=(
            P(every, "col"), P(every, "col"), P(every, None, "col"), P(None, "col"), P("col", every), P("col"), P("col"),
            P("col"), P(every, "col"), P("col"), P("col", every), P("col"), P("col"), P("col"),
        ),
        check_vma=False,
    )
```

```python
from functools import partial
import math

import jax
import jax.numpy as jnp
from jax import lax
from jax.experimental import pallas as pl
from jax.experimental.pallas import tpu as pltpu
from jax.sharding import Mesh, PartitionSpec as P

HEAD_DIM = 64
NORM_EPSILON = 1e-05
MESH = pl.DeviceIdType.MESH
LOG2E = math.log2(math.e)
BF = jnp.bfloat16
F32 = jnp.float32
CONTRACT_LAST = (((1,), (1,)), ((), ()))
CONTRACT_FIRST = (((0,), (0,)), ((), ()))
VMEM_LIMIT = 62 * 2**20


def wait_for(ref, sem):
    pltpu.make_async_copy(ref, ref, sem).wait()


def ds(start, size, multiple=128):
    return pl.ds(pl.multiple_of(start, multiple), size)


def normalize(residual, gain, shift):
    mean = jnp.mean(residual, axis=1, keepdims=True)
    centered = residual - mean
    inverse = lax.rsqrt(jnp.mean(centered * centered, axis=1, keepdims=True) + NORM_EPSILON)
    normed = centered * inverse
    return normed * gain + shift, normed, inverse


def gather_kernel(
    tok, og, par, seg, wq, wo, wu, wd,
    rows_out, lse, segc, segr, inverse, vec,
    x_out, wq_out, wo_out, wu_out, wd_out, qkv_out, ctx_out, normed_out, hidden_out, act_out, slope_out, out_half, two_out, mix_out,
    xf, wqf, wof, wuf, wdf, qkv, ctx, normed, hidden, act, slope, outh, two, mix,
    parf, ogh, wom, ctxm, hidden_one, mate_out, mate_in, segs, tq, tk, tv, tc,
    send_a, recv_a, send_f, send_b, recv_b, send_c, recv_c, recv_l, send_l, send_t, recv_t, send_g, recv_g, send_m, recv_m, send_p, recv_p,
    send_s, recv_s, send_x, recv_x, store,
    *, scale,
):
    d, r, c = lax.axis_index("dp"), lax.axis_index("core"), lax.axis_index("col")
    owner, j0 = c // 2, lax.rem(c, 2)
    half = tok.shape[0] // 4
    barrier = pltpu.get_barrier_semaphore()
    for s in range(4):
        for o in range(2):
            if s or o:
                target = {"core": lax.rem(r + o, 2), "col": lax.rem(c + s, 4)}
                pl.semaphore_signal(barrier, inc=1, device_id=target, device_id_type=MESH)
    x_peer, y_peer, far = (lax.bitwise_xor(d, p) for p in (1, 2, 3))
    peers = (x_peer, y_peer)
    for p in peers:
        pl.semaphore_signal(barrier, inc=1, device_id={"dp": p}, device_id_type=MESH)
    pl.semaphore_wait(barrier, 9)

    source, dest = (wq, wo, wu, wd), (wqf, wof, wuf, wdf)

    def whole(w, rr, j):
        rows, cols = source[w].shape
        if w in (0, 2):
            return dest[w].at[ds(rr * rows, rows), ds(j * cols, cols)]
        return dest[w].at[ds(j * rows, rows), ds(rr * cols, cols)]

    def piece(w, rr, dd, j, part=None):
        rows, cols = source[w].shape
        size = rows // 4
        base = (rr if w in (0, 2) else j) * rows + dd * size
        if part is not None:
            size = size // 2
            base = base + part * size
        return dest[w].at[ds(base, size, 32), ds((j if w in (0, 2) else rr) * cols, cols)]

    def a_copy(w, up):
        size = source[w].shape[0] // 4
        return pltpu.make_async_remote_copy(
            source[w].at[ds(d * size, size, 64)], piece(w, r, d, j0), send_a.at[w, up], recv_a.at[w, j0 * 2 + r],
            device_id={"core": owner, "col": lax.rem(c + (1 if up else 3), 4)}, device_id_type=MESH)

    def outer(up):
        return c < 3 if up else c > 0

    def mate_part(w):
        return pltpu.make_async_remote_copy(
            source[w], whole(w, r, j0), send_l.at[w], recv_l.at[w], device_id={"core": 1 - r}, device_id_type=MESH)

    def start_a(w):
        for up in (0, 1):
            @pl.when(outer(up))
            def _():
                a_copy(w, up).start()

        @pl.when(r == owner)
        def _():
            pltpu.make_async_copy(source[w], whole(w, r, j0), send_l.at[w]).start()

        @pl.when(r != owner)
        def _():
            mate_part(w).start()

    def token_copy(which, k, h, wait):
        src, dst = ((tok, xf), (og, ogh))[which]
        ssem = (send_t, send_g)[which].at[k * 2 + h]
        rsem = (recv_t, recv_g)[which].at[c]
        sref = src.at[pl.ds(k * 2 * half + h * half, half)]
        dref = dst.at[pl.ds(0, half), ds(c * 256, 256)]
        z = 2 * r + k
        me = jnp.logical_and(z == c, r == h)
        remote = pltpu.make_async_remote_copy(
            sref, dref, ssem, rsem, device_id={"core": h, "col": z}, device_id_type=MESH)
        if not wait:
            @pl.when(me)
            def _():
                pltpu.make_async_copy(sref, dref, rsem).start()

        @pl.when(jnp.logical_not(me))
        def _():
            remote.wait_send() if wait else remote.start()

    def mate_copy(q):
        src = xf.at[pl.ds(0, half), pl.ds(q * 256, 256)]
        dst = xf.at[pl.ds(half, half), pl.ds(q * 256, 256)]
        return pltpu.make_async_remote_copy(
            src, dst, send_m.at[q], recv_m.at[q], device_id={"core": 1 - r}, device_id_type=MESH)

    def par_copy(s):
        return pltpu.make_async_remote_copy(
            par, parf.at[:, ds(c * 256, 256)], send_p.at[s], recv_p.at[c],
            device_id={"col": lax.rem(c + s, 4)}, device_id_type=MESH)

    def forward(w, j, rr, up, wait):
        origin = 2 * r + j
        ref = piece(w, rr, d, j)
        copy = pltpu.make_async_remote_copy(
            ref, ref, send_f.at[w, j * 2 + rr], recv_a.at[w, j * 2 + rr],
            device_id={"col": lax.rem(c + (1 if up else 3), 4)}, device_id_type=MESH)

        @pl.when(jnp.logical_and(origin < c if up else origin > c, outer(up)))
        def _():
            copy.wait_send() if wait else copy.start()

    def b_copy(w, j, rr, p):
        ref = piece(w, rr, d, j)
        return pltpu.make_async_remote_copy(
            ref, ref, send_b.at[w, j * 2 + rr, p], recv_b.at[w, j * 2 + rr, p],
            device_id={"dp": peers[p]}, device_id_type=MESH)

    def c_copy(w, j, rr, p):
        ref = piece(w, rr, peers[p], j, p)
        return pltpu.make_async_remote_copy(
            ref, ref, send_c.at[w, j * 2 + rr, p], recv_c.at[w, j * 2 + rr, p],
            device_id={"dp": peers[1 - p]}, device_id_type=MESH)

    def b_step(w, near, rr):
        j = 1 - r if near else r

        @pl.when(2 * r + j != c)
        def _():
            wait_for(piece(w, rr, d, j), recv_a.at[w, j * 2 + rr])
            for up in (0, 1):
                forward(w, j, rr, up, False)
            for p in range(2):
                b_copy(w, j, rr, p).start()

    def c_step(w, near, rr):
        j = 1 - r if near else r

        @pl.when(2 * r + j != c)
        def _():
            for p in range(2):
                wait_for(piece(w, rr, peers[p], j), recv_b.at[w, j * 2 + rr, p])
                c_copy(w, j, rr, p).start()

    def finish_weight(w):
        @pl.when(r == owner)
        def _():
            wait_for(whole(w, r, j0), send_l.at[w])
            wait_for(whole(w, 1 - r, j0), recv_l.at[w])

        for j in range(2):
            @pl.when(2 * r + j != c)
            def _():
                for rr in range(2):
                    for p in range(2):
                        wait_for(piece(w, rr, far, j, p), recv_c.at[w, j * 2 + rr, p])

    seg_send = pltpu.make_async_remote_copy(
        seg, segs.at[r], send_s.at[0], recv_s.at[r], device_id={"core": 1 - r}, device_id_type=MESH)
    seg_own = pltpu.make_async_copy(seg, segs.at[r], recv_s.at[r])
    start_a(0)
    for s in range(1, 4):
        par_copy(s).start()
    pltpu.make_async_copy(par, parf.at[:, ds(c * 256, 256)], recv_p.at[c]).start()
    seg_send.start()
    seg_own.start()
    steps = [(w, near, rr) for w in range(4) for near in (1, 0) for rr in range(2)]

    def tokens_out(which):
        for k in range(2):
            for h in range(2):
                token_copy(which, k, h, False)

    def advance(i):
        b_step(*steps[i])
        if i >= 3:
            c_step(*steps[i - 3])
        if i == 1:
            start_a(1)
        if i == 3:
            tokens_out(0)
            start_a(2)
        if i == 7:
            start_a(3)
        if i == 15:
            tokens_out(1)

    for i in range(8):
        advance(i)
    for q in range(4):
        wait_for(xf.at[pl.ds(0, half), pl.ds(q * 256, 256)], recv_t.at[q])
        mate_copy(q).start()
    for rr in range(2):
        wait_for(segs.at[rr], recv_s.at[rr])
    length, part = xf.shape[0], wqf.shape[1] // 6
    segr[:, 0:half] = jnp.broadcast_to(segs[owner, pl.ds(j0, 1), ds(r * half, half)], (8, half))
    segr[:, half:] = jnp.broadcast_to(segs[owner, pl.ds(j0, 1), ds((1 - r) * half, half)], (8, half))
    segc[...] = jnp.transpose(jnp.broadcast_to(segr[0:1, :], (128, length)))
    finish_weight(0)
    for q in range(4):
        wait_for(parf.at[:, pl.ds(q * 256, 256)], recv_p.at[q])

    def project(t, carry):
        place = ds(t * 256, 256)

        @pl.when(t == half // 256)
        def _():
            for q in range(4):
                wait_for(xf.at[pl.ds(half, half), pl.ds(q * 256, 256)], recv_m.at[q])
        for j in range(2):
            lanes = slice(j * 3 * part, (j + 1) * 3 * part)
            value = jnp.dot(xf[place, :], wqf[:, lanes], preferred_element_type=F32)
            bias = parf[:, ds(r * 2 * part + j * part, part)].astype(F32)
            low = j * 3 * part
            qkv[place, low : low + part] = (value[:, :part] + bias[0:1]).astype(BF)
            qkv[place, low + part : low + 2 * part] = value[:, part : 2 * part].astype(BF)
            qkv[place, low + 2 * part : low + 3 * part] = (value[:, 2 * part :] + bias[1:2]).astype(BF)
        for k, i in ((0, 8), (2, 9)):
            @pl.when(t == k)
            def _():
                advance(i)
        return carry
    lax.fori_loop(0, length // 256, project, 0)
    pairs = (
        (xf, x_out), (wqf, wq_out), (wof, wo_out), (wuf, wu_out), (wdf, wd_out), (qkv, qkv_out), (ctx, ctx_out), (normed, normed_out),
        (hidden, hidden_out), (act, act_out), (slope, slope_out), (outh, out_half), (two, two_out), (mix, mix_out))
    stores = [pltpu.make_async_copy(near, out, store.at[i]) for i, (near, out) in enumerate(pairs)]
    for i in (0, 1, 5):
        stores[i].start()

    def to_mate(src, dst, i):
        return pltpu.make_async_remote_copy(
            src, dst, send_x.at[i], recv_x.at[i], device_id={"core": 1 - r}, device_id_type=MESH)

    top_half, low_half = pl.ds(0, half), pl.ds(half, half)
    swaps = [
        to_mate(wof, wom, 0), to_mate(ctx.at[low_half], ctxm, 1), to_mate(hidden.at[top_half], hidden.at[low_half], 2),
        to_mate(mate_out.at[pl.ds(0, 256)], mate_in.at[pl.ds(0, 256)], 3),
        to_mate(mate_out.at[pl.ds(256, 256)], mate_in.at[pl.ds(256, 256)], 4), to_mate(mix.at[top_half], mix.at[low_half], 5)]

    rows = 256

    def pair(i, carry):
        base = (i // 2) * 3 * part + lax.rem(i, 2) * 128
        tq[...] = qkv[:, ds(base, 128)]
        tk[...] = qkv[:, ds(base + part, 128)]
        tv[...] = qkv[:, ds(base + 2 * part, 128)]
        seg_k = segr[0:1, :]
        for h in range(2):
            lanes = slice(h * HEAD_DIM, (h + 1) * HEAD_DIM)
            k, v = tk[:, lanes], tv[:, lanes]
            for start in range(0, length, rows):
                q = tq[start : start + rows, lanes]
                s = lax.dot_general(q, k, CONTRACT_LAST, preferred_element_type=F32) * (scale * LOG2E)
                s = jnp.where(segc[start : start + rows, 0:1] == seg_k, s, -1e9 * LOG2E)
                top = jnp.max(s, axis=1, keepdims=True)
                e = jnp.exp2(s - top)
                total = jnp.sum(e, axis=1, keepdims=True)
                out = jnp.dot(e.astype(BF), v, preferred_element_type=F32) / total
                tc[start : start + rows, lanes] = out.astype(BF)
                log_total = top + jnp.log2(total)
                lse[i, h : h + 1, start : start + rows] = jnp.transpose(jnp.broadcast_to(log_total, (rows, 128)))[0:1, :]
            for place, step in ATTEND_STEPS:
                if place[1] == h:
                    @pl.when(i == place[0])
                    def _():
                        advance(step)
        ctx[:, ds(i * 128, 128)] = tc[...]

        @pl.when(i == 2)
        def _():
            finish_weight(1)
            swaps[0].start()
            stores[2].start()
        return carry
    lax.fori_loop(0, ctx.shape[1] // 128, pair, 0)

    swaps[1].start()
    stores[6].start()
    advance(15)
    c_step(*steps[13])
    rowsf = parf[...].astype(F32)
    rows_out[...] = rowsf
    swaps[0].wait_recv()
    swaps[1].wait_recv()

    def out_rows(t, carry):
        place = ds(t * 256, 256)
        value = jnp.dot(ctx[place, :], wof[...], preferred_element_type=F32) + jnp.dot(ctxm[place, :], wom[...], preferred_element_type=F32)
        value = xf[place, :].astype(F32) + value + rowsf[2:3]
        out, norm, inv = normalize(value, rowsf[3:4], rowsf[4:5])
        hidden_one[place, :] = out
        normed[place, :] = norm
        inverse[place, :] = inv
        hidden[place, :] = out.astype(BF)
        return carry
    lax.fori_loop(0, half // 256, out_rows, 0)
    swaps[2].start()
    stores[7].start()
    c_step(*steps[14])
    c_step(*steps[15])
    finish_weight(2)
    stores[3].start()
    n = act.shape[1] // 2
    bias = []
    for j in range(2):
        block = parf[:, ds(r * 2 * part + j * part, part)].astype(F32)
        bias.append(jnp.concatenate([block[8 + k : 9 + k] for k in range(4)], axis=1))

    def up_rows(t, carry):
        place = ds(t * 256, 256)

        @pl.when(t == half // 256)
        def _():
            swaps[2].wait_recv()
            stores[8].start()
        for j in range(2):
            lanes = slice(j * n, (j + 1) * n)
            value = jnp.dot(hidden[place, :], wuf[:, lanes], preferred_element_type=F32) + bias[j]
            gate = 0.5 * (1.0 + lax.erf(value * math.sqrt(0.5)))
            act[place, lanes] = (value * gate).astype(BF)
            slope[place, lanes] = (gate + value * (math.sqrt(0.5 / math.pi) * jnp.exp(-0.5 * value * value))).astype(BF)
        return carry
    lax.fori_loop(0, length // 256, up_rows, 0)
    stores[9].start()
    stores[10].start()
    finish_weight(3)
    stores[4].start()
    vec[...] = jnp.zeros(vec.shape, F32)

    def mate_rows(t, carry):
        mate_out[ds(t * 256, 256), :] = jnp.dot(act[ds(half + t * 256, 256), :], wdf[...], preferred_element_type=F32)
        for k in range(2):
            @pl.when(t == k)
            def _():
                swaps[3 + k].start()
        return carry
    lax.fori_loop(0, half // 256, mate_rows, 0)
    for q in range(4):
        wait_for(ogh.at[:, pl.ds(q * 256, 256)], recv_g.at[q])

    def last_rows(t, carry):
        place = ds(t * 256, 256)
        value = jnp.dot(act[place, :], wdf[...], preferred_element_type=F32)
        for k in range(2):
            @pl.when(t == k)
            def _():
                swaps[3 + k].wait_recv()
        value = hidden_one[place, :] + (value + mate_in[place, :]) + rowsf[5:6]
        out, norm, inv = normalize(value, rowsf[6:7], rowsf[7:8])
        outh[place, :] = out.astype(BF)
        dy = ogh[place, :].astype(F32)
        scaled = dy * rowsf[6:7]
        mean = jnp.mean(scaled, axis=1, keepdims=True)
        slant = jnp.mean(scaled * norm, axis=1, keepdims=True)
        grad = inv * (scaled - mean - norm * slant)
        two[place, :] = grad
        mix[place, :] = grad.astype(BF)
        vec[3:4, :] += jnp.sum(grad, axis=0, keepdims=True)
        vec[4:5, :] += jnp.sum(dy * norm, axis=0, keepdims=True)
        vec[5:6, :] += jnp.sum(dy, axis=0, keepdims=True)
        return carry
    lax.fori_loop(0, half // 256, last_rows, 0)
    swaps[5].start()
    stores[11].start()
    stores[12].start()
    for s in range(1, 4):
        par_copy(s).wait_send()
    seg_send.wait_send()
    swaps[5].wait_recv()
    stores[13].start()
    for copy in swaps:
        copy.wait_send()
    for q in range(4):
        mate_copy(q).wait_send()
    for which in range(2):
        for k in range(2):
            for h in range(2):
                token_copy(which, k, h, True)
    for w in range(4):
        for up in (0, 1):
            @pl.when(outer(up))
            def _():
                a_copy(w, up).wait_send()

        @pl.when(r != owner)
        def _():
            mate_part(w).wait_send()

        for j in range(2):
            @pl.when(2 * r + j != c)
            def _():
                for rr in range(2):
                    for up in (0, 1):
                        forward(w, j, rr, up, True)
                    for p in range(2):
                        b_copy(w, j, rr, p).wait_send()
                        c_copy(w, j, rr, p).wait_send()
    for copy in stores:
        copy.wait()


ATTEND_STEPS = (((0, 0), 10), ((0, 1), 11), ((1, 1), 12), ((2, 1), 13), ((3, 0), 14))


def gather(tok, og, par, seg, weights, scale):
    dma = pltpu.SemaphoreType.DMA
    vmem, anywhere = pl.BlockSpec(memory_space=pltpu.VMEM), pl.BlockSpec(memory_space=pl.ANY)
    half, width = tok.shape[0] // 4, tok.shape[1] * 4
    length, heads, units = 2 * half, weights[1].shape[0] * 2, weights[2].shape[1] * 2
    rows = (half, width)
    out = [((16, width), F32), ((heads // 128, 2, length), F32), ((length, 128), jnp.int32), ((8, length), jnp.int32), ((half, 1), F32), ((16, width), F32)]
    large = [((length, width), BF)] + [((w.shape[0] * 2, w.shape[1] * 2), BF) for w in weights]
    large += [((length, 3 * heads), BF), ((length, heads), BF), (rows, F32), ((length, width), BF), ((length, units), BF), ((length, units), BF)]
    large += [(rows, BF), (rows, F32), ((length, width), BF)]
    scratch = large + [((16, width), BF), (rows, BF), ((heads, width), BF), ((half, heads), BF)] + [(rows, F32)] * 3 + [((2,) + seg.shape, jnp.int32)]
    scratch += [((length, 128), BF)] * 4
    sems = [(4, 2), (4, 4), (4, 4)] + [(4, 4, 2)] * 4 + [(4,)] * 10 + [(1,), (2,), (6,), (6,), (14,)]
    return pl.pallas_call(
        partial(gather_kernel, scale=scale),
        out_shape=[jax.ShapeDtypeStruct(s, t) for s, t in out + large],
        in_specs=[vmem] * 8,
        out_specs=[vmem] * 6 + [anywhere] * 14,
        scratch_shapes=[pltpu.VMEM(s, t) for s, t in scratch] + [dma(s) for s in sems],
        compiler_params=pltpu.CompilerParams(collective_id=0, has_side_effects=True, vmem_limit_bytes=VMEM_LIMIT),
        name="gather",
    )(tok, og, par, seg, *weights)


def mid_kernel(
    inverse, gain, vec_in, out_half, act_far, cols_far, mix_far, slope_far, wd_far, two_far, normed_far, hidden_far, wu_far, wo_far,
    outp, gu_out, attn_out, do, one_grad, vec, gsum, early,
    act, attn, mix, slope, wd, two_grad, normed, hidden, wu, wo, gd, gu, up_low, ub, mate_out, mate_in, first, second, third,
    send1, recv1, send2, recv2, send3, recv3, send_y, recv_y, send_m, recv_m, load, store,
):
    d, r, c = lax.axis_index("dp"), lax.axis_index("core"), lax.axis_index("col")
    a, b = d // 2, lax.rem(d, 2)
    barrier = pltpu.get_barrier_semaphore()
    for s in range(4):
        for o in range(2):
            if s or o:
                target = {"core": lax.rem(r + o, 2), "col": lax.rem(c + s, 4)}
                pl.semaphore_signal(barrier, inc=1, device_id=target, device_id_type=MESH)
    x_peer, y_peer = lax.bitwise_xor(d, 1), lax.bitwise_xor(d, 2)
    for p in (x_peer, y_peer):
        pl.semaphore_signal(barrier, inc=1, device_id={"dp": p}, device_id_type=MESH)
    pl.semaphore_wait(barrier, 9)

    half, n = out_half.shape[0], gd.shape[1] // 2
    size, cut = gd.shape[0] // 4, n // 2

    def local(p, j, slab):
        return gd.at[ds(slab * size, size), pl.ds(j * n + p * cut, cut)]

    def slab_of(j, i, mine):
        if j == 0:
            return i * 2 + (b if mine else 1 - b)
        return (a if mine else 1 - a) * 2 + i

    def turn(j, kept):
        own = a if j == 0 else b
        return own if kept else 1 - own

    def copy1(p, j, kept):
        i = turn(j, kept)
        return pltpu.make_async_remote_copy(
            local(p, j, slab_of(j, i, False)), first.at[p, j, i], send1.at[p, j, i], recv1.at[p, j, i],
            device_id={"dp": x_peer if j == 0 else y_peer}, device_id_type=MESH)

    def copy2(p, j):
        return pltpu.make_async_remote_copy(
            first.at[p, j, turn(j, False)], second.at[p, j], send2.at[p, j], recv2.at[p, j],
            device_id={"dp": y_peer if j == 0 else x_peer}, device_id_type=MESH)

    def copy3(j, rr, wait):
        src, dst = first.at[0, j, turn(j, True)].at[pl.ds(rr * 128, 128), :], third.at[c]
        z = 2 * r + j
        me = jnp.logical_and(z == c, r == rr)
        remote = pltpu.make_async_remote_copy(
            src, dst, send3.at[j, rr], recv3.at[c], device_id={"core": rr, "col": z}, device_id_type=MESH)
        if not wait:
            @pl.when(me)
            def _():
                pltpu.make_async_copy(src, dst, recv3.at[c]).start()

        @pl.when(jnp.logical_not(me))
        def _():
            remote.wait_send() if wait else remote.start()

    def step2(p):
        for j in range(2):
            give = turn(j, False)
            wait_for(first.at[p, j, give], recv1.at[p, j, give])
            src, dst = local(p, j, slab_of(j, give, True)), first.at[p, j, give]

            def add_two(t, carry):
                rows = ds(t * 64, 64, 64)
                dst[rows, :] = (src[rows, :].astype(F32) + dst[rows, :].astype(F32)).astype(BF)
                return carry
            lax.fori_loop(0, size // 64, add_two, 0)
            copy2(p, j).start()

    def step3(p):
        for j in range(2):
            kept = turn(j, True)
            wait_for(first.at[p, j, kept], recv1.at[p, j, kept])
            wait_for(second.at[p, j], recv2.at[p, j])
            src, more = local(p, j, slab_of(j, kept, True)), first.at[p, j, kept]
            dst = gsum.at[j] if p else more

            def add_three(t, carry):
                rows = ds(t * 64, 64, 64)
                value = src[rows, :].astype(F32) + more[rows, :].astype(F32) + second[p, j, rows, :].astype(F32)
                dst[rows, :] = value.astype(BF)
                return carry
            lax.fori_loop(0, size // 64, add_three, 0)
            if p == 0:
                for rr in range(2):
                    copy3(j, rr, False)

    def token_copy(q, wait):
        rr, k = c // 2, lax.rem(c, 2)
        sref = out_half.at[:, pl.ds(q * 256, 256)]
        dref = outp.at[ds(k * 2 * half + r * half, half)]
        sem = recv_y.at[k * 2 + r]
        me = jnp.logical_and(rr == r, q == c)
        remote = pltpu.make_async_remote_copy(
            sref, dref, send_y.at[q], sem, device_id={"core": rr, "col": q}, device_id_type=MESH)
        if not wait:
            @pl.when(me)
            def _():
                pltpu.make_async_copy(sref, dref, sem).start()

        @pl.when(jnp.logical_not(me))
        def _():
            remote.wait_send() if wait else remote.start()

    for q in range(4):
        token_copy(q, False)
    far_near = (
        (cols_far, attn), (act_far, act), (mix_far, mix), (wd_far, wd), (slope_far, slope), (wu_far, wu), (two_far, two_grad),
        (normed_far, normed), (hidden_far, hidden), (wo_far, wo))
    loads = [pltpu.make_async_copy(far, near, load.at[i]) for i, (far, near) in enumerate(far_near)]
    for copy in loads:
        copy.start()
    vec[...] = vec_in[...]
    ub[...] = jnp.zeros(ub.shape, F32)
    loads[0].wait()
    loads[1].wait()

    def down_rows(t, carry):
        slab = lax.bitwise_xor(d, 3 - t)
        xt = jnp.transpose(attn[:, ds(slab * size, size)])
        for j in range(2):
            lanes = slice(j * n, (j + 1) * n)
            gd[ds(slab * size, size), lanes] = jnp.dot(xt, act[:, lanes], preferred_element_type=F32).astype(BF)
        for k, sends in ((0, ((0, False), (1, False))), (1, ((1, True),)), (2, ((0, True),))):
            @pl.when(t == k)
            def _():
                for j, kept in sends:
                    copy1(0, j, kept).start()
        return carry
    lax.fori_loop(0, 4, down_rows, 0)
    for copy in loads[2:5]:
        copy.wait()

    def up_rows(t, carry):
        place = ds(t * 256, 256)
        for j in range(2):
            lanes = slice(j * n, (j + 1) * n)
            value = lax.dot_general(mix[place, :], wd[lanes, :], CONTRACT_LAST, preferred_element_type=F32) * slope[place, lanes].astype(F32)
            up_low[place, lanes] = value.astype(BF)
            ub[0:1, lanes] += jnp.sum(value, axis=0, keepdims=True)

        @pl.when(t == 0)
        def _():
            step2(0)
            for kept in (False, True):
                for j in range(2):
                    copy1(1, j, kept).start()
        return carry
    lax.fori_loop(0, 2 * half // 256, up_rows, 0)

    loads[5].wait()

    def mate_rows(t, carry):
        mate_out[ds(t * 256, 256), :] = lax.dot_general(
            up_low[ds(half + t * 256, 256), :], wu[...], CONTRACT_LAST, preferred_element_type=F32)
        return carry
    lax.fori_loop(0, half // 256, mate_rows, 0)
    mate = pltpu.make_async_remote_copy(
        mate_out, mate_in, send_m.at[0], recv_m.at[0], device_id={"core": 1 - r}, device_id_type=MESH)
    mate.start()
    for copy in loads[6:]:
        copy.wait()

    step3(0)
    mate.wait_recv()
    width = mate_in.shape[1]
    vec[0:3, :] = jnp.zeros((3, width), F32)

    def own_rows(t, carry):
        place = ds(t * 256, 256)
        value = lax.dot_general(up_low[place, :], wu[...], CONTRACT_LAST, preferred_element_type=F32)
        value = value + mate_in[place, :] + two_grad[place, :]
        norm = normed[place, :]
        scaled = value * gain[3:4, :]
        mean = jnp.mean(scaled, axis=1, keepdims=True)
        slant = jnp.mean(scaled * norm, axis=1, keepdims=True)
        grad = inverse[place, :] * (scaled - mean - norm * slant)
        one_grad[place, :] = grad
        attn[place, :] = grad.astype(BF)
        vec[0:1, :] += jnp.sum(grad, axis=0, keepdims=True)
        vec[1:2, :] += jnp.sum(value * norm, axis=0, keepdims=True)
        vec[2:3, :] += jnp.sum(value, axis=0, keepdims=True)
        return carry
    lax.fori_loop(0, half // 256, own_rows, 0)
    step2(1)
    pair = pltpu.make_async_remote_copy(
        attn.at[pl.ds(0, half)], attn.at[pl.ds(half, half)], send_m.at[1], recv_m.at[1],
        device_id={"core": 1 - r}, device_id_type=MESH)
    pair.start()

    def weight_rows(t, carry):
        xt = jnp.transpose(hidden[:, ds(t * 256, 256)])
        for j in range(2):
            lanes = slice(j * n, (j + 1) * n)
            gu[ds(t * 256, 256), lanes] = jnp.dot(xt, up_low[:, lanes], preferred_element_type=F32).astype(BF)
        return carry
    lax.fori_loop(0, hidden.shape[1] // 256, weight_rows, 0)
    gu_store = pltpu.make_async_copy(gu, gu_out, store.at[0])
    gu_store.start()
    part = n // 4
    for k in range(4):
        for j in range(2):
            vec[8 + k : 9 + k, ds(r * 2 * part + j * part, part)] = ub[0:1, j * n + k * part : j * n + (k + 1) * part]
    pair.wait_recv()
    attn_store = pltpu.make_async_copy(attn, attn_out, store.at[1])
    attn_store.start()

    def ctx_rows(t, carry):
        place = ds(t * 256, 256)
        do[place, :] = lax.dot_general(attn[place, :], wo[...], CONTRACT_LAST, preferred_element_type=F32).astype(BF)
        return carry
    lax.fori_loop(0, 2 * half // 256, ctx_rows, 0)

    for z in range(4):
        wait_for(third.at[z], recv3.at[z])
    value = (third[0].astype(F32) + third[1].astype(F32)) + (third[2].astype(F32) + third[3].astype(F32))
    early[...] = jnp.transpose(value)
    step3(1)
    for j in range(2):
        for i in range(2):
            for p in range(2):
                copy1(p, j, i).wait_send()
            copy3(j, i, True)
        for p in range(2):
            copy2(p, j).wait_send()
    mate.wait_send()
    pair.wait_send()
    gu_store.wait()
    attn_store.wait()
    for q in range(4):
        token_copy(q, True)
        wait_for(outp.at[pl.ds(q * half, half)], recv_y.at[q])


def middle(out_half, act, cols, mix, slope, wd, two_grad, normed, inverse, gain, vec, hidden, wu, wo):
    dma = pltpu.SemaphoreType.DMA
    vmem, anywhere = pl.BlockSpec(memory_space=pltpu.VMEM), pl.BlockSpec(memory_space=pl.ANY)
    half, width = out_half.shape
    slab = (width // 4, act.shape[1] // 4)
    out = [((4 * half, width // 4), BF), (wu.shape, BF), (cols.shape, BF), ((2 * half, wo.shape[0]), BF), ((half, width), F32), (vec.shape, F32), ((2,) + slab, BF), ((slab[1], width // 8), F32)]
    scratch = [(v.shape, v.dtype) for v in (act, cols, mix, slope, wd, two_grad, normed, hidden, wu, wo)]
    scratch += [(wu.shape, BF), (wu.shape, BF), (slope.shape, BF)]
    scratch += [((8, slope.shape[1]), F32), ((half, width), F32), ((half, width), F32), ((2, 2, 2) + slab, BF), ((2, 2) + slab, BF), ((4, width // 8, slab[1]), BF)]
    sems = [(2, 2, 2), (2, 2, 2), (2, 2), (2, 2), (2, 2), (4,), (4,), (4,), (2,), (2,), (10,), (2,)]
    return pl.pallas_call(
        mid_kernel,
        out_shape=[jax.ShapeDtypeStruct(s, t) for s, t in out],
        in_specs=[vmem] * 3 + [anywhere] * 11,
        out_specs=[anywhere] * 3 + [vmem] * 5,
        scratch_shapes=[pltpu.VMEM(s, t) for s, t in scratch] + [dma(s) for s in sems],
        compiler_params=pltpu.CompilerParams(collective_id=2, has_side_effects=True, vmem_limit_bytes=VMEM_LIMIT),
        name="mid",
    )(inverse, gain, vec, out_half, act, cols, mix, slope, wd, two_grad, normed, hidden, wu, wo)


def back_kernel(
    lse, segk, segq, vec, early, qkv_far, do_far, ctx_far, gu_far, attn_far, x_far, wq_far, one_far, gsum,
    inp, total, rq, ro, ru, rd,
    qkv, do, ctx, gu, attn, x, wq, one_grad, go, inp_low, gq, low, tq, tk, tv, tg, vbuf, mate_out, mate_in, in_half,
    r1q, r1o, r1u, r1v, r2q, r2o, r2u, r2v, r3q, r3o, r3u, r3d, r3v, tall, v1, s4, v2,
    send1, recv1, send2, recv2, send3, recv3, send_i, recv_i, send_v, recv_v, send_w, recv_w, send_m, recv_m, load,
    *, scale,
):
    d, r, c = lax.axis_index("dp"), lax.axis_index("core"), lax.axis_index("col")
    a, b = d // 2, lax.rem(d, 2)
    barrier = pltpu.get_barrier_semaphore()
    for s in range(4):
        for o in range(2):
            if s or o:
                target = {"core": lax.rem(r + o, 2), "col": lax.rem(c + s, 4)}
                pl.semaphore_signal(barrier, inc=1, device_id=target, device_id_type=MESH)
    x_peer, y_peer = lax.bitwise_xor(d, 1), lax.bitwise_xor(d, 2)
    plane = [(p, o) for p in range(4) for o in range(2) if p or o]
    for p, o in plane:
        if p:
            target = {"dp": lax.bitwise_xor(d, p), "core": lax.rem(r + o, 2)}
            pl.semaphore_signal(barrier, inc=1, device_id=target, device_id_type=MESH)
    pl.semaphore_wait(barrier, 13)

    first, second = (r1q, r1o, r1u, None, r1v), (r2q, r2o, r2u, None, r2v)
    third = (r3q, r3o, r3u, r3d, r3v)
    by_rows = (True, False, True, True, True)
    half_up = gu.shape[1] // 4
    result = (rq, ro, ru.at[:, pl.ds(0, half_up)], rd, ru.at[:, pl.ds(half_up, half_up)])
    length, part3q = low.shape[0], low.shape[1] // 2
    part = part3q // 3

    def local(w, j, slab, far=False):
        if w == 0:
            return gq.at[j, slab]
        if w == 1:
            rows, cols = go.shape
            return go.at[pl.ds(j * (rows // 2), rows // 2), ds(slab * (cols // 4), cols // 4)]
        ref, start = gu_far if far else gu, 2 * j * half_up + (half_up if w == 4 else 0)
        return ref.at[ds(slab * (gu.shape[0] // 4), gu.shape[0] // 4), pl.ds(start, half_up)]

    def slab_of(j, i, mine):
        if j == 0:
            return i * 2 + (b if mine else 1 - b)
        return (a if mine else 1 - a) * 2 + i

    def turn(j, kept):
        own = a if j == 0 else b
        return own if kept else 1 - own

    def copy1(w, j, kept):
        i = turn(j, kept)
        return pltpu.make_async_remote_copy(
            local(w, j, slab_of(j, i, False), True), first[w].at[j, i], send1.at[w, j, i], recv1.at[w, j, i],
            device_id={"dp": x_peer if j == 0 else y_peer}, device_id_type=MESH)

    def copy2(w, j):
        return pltpu.make_async_remote_copy(
            first[w].at[j, turn(j, False)], second[w].at[j], send2.at[w, j], recv2.at[w, j],
            device_id={"dp": y_peer if j == 0 else x_peer}, device_id_type=MESH)

    def copy3(w, j, rr, wait):
        src = gsum.at[j] if w == 3 else first[w].at[j, turn(j, True)]
        src = src.at[pl.ds(rr * 128, 128), :] if by_rows[w] else src.at[:, pl.ds(rr * 128, 128)]
        dst = third[w].at[c]
        z = 2 * r + j
        me = jnp.logical_and(z == c, r == rr)
        remote = pltpu.make_async_remote_copy(
            src, dst, send3.at[w, j, rr], recv3.at[w, c], device_id={"core": rr, "col": z}, device_id_type=MESH)
        if not wait:
            @pl.when(me)
            def _():
                pltpu.make_async_copy(src, dst, recv3.at[w, c]).start()

        @pl.when(jnp.logical_not(me))
        def _():
            remote.wait_send() if wait else remote.start()

    def send_first(w, kept):
        for j in range(2):
            copy1(w, j, kept).start()

    def step2(w):
        for j in range(2):
            give = turn(j, False)
            wait_for(first[w].at[j, give], recv1.at[w, j, give])
            src, dst = local(w, j, slab_of(j, give, True)), first[w].at[j, give]

            def body(t, carry):
                rows = ds(t * 64, 64, 64)
                dst[rows, :] = (src[rows, :].astype(F32) + dst[rows, :].astype(F32)).astype(BF)
                return carry
            lax.fori_loop(0, dst.shape[0] // 64, body, 0)
            copy2(w, j).start()

    def step3(w):
        for j in range(2):
            kept = turn(j, True)
            wait_for(first[w].at[j, kept], recv1.at[w, j, kept])
            wait_for(second[w].at[j], recv2.at[w, j])
            src, dst, more = local(w, j, slab_of(j, kept, True)), first[w].at[j, kept], second[w].at[j]

            def body(t, carry):
                rows = ds(t * 64, 64, 64)
                dst[rows, :] = (src[rows, :].astype(F32) + dst[rows, :].astype(F32) + more[rows, :].astype(F32)).astype(BF)
                return carry
            lax.fori_loop(0, dst.shape[0] // 64, body, 0)
            for rr in range(2):
                copy3(w, j, rr, False)

    def finish(w):
        for z in range(4):
            wait_for(third[w].at[z], recv3.at[w, z])

        def body(t, carry):
            rows = ds(t * 64, 64, 64)
            value = (third[w][0, rows, :].astype(F32) + third[w][1, rows, :].astype(F32)) + (
                third[w][2, rows, :].astype(F32) + third[w][3, rows, :].astype(F32))
            if w == 3:
                tall[rows, :] = value
            else:
                result[w][rows, :] = value
            return carry
        lax.fori_loop(0, third[w].shape[1] // 64, body, 0)
        if w == 3:
            cut = tall.shape[1]
            rd[0:cut, :] = early[...]
            rd[cut:, :] = jnp.transpose(tall[...])

    half = in_half.shape[0]

    def token_copy(q, wait):
        rr, k = c // 2, lax.rem(c, 2)
        sref = in_half.at[:, pl.ds(q * 256, 256)]
        dref = inp_low.at[ds(k * 2 * half + r * half, half)]
        sem = recv_i.at[k * 2 + r]
        me = jnp.logical_and(rr == r, q == c)
        remote = pltpu.make_async_remote_copy(
            sref, dref, send_i.at[q], sem, device_id={"core": rr, "col": q}, device_id_type=MESH)
        if not wait:
            @pl.when(me)
            def _():
                pltpu.make_async_copy(sref, dref, sem).start()

        @pl.when(jnp.logical_not(me))
        def _():
            remote.wait_send() if wait else remote.start()

    def vec_z(s):
        z = lax.rem(c + s, 4)
        return pltpu.make_async_remote_copy(
            vbuf.at[:, ds(z * 256, 256)], v1.at[s], send_v.at[s], recv_v.at[s], device_id={"col": z}, device_id_type=MESH)

    def vec_plane(i):
        p, o = plane[i]
        return pltpu.make_async_remote_copy(
            s4, v2.at[i], send_w.at[i], recv_w.at[i],
            device_id={"dp": lax.bitwise_xor(d, p), "core": lax.rem(r + o, 2)}, device_id_type=MESH)

    mate = pltpu.make_async_remote_copy(
        mate_out, mate_in, send_m.at[0], recv_m.at[0], device_id={"core": 1 - r}, device_id_type=MESH)

    send_first(2, False)
    send_first(2, True)
    for j in range(2):
        for rr in range(2):
            copy3(3, j, rr, False)
    far_near = (
        (qkv_far, qkv), (do_far, do), (ctx_far, ctx), (gu_far, gu), (attn_far, attn), (x_far, x), (wq_far, wq), (one_far, one_grad))
    loads = [pltpu.make_async_copy(far, near, load.at[i]) for i, (far, near) in enumerate(far_near)]
    for copy in loads:
        copy.start()
    vbuf[...] = vec[...]
    for copy in loads[:3]:
        copy.wait()

    rows = 256

    def pair(i, carry):
        base = (i // 2) * part3q + lax.rem(i, 2) * 128
        tq[...] = qkv[:, ds(base, 128)]
        tg[...] = do[:, ds(i * 128, 128)]
        prod = jnp.transpose(tg[...].astype(F32) * ctx[:, ds(i * 128, 128)].astype(F32))
        tk[...] = qkv[:, ds(base + part, 128)]
        tv[...] = qkv[:, ds(base + 2 * part, 128)]
        seg_q = segq[0:1, :]
        for h in range(2):
            lanes = slice(h * HEAD_DIM, (h + 1) * HEAD_DIM)
            qh, doh = tq[:, lanes], tg[:, lanes]
            delta = jnp.sum(prod[h * HEAD_DIM : (h + 1) * HEAD_DIM], axis=0, keepdims=True)
            top = lse[i, h : h + 1, :]
            dqt = jnp.zeros((HEAD_DIM, length), F32)
            vsum = jnp.zeros((1, HEAD_DIM), F32)
            for start in range(0, length, rows):
                kh = tk[start : start + rows, lanes]
                vh = tv[start : start + rows, lanes]
                s = lax.dot_general(kh, qh, CONTRACT_LAST, preferred_element_type=F32) * (scale * LOG2E)
                s = jnp.where(segk[start : start + rows, 0:1] == seg_q, s, -1e9 * LOG2E)
                p = jnp.exp2(s - top)
                dp = lax.dot_general(vh, doh, CONTRACT_LAST, preferred_element_type=F32)
                g = (p * (dp - delta)).astype(BF)
                dk = jnp.dot(g, qh, preferred_element_type=F32) * scale
                tk[start : start + rows, lanes] = dk.astype(BF)
                dv = jnp.dot(p.astype(BF), doh, preferred_element_type=F32)
                tv[start : start + rows, lanes] = dv.astype(BF)
                vsum += jnp.sum(dv, axis=0, keepdims=True)
                dqt += jnp.dot(jnp.transpose(kh), g, preferred_element_type=F32)
            dq = jnp.transpose(dqt) * scale
            tq[:, lanes] = dq.astype(BF)
            v1[0, h : h + 1, 0:HEAD_DIM] = jnp.sum(dq, axis=0, keepdims=True)
            v1[0, h : h + 1, 128 : 128 + HEAD_DIM] = vsum
        low[:, ds(base, 128)] = tq[...]
        low[:, ds(base + part, 128)] = tk[...]
        low[:, ds(base + 2 * part, 128)] = tv[...]
        place = ds(r * 2 * part + i * 128, 128)
        vbuf[6:7, place] = jnp.concatenate([v1[0, 0:1, 0:HEAD_DIM], v1[0, 1:2, 0:HEAD_DIM]], axis=1)
        vbuf[7:8, place] = jnp.concatenate([v1[0, 0:1, 128 : 128 + HEAD_DIM], v1[0, 1:2, 128 : 128 + HEAD_DIM]], axis=1)

        @pl.when(i == 0)
        def _():
            for copy in loads[3:]:
                copy.wait()
            step2(2)
            send_first(4, False)
            send_first(4, True)

        @pl.when(i == 2)
        def _():
            step3(2)
            step2(4)
        return carry
    lax.fori_loop(0, do.shape[1] // 128, pair, 0)

    for s in range(1, 4):
        vec_z(s).start()

    def weight_rows(t, carry):
        xt = jnp.transpose(x[:, ds(t * 256, 256)])
        for j in range(2):
            gq[j, t] = jnp.dot(xt, low[:, j * part3q : (j + 1) * part3q], preferred_element_type=F32).astype(BF)
        return carry
    lax.fori_loop(0, 4, weight_rows, 0)
    send_first(0, False)
    send_first(0, True)

    def out_rows(t, carry):
        xt = jnp.transpose(ctx[:, ds(t * 256, 256)])
        go[ds(t * 256, 256), :] = jnp.dot(xt, attn[...], preferred_element_type=F32).astype(BF)
        return carry
    lax.fori_loop(0, ctx.shape[1] // 256, out_rows, 0)
    send_first(1, False)
    send_first(1, True)

    def mate_rows(t, carry):
        mate_out[ds(t * 256, 256), :] = lax.dot_general(
            low[ds(half + t * 256, 256), :], wq[...], CONTRACT_LAST, preferred_element_type=F32)
        return carry
    lax.fori_loop(0, half // 256, mate_rows, 0)
    mate.start()
    step3(4)
    for s in range(1, 4):
        vec_z(s).wait()
    s4[...] = (vbuf[:, ds(c * 256, 256)] + v1[1]) + (v1[2] + v1[3])
    for i in range(7):
        vec_plane(i).start()
    mate.wait_recv()

    def own_rows(t, carry):
        place = ds(t * 256, 256)
        value = lax.dot_general(low[place, :], wq[...], CONTRACT_LAST, preferred_element_type=F32)
        in_half[place, :] = (value + mate_in[place, :] + one_grad[place, :]).astype(BF)
        return carry
    lax.fori_loop(0, half // 256, own_rows, 0)
    for q in range(4):
        token_copy(q, False)
    step2(0)
    step2(1)
    step3(1)
    finish(3)
    for i in range(7):
        vec_plane(i).wait()
    total[...] = ((s4[...] + v2[0]) + (v2[1] + v2[2])) + ((v2[3] + v2[4]) + (v2[5] + v2[6]))
    finish(2)
    finish(4)
    for q in range(4):
        place = pl.ds(q * half, half)
        wait_for(inp_low.at[place], recv_i.at[q])
        inp[place, :] = inp_low[place, :].astype(F32)
    step3(0)
    finish(1)
    finish(0)
    for w in range(5):
        for j in range(2):
            for i in range(2):
                if w != 3:
                    copy1(w, j, i).wait_send()
                copy3(w, j, i, True)
            if w != 3:
                copy2(w, j).wait_send()
    mate.wait_send()
    for q in range(4):
        token_copy(q, True)


def back(x, wq, qkv, do, ctx, lse, segk, segq, one_grad, vec, grads, scale):
    dma = pltpu.SemaphoreType.DMA
    vmem, anywhere = pl.BlockSpec(memory_space=pltpu.VMEM), pl.BlockSpec(memory_space=pl.ANY)
    half, width = one_grad.shape
    far = (qkv, do, ctx, grads[1], grads[0], x, wq, one_grad)
    length, part = 2 * half, width // 4
    rows_q, heads, units = wq.shape[1] // 2, do.shape[1], grads[1].shape[1] // 2
    slab, own, cut = width // 4, width // 8, units // 2
    out = [((4 * half, part), F32), ((vec.shape[0], part), F32), ((own, rows_q), F32), ((heads // 2, own), F32), ((own, units), F32), ((units, own), F32)]
    slabs = [(slab, rows_q), (heads // 2, slab), (slab, cut), (slab, cut)]
    r1, r2 = [(2, 2) + v for v in slabs], [(2,) + v for v in slabs]
    r3 = [(4, own, rows_q), (4, heads // 2, own), (4, own, cut), (4, own, cut), (4, own, cut)]
    scratch = [(v.shape, v.dtype) for v in far] + [((heads, width), BF), ((4 * half, part), BF), ((2, 4, width // 4, wq.shape[1] // 2), BF), (qkv.shape, BF)] + [((length, 128), BF)] * 4
    scratch += [(vec.shape, F32), ((half, width), F32), ((half, width), F32), ((half, width), BF)]
    scratch += [(s, BF) for s in r1 + r2 + r3] + [(r3[3][1:], F32)]
    scratch += [((4, vec.shape[0], part), F32), ((vec.shape[0], part), F32), ((7, vec.shape[0], part), F32)]
    sems = [(5, 2, 2), (5, 2, 2), (5, 2), (5, 2), (5, 2, 2), (5, 4), (4,), (4,), (4,), (4,), (7,), (7,), (1,), (1,), (8,)]
    return pl.pallas_call(
        partial(back_kernel, scale=scale),
        out_shape=[jax.ShapeDtypeStruct(s, t) for s, t in out],
        in_specs=[vmem] * 5 + [anywhere] * 9,
        out_specs=[vmem] * 6,
        scratch_shapes=[pltpu.VMEM(s, t) for s, t in scratch] + [dma(s) for s in sems],
        compiler_params=pltpu.CompilerParams(collective_id=1, has_side_effects=True, vmem_limit_bytes=VMEM_LIMIT),
        name="back",
    )(lse, segk, segq, vec, grads[3], *far, grads[2])


def part_rows(values, groups):
    if groups == 1:
        return values
    rows, cols = values.shape
    return values.reshape(4, groups, 2, rows // (8 * groups), cols).transpose(0, 2, 1, 3, 4).reshape(rows, cols)


def on_device(
    tokens, segment_ids, w_qkv, b_qv, w_out, b_out, norm1_gain, norm1_shift,
    w_up, b_up, w_down, b_down, norm2_gain, norm2_shift, out_grad,
):
    groups = lax.axis_size("rh")
    core, col = lax.axis_index("core"), lax.axis_index("col")
    part = tokens.shape[1]
    scale = 1.0 / math.sqrt(HEAD_DIM)
    wq, wo, wu, wd = w_qkv.reshape(w_qkv.shape[0], 3 * part), w_out, w_up, w_down
    if groups > 1:
        both_rows = ("rh", "core")
        wq, wu = (lax.all_gather(w, both_rows, axis=0, tiled=True) for w in (wq, wu))
        wo, wd = (lax.all_gather(w, both_rows, axis=1, tiled=True) for w in (wo, wd))
        wq, wu = (lax.dynamic_slice_in_dim(w, core * (w.shape[0] // 2), w.shape[0] // 2, 0) for w in (wq, wu))
        wo, wd = (lax.dynamic_slice_in_dim(w, core * (w.shape[1] // 2), w.shape[1] // 2, 1) for w in (wo, wd))
    vectors = [b_qv[0], b_qv[1], b_out, norm1_gain, norm1_shift, b_down, norm2_gain, norm2_shift] + [b_up[k * part : (k + 1) * part] for k in range(4)]
    index = lax.broadcasted_iota(jnp.int32, (16, part), 0)
    par = jnp.zeros((16, part), BF)
    for k, vector in enumerate(vectors):
        par = jnp.where(index == k, vector[None], par)
    (params, lse, seg_col, seg_row, inverse_one, vec, x, wq, wo, wu, wd, qkv, ctx, normed_one, hidden, activated, slope, output, two_grad,
     mix) = gather(tokens, out_grad, par, segment_ids, (wq, wo, wu, wd), scale)
    x_cols, hidden_cols, mix_cols = x, hidden, mix
    if groups > 1:
        x_cols, hidden_cols, mix_cols = (part_rows(v.T, groups).T for v in (x, hidden, mix))
    output, up_wgrad, attn, ctx_grad, one_grad, vec, down_sum, down_early = middle(
        output, activated, mix_cols, mix, slope, wd, two_grad, normed_one, inverse_one, params, vec, hidden_cols, wu, wo)
    if groups > 1:
        attn = part_rows(attn.T, groups).T
    in_grad, sums, qkv_share, out_share, up_share, down_share = back(
        x_cols, wq, qkv, ctx_grad, ctx, lse, seg_col, seg_row, one_grad, vec, (attn, up_wgrad, down_sum, down_early), scale)
    if groups > 1:
        sums = lax.psum(sums, "rh")
        qkv_share, up_share = (lax.psum_scatter(g, "rh", scatter_dimension=0, tiled=True) for g in (qkv_share, up_share))
        out_share, down_share = (lax.psum_scatter(g, "rh", scatter_dimension=1, tiled=True) for g in (out_share, down_share))
    return (
        output,
        in_grad,
        qkv_share.reshape(qkv_share.shape[0], 3, part),
        sums[6:8],
        out_share,
        sums[0],
        sums[1],
        sums[2],
        up_share,
        sums[8:12].reshape(-1),
        down_share,
        sums[3],
        sums[4],
        sums[5],
    )


def solution(mesh):
    dp, row, col = (mesh.shape[name] for name in ("dp", "row", "col"))
    fine = Mesh(mesh.devices.reshape(dp, row // 2, 2, col), ("dp", "rh", "core", "col"))
    row, every = ("rh", "core"), ("dp", "rh", "core")
    return jax.shard_map(
        on_device,
        mesh=fine,
        in_specs=(
            P(every, "col"), P(every, None), P(row, None, "col"), P(None, "col"), P("col", row), P("col"), P("col"), P("col"),
            P(row, "col"), P("col"), P("col", row), P("col"), P("col"), P("col"), P(every, "col"),
        ),
        out_specs=(
            P(every, "col"), P(every, "col"), P(every, None, "col"), P(None, "col"), P("col", every), P("col"), P("col"),
            P("col"), P(every, "col"), P("col"), P("col", every), P("col"), P("col"), P("col"),
        ),
        check_vma=False,
    )
```

```python
from functools import partial
import math

import jax
import jax.numpy as jnp
from jax import lax
from jax.experimental import pallas as pl
from jax.experimental.pallas import tpu as pltpu
from jax.sharding import Mesh, PartitionSpec as P

HEAD_DIM = 64
NORM_EPSILON = 1e-05
MESH = pl.DeviceIdType.MESH
LOG2E = math.log2(math.e)
BF = jnp.bfloat16
F32 = jnp.float32
CONTRACT_LAST = (((1,), (1,)), ((), ()))
CONTRACT_FIRST = (((0,), (0,)), ((), ()))
VMEM_LIMIT = 62 * 2**20


def wait_for(ref, sem):
    pltpu.make_async_copy(ref, ref, sem).wait()


def ds(start, size, multiple=128):
    return pl.ds(pl.multiple_of(start, multiple), size)


def normalize(residual, gain, shift):
    mean = jnp.mean(residual, axis=1, keepdims=True)
    centered = residual - mean
    inverse = lax.rsqrt(jnp.mean(centered * centered, axis=1, keepdims=True) + NORM_EPSILON)
    normed = centered * inverse
    return normed * gain + shift, normed, inverse


def gather_kernel(
    tok, og, par, seg, wq, wo, wu, wd,
    rows_out, lse, segc, segr, inverse, vec,
    x_out, wq_out, wo_out, wu_out, wd_out, qkv_out, ctx_out, normed_out, hidden_out, act_out, slope_out, out_half, two_out, mix_out,
    xf, wqf, wof, wuf, wdf, qkv, ctx, normed, hidden, act, slope, outh, two, mix,
    parf, ogh, wom, ctxm, hidden_one, mate_out, mate_in, segs, tq, tk, tv, tc,
    send_a, recv_a, send_f, send_b, recv_b, send_c, recv_c, recv_l, send_l, send_t, recv_t, send_g, recv_g, send_m, recv_m, send_p, recv_p,
    send_s, recv_s, send_x, recv_x, store,
    *, scale,
):
    d, r, c = lax.axis_index("dp"), lax.axis_index("core"), lax.axis_index("col")
    owner, j0 = c // 2, lax.rem(c, 2)
    half = tok.shape[0] // 4
    barrier = pltpu.get_barrier_semaphore()
    for s in range(4):
        for o in range(2):
            if s or o:
                target = {"core": lax.rem(r + o, 2), "col": lax.rem(c + s, 4)}
                pl.semaphore_signal(barrier, inc=1, device_id=target, device_id_type=MESH)
    x_peer, y_peer, far = (lax.bitwise_xor(d, p) for p in (1, 2, 3))
    peers = (x_peer, y_peer)
    for p in peers:
        pl.semaphore_signal(barrier, inc=1, device_id={"dp": p}, device_id_type=MESH)
    pl.semaphore_wait(barrier, 9)

    source, dest = (wq, wo, wu, wd), (wqf, wof, wuf, wdf)

    def whole(w, rr, j):
        rows, cols = source[w].shape
        if w in (0, 2):
            return dest[w].at[ds(rr * rows, rows), ds(j * cols, cols)]
        return dest[w].at[ds(j * rows, rows), ds(rr * cols, cols)]

    def piece(w, rr, dd, j, part=None):
        rows, cols = source[w].shape
        size = rows // 4
        base = (rr if w in (0, 2) else j) * rows + dd * size
        if part is not None:
            size = size // 2
            base = base + part * size
        return dest[w].at[ds(base, size, 32), ds((j if w in (0, 2) else rr) * cols, cols)]

    def a_copy(w, up):
        size = source[w].shape[0] // 4
        return pltpu.make_async_remote_copy(
            source[w].at[ds(d * size, size, 64)], piece(w, r, d, j0), send_a.at[w, up], recv_a.at[w, j0 * 2 + r],
            device_id={"core": owner, "col": lax.rem(c + (1 if up else 3), 4)}, device_id_type=MESH)

    def outer(up):
        return c < 3 if up else c > 0

    def mate_part(w):
        return pltpu.make_async_remote_copy(
            source[w], whole(w, r, j0), send_l.at[w], recv_l.at[w], device_id={"core": 1 - r}, device_id_type=MESH)

    def start_a(w):
        for up in (0, 1):
            @pl.when(outer(up))
            def _():
                a_copy(w, up).start()

        @pl.when(r == owner)
        def _():
            pltpu.make_async_copy(source[w], whole(w, r, j0), send_l.at[w]).start()

        @pl.when(r != owner)
        def _():
            mate_part(w).start()

    def token_copy(which, k, h, wait):
        src, dst = ((tok, xf), (og, ogh))[which]
        ssem = (send_t, send_g)[which].at[k * 2 + h]
        rsem = (recv_t, recv_g)[which].at[c]
        sref = src.at[pl.ds(k * 2 * half + h * half, half)]
        dref = dst.at[pl.ds(0, half), ds(c * 256, 256)]
        z = 2 * r + k
        me = jnp.logical_and(z == c, r == h)
        remote = pltpu.make_async_remote_copy(
            sref, dref, ssem, rsem, device_id={"core": h, "col": z}, device_id_type=MESH)
        if not wait:
            @pl.when(me)
            def _():
                pltpu.make_async_copy(sref, dref, rsem).start()

        @pl.when(jnp.logical_not(me))
        def _():
            remote.wait_send() if wait else remote.start()

    def mate_copy(q):
        src = xf.at[pl.ds(0, half), pl.ds(q * 256, 256)]
        dst = xf.at[pl.ds(half, half), pl.ds(q * 256, 256)]
        return pltpu.make_async_remote_copy(
            src, dst, send_m.at[q], recv_m.at[q], device_id={"core": 1 - r}, device_id_type=MESH)

    def par_copy(s):
        return pltpu.make_async_remote_copy(
            par, parf.at[:, ds(c * 256, 256)], send_p.at[s], recv_p.at[c],
            device_id={"col": lax.rem(c + s, 4)}, device_id_type=MESH)

    def forward(w, j, rr, up, wait):
        origin = 2 * r + j
        ref = piece(w, rr, d, j)
        copy = pltpu.make_async_remote_copy(
            ref, ref, send_f.at[w, j * 2 + rr], recv_a.at[w, j * 2 + rr],
            device_id={"col": lax.rem(c + (1 if up else 3), 4)}, device_id_type=MESH)

        @pl.when(jnp.logical_and(origin < c if up else origin > c, outer(up)))
        def _():
            copy.wait_send() if wait else copy.start()

    def b_copy(w, j, rr, p):
        ref = piece(w, rr, d, j)
        return pltpu.make_async_remote_copy(
            ref, ref, send_b.at[w, j * 2 + rr, p], recv_b.at[w, j * 2 + rr, p],
            device_id={"dp": peers[p]}, device_id_type=MESH)

    def c_copy(w, j, rr, p):
        ref = piece(w, rr, peers[p], j, p)
        return pltpu.make_async_remote_copy(
            ref, ref, send_c.at[w, j * 2 + rr, p], recv_c.at[w, j * 2 + rr, p],
            device_id={"dp": peers[1 - p]}, device_id_type=MESH)

    def b_step(w, near, rr):
        j = 1 - r if near else r

        @pl.when(2 * r + j != c)
        def _():
            wait_for(piece(w, rr, d, j), recv_a.at[w, j * 2 + rr])
            for up in (0, 1):
                forward(w, j, rr, up, False)
            for p in range(2):
                b_copy(w, j, rr, p).start()

    def c_step(w, near, rr):
        j = 1 - r if near else r

        @pl.when(2 * r + j != c)
        def _():
            for p in range(2):
                wait_for(piece(w, rr, peers[p], j), recv_b.at[w, j * 2 + rr, p])
                c_copy(w, j, rr, p).start()

    def finish_weight(w):
        @pl.when(r == owner)
        def _():
            wait_for(whole(w, r, j0), send_l.at[w])
            wait_for(whole(w, 1 - r, j0), recv_l.at[w])

        for j in range(2):
            @pl.when(2 * r + j != c)
            def _():
                for rr in range(2):
                    for p in range(2):
                        wait_for(piece(w, rr, far, j, p), recv_c.at[w, j * 2 + rr, p])

    seg_send = pltpu.make_async_remote_copy(
        seg, segs.at[r], send_s.at[0], recv_s.at[r], device_id={"core": 1 - r}, device_id_type=MESH)
    seg_own = pltpu.make_async_copy(seg, segs.at[r], recv_s.at[r])
    start_a(0)
    for s in range(1, 4):
        par_copy(s).start()
    pltpu.make_async_copy(par, parf.at[:, ds(c * 256, 256)], recv_p.at[c]).start()
    seg_send.start()
    seg_own.start()
    steps = [(w, near, rr) for w in range(4) for near in (1, 0) for rr in range(2)]

    def tokens_out(which):
        for k in range(2):
            for h in range(2):
                token_copy(which, k, h, False)

    def advance(i):
        b_step(*steps[i])
        if i >= 3:
            c_step(*steps[i - 3])
        if i == 1:
            start_a(1)
        if i == 3:
            tokens_out(0)
            start_a(2)
        if i == 7:
            start_a(3)
        if i == 15:
            tokens_out(1)

    for i in range(8):
        advance(i)
    for q in range(4):
        wait_for(xf.at[pl.ds(0, half), pl.ds(q * 256, 256)], recv_t.at[q])
        mate_copy(q).start()
    for rr in range(2):
        wait_for(segs.at[rr], recv_s.at[rr])
    length, part = xf.shape[0], wqf.shape[1] // 6
    segr[:, 0:half] = jnp.broadcast_to(segs[owner, pl.ds(j0, 1), ds(r * half, half)], (8, half))
    segr[:, half:] = jnp.broadcast_to(segs[owner, pl.ds(j0, 1), ds((1 - r) * half, half)], (8, half))
    segc[...] = jnp.transpose(jnp.broadcast_to(segr[0:1, :], (128, length)))
    finish_weight(0)
    for q in range(4):
        wait_for(parf.at[:, pl.ds(q * 256, 256)], recv_p.at[q])

    def project(t, carry):
        place = ds(t * 256, 256)

        @pl.when(t == half // 256)
        def _():
            for q in range(4):
                wait_for(xf.at[pl.ds(half, half), pl.ds(q * 256, 256)], recv_m.at[q])
        for j in range(2):
            lanes = slice(j * 3 * part, (j + 1) * 3 * part)
            value = jnp.dot(xf[place, :], wqf[:, lanes], preferred_element_type=F32)
            bias = parf[:, ds(r * 2 * part + j * part, part)].astype(F32)
            low = j * 3 * part
            qkv[place, low : low + part] = (value[:, :part] + bias[0:1]).astype(BF)
            qkv[place, low + part : low + 2 * part] = value[:, part : 2 * part].astype(BF)
            qkv[place, low + 2 * part : low + 3 * part] = (value[:, 2 * part :] + bias[1:2]).astype(BF)
        for k, i in ((0, 8), (2, 9)):
            @pl.when(t == k)
            def _():
                advance(i)
        return carry
    lax.fori_loop(0, length // 256, project, 0)
    pairs = (
        (xf, x_out), (wqf, wq_out), (wof, wo_out), (wuf, wu_out), (wdf, wd_out), (qkv, qkv_out), (ctx, ctx_out), (normed, normed_out),
        (hidden, hidden_out), (act, act_out), (slope, slope_out), (outh, out_half), (two, two_out), (mix, mix_out))
    stores = [pltpu.make_async_copy(near, out, store.at[i]) for i, (near, out) in enumerate(pairs)]
    for i in (0, 1, 5):
        stores[i].start()

    def to_mate(src, dst, i):
        return pltpu.make_async_remote_copy(
            src, dst, send_x.at[i], recv_x.at[i], device_id={"core": 1 - r}, device_id_type=MESH)

    top_half, low_half = pl.ds(0, half), pl.ds(half, half)
    swaps = [
        to_mate(wof, wom, 0), to_mate(ctx.at[low_half], ctxm, 1), to_mate(hidden.at[top_half], hidden.at[low_half], 2),
        to_mate(mate_out.at[pl.ds(0, 256)], mate_in.at[pl.ds(0, 256)], 3),
        to_mate(mate_out.at[pl.ds(256, 256)], mate_in.at[pl.ds(256, 256)], 4), to_mate(mix.at[top_half], mix.at[low_half], 5)]

    rows = 256

    def pair(i, carry):
        base = (i // 2) * 3 * part + lax.rem(i, 2) * 128
        tq[...] = qkv[:, ds(base, 128)]
        tk[...] = qkv[:, ds(base + part, 128)]
        tv[...] = qkv[:, ds(base + 2 * part, 128)]
        seg_k = segr[0:1, :]
        for h in range(2):
            lanes = slice(h * HEAD_DIM, (h + 1) * HEAD_DIM)
            k, v = tk[:, lanes], tv[:, lanes]
            for start in range(0, length, rows):
                q = tq[start : start + rows, lanes]
                s = lax.dot_general(q, k, CONTRACT_LAST, preferred_element_type=F32) * (scale * LOG2E)
                s = jnp.where(segc[start : start + rows, 0:1] == seg_k, s, -1e9 * LOG2E)
                top = jnp.max(s, axis=1, keepdims=True)
                e = jnp.exp2(s - top)
                total = jnp.sum(e, axis=1, keepdims=True)
                out = jnp.dot(e.astype(BF), v, preferred_element_type=F32) / total
                tc[start : start + rows, lanes] = out.astype(BF)
                log_total = top + jnp.log2(total)
                lse[i, h : h + 1, start : start + rows] = jnp.transpose(jnp.broadcast_to(log_total, (rows, 128)))[0:1, :]
            for place, step in ATTEND_STEPS:
                if place[1] == h:
                    @pl.when(i == place[0])
                    def _():
                        advance(step)
        ctx[:, ds(i * 128, 128)] = tc[...]

        @pl.when(i == 2)
        def _():
            finish_weight(1)
            swaps[0].start()
            stores[2].start()
        return carry
    lax.fori_loop(0, ctx.shape[1] // 128, pair, 0)

    swaps[1].start()
    stores[6].start()
    advance(15)
    c_step(*steps[13])
    rowsf = parf[...].astype(F32)
    rows_out[...] = rowsf
    swaps[0].wait_recv()
    swaps[1].wait_recv()

    def out_rows(t, carry):
        place = ds(t * 256, 256)
        value = jnp.dot(ctx[place, :], wof[...], preferred_element_type=F32) + jnp.dot(ctxm[place, :], wom[...], preferred_element_type=F32)
        value = xf[place, :].astype(F32) + value + rowsf[2:3]
        out, norm, inv = normalize(value, rowsf[3:4], rowsf[4:5])
        hidden_one[place, :] = out
        normed[place, :] = norm
        inverse[place, :] = inv
        hidden[place, :] = out.astype(BF)
        return carry
    lax.fori_loop(0, half // 256, out_rows, 0)
    swaps[2].start()
    stores[7].start()
    c_step(*steps[14])
    c_step(*steps[15])
    finish_weight(2)
    stores[3].start()
    n = act.shape[1] // 2
    bias = []
    for j in range(2):
        block = parf[:, ds(r * 2 * part + j * part, part)].astype(F32)
        bias.append(jnp.concatenate([block[8 + k : 9 + k] for k in range(4)], axis=1))

    def up_rows(t, carry):
        place = ds(t * 256, 256)

        @pl.when(t == half // 256)
        def _():
            swaps[2].wait_recv()
            stores[8].start()
        for j in range(2):
            lanes = slice(j * n, (j + 1) * n)
            value = jnp.dot(hidden[place, :], wuf[:, lanes], preferred_element_type=F32) + bias[j]
            gate = 0.5 * (1.0 + lax.erf(value * math.sqrt(0.5)))
            act[place, lanes] = (value * gate).astype(BF)
            slope[place, lanes] = (gate + value * (math.sqrt(0.5 / math.pi) * jnp.exp(-0.5 * value * value))).astype(BF)
        return carry
    lax.fori_loop(0, length // 256, up_rows, 0)
    stores[9].start()
    stores[10].start()
    finish_weight(3)
    stores[4].start()
    vec[...] = jnp.zeros(vec.shape, F32)

    def mate_rows(t, carry):
        mate_out[ds(t * 256, 256), :] = jnp.dot(act[ds(half + t * 256, 256), :], wdf[...], preferred_element_type=F32)
        for k in range(2):
            @pl.when(t == k)
            def _():
                swaps[3 + k].start()
        return carry
    lax.fori_loop(0, half // 256, mate_rows, 0)
    for q in range(4):
        wait_for(ogh.at[:, pl.ds(q * 256, 256)], recv_g.at[q])

    def last_rows(t, carry):
        place = ds(t * 256, 256)
        value = jnp.dot(act[place, :], wdf[...], preferred_element_type=F32)
        for k in range(2):
            @pl.when(t == k)
            def _():
                swaps[3 + k].wait_recv()
        value = hidden_one[place, :] + (value + mate_in[place, :]) + rowsf[5:6]
        out, norm, inv = normalize(value, rowsf[6:7], rowsf[7:8])
        outh[place, :] = out.astype(BF)
        dy = ogh[place, :].astype(F32)
        scaled = dy * rowsf[6:7]
        mean = jnp.mean(scaled, axis=1, keepdims=True)
        slant = jnp.mean(scaled * norm, axis=1, keepdims=True)
        grad = inv * (scaled - mean - norm * slant)
        two[place, :] = grad
        mix[place, :] = grad.astype(BF)
        vec[3:4, :] += jnp.sum(grad, axis=0, keepdims=True)
        vec[4:5, :] += jnp.sum(dy * norm, axis=0, keepdims=True)
        vec[5:6, :] += jnp.sum(dy, axis=0, keepdims=True)
        return carry
    lax.fori_loop(0, half // 256, last_rows, 0)
    swaps[5].start()
    stores[11].start()
    stores[12].start()
    for s in range(1, 4):
        par_copy(s).wait_send()
    seg_send.wait_send()
    swaps[5].wait_recv()
    stores[13].start()
    for copy in swaps:
        copy.wait_send()
    for q in range(4):
        mate_copy(q).wait_send()
    for which in range(2):
        for k in range(2):
            for h in range(2):
                token_copy(which, k, h, True)
    for w in range(4):
        for up in (0, 1):
            @pl.when(outer(up))
            def _():
                a_copy(w, up).wait_send()

        @pl.when(r != owner)
        def _():
            mate_part(w).wait_send()

        for j in range(2):
            @pl.when(2 * r + j != c)
            def _():
                for rr in range(2):
                    for up in (0, 1):
                        forward(w, j, rr, up, True)
                    for p in range(2):
                        b_copy(w, j, rr, p).wait_send()
                        c_copy(w, j, rr, p).wait_send()
    for copy in stores:
        copy.wait()


ATTEND_STEPS = (((0, 0), 10), ((0, 1), 11), ((1, 1), 12), ((2, 1), 13), ((3, 0), 14))


def gather(tok, og, par, seg, weights, scale):
    dma = pltpu.SemaphoreType.DMA
    vmem, anywhere = pl.BlockSpec(memory_space=pltpu.VMEM), pl.BlockSpec(memory_space=pl.ANY)
    half, width = tok.shape[0] // 4, tok.shape[1] * 4
    length, heads, units = 2 * half, weights[1].shape[0] * 2, weights[2].shape[1] * 2
    rows = (half, width)
    out = [((16, width), F32), ((heads // 128, 2, length), F32), ((length, 128), jnp.int32), ((8, length), jnp.int32), ((half, 1), F32), ((16, width), F32)]
    large = [((length, width), BF)] + [((w.shape[0] * 2, w.shape[1] * 2), BF) for w in weights]
    large += [((length, 3 * heads), BF), ((length, heads), BF), (rows, F32), ((length, width), BF), ((length, units), BF), ((length, units), BF)]
    large += [(rows, BF), (rows, F32), ((length, width), BF)]
    scratch = large + [((16, width), BF), (rows, BF), ((heads, width), BF), ((half, heads), BF)] + [(rows, F32)] * 3 + [((2,) + seg.shape, jnp.int32)]
    scratch += [((length, 128), BF)] * 4
    sems = [(4, 2), (4, 4), (4, 4)] + [(4, 4, 2)] * 4 + [(4,)] * 10 + [(1,), (2,), (6,), (6,), (14,)]
    return pl.pallas_call(
        partial(gather_kernel, scale=scale),
        out_shape=[jax.ShapeDtypeStruct(s, t) for s, t in out + large],
        in_specs=[vmem] * 8,
        out_specs=[vmem] * 6 + [anywhere] * 14,
        scratch_shapes=[pltpu.VMEM(s, t) for s, t in scratch] + [dma(s) for s in sems],
        compiler_params=pltpu.CompilerParams(collective_id=0, has_side_effects=True, vmem_limit_bytes=VMEM_LIMIT),
        name="gather",
    )(tok, og, par, seg, *weights)


def mid_kernel(
    inverse, gain, vec_in, out_half, act_far, cols_far, mix_far, slope_far, wd_far, two_far, normed_far, hidden_far, wu_far, wo_far,
    outp, gu_out, attn_out, do, one_grad, vec, gsum, early,
    act, attn, mix, slope, wd, two_grad, normed, hidden, wu, wo, gd, gu, up_low, ub, mate_out, mate_in, first, second, third,
    send1, recv1, send2, recv2, send3, recv3, send_y, recv_y, send_m, recv_m, load, store,
):
    d, r, c = lax.axis_index("dp"), lax.axis_index("core"), lax.axis_index("col")
    a, b = d // 2, lax.rem(d, 2)
    barrier = pltpu.get_barrier_semaphore()
    for s in range(4):
        for o in range(2):
            if s or o:
                target = {"core": lax.rem(r + o, 2), "col": lax.rem(c + s, 4)}
                pl.semaphore_signal(barrier, inc=1, device_id=target, device_id_type=MESH)
    x_peer, y_peer = lax.bitwise_xor(d, 1), lax.bitwise_xor(d, 2)
    for p in (x_peer, y_peer):
        pl.semaphore_signal(barrier, inc=1, device_id={"dp": p}, device_id_type=MESH)
    pl.semaphore_wait(barrier, 9)

    half, n = out_half.shape[0], gd.shape[1] // 2
    size, cut = gd.shape[0] // 4, n // 2

    def local(p, j, slab):
        return gd.at[ds(slab * size, size), pl.ds(j * n + p * cut, cut)]

    def slab_of(j, i, mine):
        if j == 0:
            return i * 2 + (b if mine else 1 - b)
        return (a if mine else 1 - a) * 2 + i

    def turn(j, kept):
        own = a if j == 0 else b
        return own if kept else 1 - own

    def copy1(p, j, kept):
        i = turn(j, kept)
        return pltpu.make_async_remote_copy(
            local(p, j, slab_of(j, i, False)), first.at[p, j, i], send1.at[p, j, i], recv1.at[p, j, i],
            device_id={"dp": x_peer if j == 0 else y_peer}, device_id_type=MESH)

    def copy2(p, j):
        return pltpu.make_async_remote_copy(
            first.at[p, j, turn(j, False)], second.at[p, j], send2.at[p, j], recv2.at[p, j],
            device_id={"dp": y_peer if j == 0 else x_peer}, device_id_type=MESH)

    def copy3(j, rr, wait):
        src, dst = first.at[0, j, turn(j, True)].at[pl.ds(rr * 128, 128), :], third.at[c]
        z = 2 * r + j
        me = jnp.logical_and(z == c, r == rr)
        remote = pltpu.make_async_remote_copy(
            src, dst, send3.at[j, rr], recv3.at[c], device_id={"core": rr, "col": z}, device_id_type=MESH)
        if not wait:
            @pl.when(me)
            def _():
                pltpu.make_async_copy(src, dst, recv3.at[c]).start()

        @pl.when(jnp.logical_not(me))
        def _():
            remote.wait_send() if wait else remote.start()

    def step2(p):
        for j in range(2):
            give = turn(j, False)
            wait_for(first.at[p, j, give], recv1.at[p, j, give])
            src, dst = local(p, j, slab_of(j, give, True)), first.at[p, j, give]

            def add_two(t, carry):
                rows = ds(t * 64, 64, 64)
                dst[rows, :] = (src[rows, :].astype(F32) + dst[rows, :].astype(F32)).astype(BF)
                return carry
            lax.fori_loop(0, size // 64, add_two, 0)
            copy2(p, j).start()

    def step3(p):
        for j in range(2):
            kept = turn(j, True)
            wait_for(first.at[p, j, kept], recv1.at[p, j, kept])
            wait_for(second.at[p, j], recv2.at[p, j])
            src, more = local(p, j, slab_of(j, kept, True)), first.at[p, j, kept]
            dst = gsum.at[j] if p else more

            def add_three(t, carry):
                rows = ds(t * 64, 64, 64)
                value = src[rows, :].astype(F32) + more[rows, :].astype(F32) + second[p, j, rows, :].astype(F32)
                dst[rows, :] = value.astype(BF)
                return carry
            lax.fori_loop(0, size // 64, add_three, 0)
            if p == 0:
                for rr in range(2):
                    copy3(j, rr, False)

    def token_copy(q, wait):
        rr, k = c // 2, lax.rem(c, 2)
        sref = out_half.at[:, pl.ds(q * 256, 256)]
        dref = outp.at[ds(k * 2 * half + r * half, half)]
        sem = recv_y.at[k * 2 + r]
        me = jnp.logical_and(rr == r, q == c)
        remote = pltpu.make_async_remote_copy(
            sref, dref, send_y.at[q], sem, device_id={"core": rr, "col": q}, device_id_type=MESH)
        if not wait:
            @pl.when(me)
            def _():
                pltpu.make_async_copy(sref, dref, sem).start()

        @pl.when(jnp.logical_not(me))
        def _():
            remote.wait_send() if wait else remote.start()

    for q in range(4):
        token_copy(q, False)
    far_near = (
        (cols_far, attn), (act_far, act), (mix_far, mix), (wd_far, wd), (slope_far, slope), (wu_far, wu), (two_far, two_grad),
        (normed_far, normed), (hidden_far, hidden), (wo_far, wo))
    loads = [pltpu.make_async_copy(far, near, load.at[i]) for i, (far, near) in enumerate(far_near)]
    for copy in loads:
        copy.start()
    vec[...] = vec_in[...]
    ub[...] = jnp.zeros(ub.shape, F32)
    loads[0].wait()
    loads[1].wait()

    def down_rows(t, carry):
        slab = lax.bitwise_xor(d, 3 - t)
        xt = jnp.transpose(attn[:, ds(slab * size, size)])
        for j in range(2):
            lanes = slice(j * n, (j + 1) * n)
            gd[ds(slab * size, size), lanes] = jnp.dot(xt, act[:, lanes], preferred_element_type=F32).astype(BF)
        for k, sends in ((0, ((0, False), (1, False))), (1, ((1, True),)), (2, ((0, True),))):
            @pl.when(t == k)
            def _():
                for j, kept in sends:
                    copy1(0, j, kept).start()
        return carry
    lax.fori_loop(0, 4, down_rows, 0)
    for copy in loads[2:5]:
        copy.wait()

    def up_rows(t, carry):
        place = ds(t * 256, 256)
        for j in range(2):
            lanes = slice(j * n, (j + 1) * n)
            value = lax.dot_general(mix[place, :], wd[lanes, :], CONTRACT_LAST, preferred_element_type=F32) * slope[place, lanes].astype(F32)
            up_low[place, lanes] = value.astype(BF)
            ub[0:1, lanes] += jnp.sum(value, axis=0, keepdims=True)

        @pl.when(t == 0)
        def _():
            step2(0)
            for kept in (False, True):
                for j in range(2):
                    copy1(1, j, kept).start()
        return carry
    lax.fori_loop(0, 2 * half // 256, up_rows, 0)

    loads[5].wait()

    def mate_rows(t, carry):
        mate_out[ds(t * 256, 256), :] = lax.dot_general(
            up_low[ds(half + t * 256, 256), :], wu[...], CONTRACT_LAST, preferred_element_type=F32)
        return carry
    lax.fori_loop(0, half // 256, mate_rows, 0)
    mate = pltpu.make_async_remote_copy(
        mate_out, mate_in, send_m.at[0], recv_m.at[0], device_id={"core": 1 - r}, device_id_type=MESH)
    mate.start()
    for copy in loads[6:]:
        copy.wait()

    step3(0)
    mate.wait_recv()
    width = mate_in.shape[1]
    vec[0:3, :] = jnp.zeros((3, width), F32)

    def own_rows(t, carry):
        place = ds(t * 256, 256)
        value = lax.dot_general(up_low[place, :], wu[...], CONTRACT_LAST, preferred_element_type=F32)
        value = value + mate_in[place, :] + two_grad[place, :]
        norm = normed[place, :]
        scaled = value * gain[3:4, :]
        mean = jnp.mean(scaled, axis=1, keepdims=True)
        slant = jnp.mean(scaled * norm, axis=1, keepdims=True)
        grad = inverse[place, :] * (scaled - mean - norm * slant)
        one_grad[place, :] = grad
        attn[place, :] = grad.astype(BF)
        vec[0:1, :] += jnp.sum(grad, axis=0, keepdims=True)
        vec[1:2, :] += jnp.sum(value * norm, axis=0, keepdims=True)
        vec[2:3, :] += jnp.sum(value, axis=0, keepdims=True)
        return carry
    lax.fori_loop(0, half // 256, own_rows, 0)
    step2(1)
    pair = pltpu.make_async_remote_copy(
        attn.at[pl.ds(0, half)], attn.at[pl.ds(half, half)], send_m.at[1], recv_m.at[1],
        device_id={"core": 1 - r}, device_id_type=MESH)
    pair.start()

    def weight_rows(t, carry):
        xt = jnp.transpose(hidden[:, ds(t * 256, 256)])
        for j in range(2):
            lanes = slice(j * n, (j + 1) * n)
            gu[ds(t * 256, 256), lanes] = jnp.dot(xt, up_low[:, lanes], preferred_element_type=F32).astype(BF)
        return carry
    lax.fori_loop(0, hidden.shape[1] // 256, weight_rows, 0)
    gu_store = pltpu.make_async_copy(gu, gu_out, store.at[0])
    gu_store.start()
    part = n // 4
    for k in range(4):
        for j in range(2):
            vec[8 + k : 9 + k, ds(r * 2 * part + j * part, part)] = ub[0:1, j * n + k * part : j * n + (k + 1) * part]
    pair.wait_recv()
    attn_store = pltpu.make_async_copy(attn, attn_out, store.at[1])
    attn_store.start()

    def ctx_rows(t, carry):
        place = ds(t * 256, 256)
        do[place, :] = lax.dot_general(attn[place, :], wo[...], CONTRACT_LAST, preferred_element_type=F32).astype(BF)
        return carry
    lax.fori_loop(0, 2 * half // 256, ctx_rows, 0)

    for z in range(4):
        wait_for(third.at[z], recv3.at[z])
    value = (third[0].astype(F32) + third[1].astype(F32)) + (third[2].astype(F32) + third[3].astype(F32))
    early[...] = jnp.transpose(value)
    step3(1)
    for j in range(2):
        for i in range(2):
            for p in range(2):
                copy1(p, j, i).wait_send()
            copy3(j, i, True)
        for p in range(2):
            copy2(p, j).wait_send()
    mate.wait_send()
    pair.wait_send()
    gu_store.wait()
    attn_store.wait()
    for q in range(4):
        token_copy(q, True)
        wait_for(outp.at[pl.ds(q * half, half)], recv_y.at[q])


def middle(out_half, act, cols, mix, slope, wd, two_grad, normed, inverse, gain, vec, hidden, wu, wo):
    dma = pltpu.SemaphoreType.DMA
    vmem, anywhere = pl.BlockSpec(memory_space=pltpu.VMEM), pl.BlockSpec(memory_space=pl.ANY)
    half, width = out_half.shape
    slab = (width // 4, act.shape[1] // 4)
    out = [((4 * half, width // 4), BF), (wu.shape, BF), (cols.shape, BF), ((2 * half, wo.shape[0]), BF), ((half, width), F32), (vec.shape, F32), ((2,) + slab, BF), ((slab[1], width // 8), F32)]
    scratch = [(v.shape, v.dtype) for v in (act, cols, mix, slope, wd, two_grad, normed, hidden, wu, wo)]
    scratch += [(wu.shape, BF), (wu.shape, BF), (slope.shape, BF)]
    scratch += [((8, slope.shape[1]), F32), ((half, width), F32), ((half, width), F32), ((2, 2, 2) + slab, BF), ((2, 2) + slab, BF), ((4, width // 8, slab[1]), BF)]
    sems = [(2, 2, 2), (2, 2, 2), (2, 2), (2, 2), (2, 2), (4,), (4,), (4,), (2,), (2,), (10,), (2,)]
    return pl.pallas_call(
        mid_kernel,
        out_shape=[jax.ShapeDtypeStruct(s, t) for s, t in out],
        in_specs=[vmem] * 3 + [anywhere] * 11,
        out_specs=[anywhere] * 3 + [vmem] * 5,
        scratch_shapes=[pltpu.VMEM(s, t) for s, t in scratch] + [dma(s) for s in sems],
        compiler_params=pltpu.CompilerParams(collective_id=2, has_side_effects=True, vmem_limit_bytes=VMEM_LIMIT),
        name="mid",
    )(inverse, gain, vec, out_half, act, cols, mix, slope, wd, two_grad, normed, hidden, wu, wo)


def back_kernel(
    lse, segk, segq, vec, early, qkv_far, do_far, ctx_far, gu_far, attn_far, x_far, wq_far, one_far, gsum,
    inp, total, rq, ro, ru, rd,
    qkv, do, ctx, gu, attn, x, wq, one_grad, go, inp_low, gq, low, tq, tk, tv, tg, vbuf, mate_out, mate_in, in_half,
    r1q, r1o, r1u, r1v, r2q, r2o, r2u, r2v, r3q, r3o, r3u, r3d, r3v, tall, v1, s4, v2,
    send1, recv1, send2, recv2, send3, recv3, send_i, recv_i, send_v, recv_v, send_w, recv_w, send_m, recv_m, load,
    *, scale,
):
    d, r, c = lax.axis_index("dp"), lax.axis_index("core"), lax.axis_index("col")
    a, b = d // 2, lax.rem(d, 2)
    barrier = pltpu.get_barrier_semaphore()
    for s in range(4):
        for o in range(2):
            if s or o:
                target = {"core": lax.rem(r + o, 2), "col": lax.rem(c + s, 4)}
                pl.semaphore_signal(barrier, inc=1, device_id=target, device_id_type=MESH)
    x_peer, y_peer = lax.bitwise_xor(d, 1), lax.bitwise_xor(d, 2)
    plane = [(p, o) for p in range(4) for o in range(2) if p or o]
    for p, o in plane:
        if p:
            target = {"dp": lax.bitwise_xor(d, p), "core": lax.rem(r + o, 2)}
            pl.semaphore_signal(barrier, inc=1, device_id=target, device_id_type=MESH)
    pl.semaphore_wait(barrier, 13)

    first, second = (r1q, r1o, r1u, None, r1v), (r2q, r2o, r2u, None, r2v)
    third = (r3q, r3o, r3u, r3d, r3v)
    by_rows = (True, False, True, True, True)
    half_up = gu.shape[1] // 4
    result = (rq, ro, ru.at[:, pl.ds(0, half_up)], rd, ru.at[:, pl.ds(half_up, half_up)])
    length, part3q = low.shape[0], low.shape[1] // 2
    part = part3q // 3

    def local(w, j, slab, far=False):
        if w == 0:
            return gq.at[j, slab]
        if w == 1:
            rows, cols = go.shape
            return go.at[pl.ds(j * (rows // 2), rows // 2), ds(slab * (cols // 4), cols // 4)]
        ref, start = gu_far if far else gu, 2 * j * half_up + (half_up if w == 4 else 0)
        return ref.at[ds(slab * (gu.shape[0] // 4), gu.shape[0] // 4), pl.ds(start, half_up)]

    def slab_of(j, i, mine):
        if j == 0:
            return i * 2 + (b if mine else 1 - b)
        return (a if mine else 1 - a) * 2 + i

    def turn(j, kept):
        own = a if j == 0 else b
        return own if kept else 1 - own

    def copy1(w, j, kept):
        i = turn(j, kept)
        return pltpu.make_async_remote_copy(
            local(w, j, slab_of(j, i, False), True), first[w].at[j, i], send1.at[w, j, i], recv1.at[w, j, i],
            device_id={"dp": x_peer if j == 0 else y_peer}, device_id_type=MESH)

    def copy2(w, j):
        return pltpu.make_async_remote_copy(
            first[w].at[j, turn(j, False)], second[w].at[j], send2.at[w, j], recv2.at[w, j],
            device_id={"dp": y_peer if j == 0 else x_peer}, device_id_type=MESH)

    def copy3(w, j, rr, wait):
        src = gsum.at[j] if w == 3 else first[w].at[j, turn(j, True)]
        src = src.at[pl.ds(rr * 128, 128), :] if by_rows[w] else src.at[:, pl.ds(rr * 128, 128)]
        dst = third[w].at[c]
        z = 2 * r + j
        me = jnp.logical_and(z == c, r == rr)
        remote = pltpu.make_async_remote_copy(
            src, dst, send3.at[w, j, rr], recv3.at[w, c], device_id={"core": rr, "col": z}, device_id_type=MESH)
        if not wait:
            @pl.when(me)
            def _():
                pltpu.make_async_copy(src, dst, recv3.at[w, c]).start()

        @pl.when(jnp.logical_not(me))
        def _():
            remote.wait_send() if wait else remote.start()

    def send_first(w, kept):
        for j in range(2):
            copy1(w, j, kept).start()

    def step2(w):
        for j in range(2):
            give = turn(j, False)
            wait_for(first[w].at[j, give], recv1.at[w, j, give])
            src, dst = local(w, j, slab_of(j, give, True)), first[w].at[j, give]

            def body(t, carry):
                rows = ds(t * 64, 64, 64)
                dst[rows, :] = (src[rows, :].astype(F32) + dst[rows, :].astype(F32)).astype(BF)
                return carry
            lax.fori_loop(0, dst.shape[0] // 64, body, 0)
            copy2(w, j).start()

    def step3(w):
        for j in range(2):
            kept = turn(j, True)
            wait_for(first[w].at[j, kept], recv1.at[w, j, kept])
            wait_for(second[w].at[j], recv2.at[w, j])
            src, dst, more = local(w, j, slab_of(j, kept, True)), first[w].at[j, kept], second[w].at[j]

            def body(t, carry):
                rows = ds(t * 64, 64, 64)
                dst[rows, :] = (src[rows, :].astype(F32) + dst[rows, :].astype(F32) + more[rows, :].astype(F32)).astype(BF)
                return carry
            lax.fori_loop(0, dst.shape[0] // 64, body, 0)
            for rr in range(2):
                copy3(w, j, rr, False)

    def finish(w):
        for z in range(4):
            wait_for(third[w].at[z], recv3.at[w, z])

        def body(t, carry):
            rows = ds(t * 64, 64, 64)
            value = (third[w][0, rows, :].astype(F32) + third[w][1, rows, :].astype(F32)) + (
                third[w][2, rows, :].astype(F32) + third[w][3, rows, :].astype(F32))
            if w == 3:
                tall[rows, :] = value
            else:
                result[w][rows, :] = value
            return carry
        lax.fori_loop(0, third[w].shape[1] // 64, body, 0)
        if w == 3:
            cut = tall.shape[1]
            rd[0:cut, :] = early[...]
            rd[cut:, :] = jnp.transpose(tall[...])

    half = in_half.shape[0]

    def token_copy(q, wait):
        rr, k = c // 2, lax.rem(c, 2)
        sref = in_half.at[:, pl.ds(q * 256, 256)]
        dref = inp_low.at[ds(k * 2 * half + r * half, half)]
        sem = recv_i.at[k * 2 + r]
        me = jnp.logical_and(rr == r, q == c)
        remote = pltpu.make_async_remote_copy(
            sref, dref, send_i.at[q], sem, device_id={"core": rr, "col": q}, device_id_type=MESH)
        if not wait:
            @pl.when(me)
            def _():
                pltpu.make_async_copy(sref, dref, sem).start()

        @pl.when(jnp.logical_not(me))
        def _():
            remote.wait_send() if wait else remote.start()

    def vec_z(s):
        z = lax.rem(c + s, 4)
        return pltpu.make_async_remote_copy(
            vbuf.at[:, ds(z * 256, 256)], v1.at[s], send_v.at[s], recv_v.at[s], device_id={"col": z}, device_id_type=MESH)

    def vec_plane(i):
        p, o = plane[i]
        return pltpu.make_async_remote_copy(
            s4, v2.at[i], send_w.at[i], recv_w.at[i],
            device_id={"dp": lax.bitwise_xor(d, p), "core": lax.rem(r + o, 2)}, device_id_type=MESH)

    mate = pltpu.make_async_remote_copy(
        mate_out, mate_in, send_m.at[0], recv_m.at[0], device_id={"core": 1 - r}, device_id_type=MESH)

    send_first(2, False)
    send_first(2, True)
    for j in range(2):
        for rr in range(2):
            copy3(3, j, rr, False)
    far_near = (
        (qkv_far, qkv), (do_far, do), (ctx_far, ctx), (gu_far, gu), (attn_far, attn), (x_far, x), (wq_far, wq), (one_far, one_grad))
    loads = [pltpu.make_async_copy(far, near, load.at[i]) for i, (far, near) in enumerate(far_near)]
    for copy in loads:
        copy.start()
    vbuf[...] = vec[...]
    for copy in loads[:3]:
        copy.wait()

    rows = 256

    def pair(i, carry):
        base = (i // 2) * part3q + lax.rem(i, 2) * 128
        tq[...] = qkv[:, ds(base, 128)]
        tg[...] = do[:, ds(i * 128, 128)]
        prod = jnp.transpose(tg[...].astype(F32) * ctx[:, ds(i * 128, 128)].astype(F32))
        tk[...] = qkv[:, ds(base + part, 128)]
        tv[...] = qkv[:, ds(base + 2 * part, 128)]
        seg_q = segq[0:1, :]
        for h in range(2):
            lanes = slice(h * HEAD_DIM, (h + 1) * HEAD_DIM)
            qh, doh = tq[:, lanes], tg[:, lanes]
            delta = jnp.sum(prod[h * HEAD_DIM : (h + 1) * HEAD_DIM], axis=0, keepdims=True)
            top = lse[i, h : h + 1, :]
            dqt = jnp.zeros((HEAD_DIM, length), F32)
            vsum = jnp.zeros((1, HEAD_DIM), F32)
            for start in range(0, length, rows):
                kh = tk[start : start + rows, lanes]
                vh = tv[start : start + rows, lanes]
                s = lax.dot_general(kh, qh, CONTRACT_LAST, preferred_element_type=F32) * (scale * LOG2E)
                s = jnp.where(segk[start : start + rows, 0:1] == seg_q, s, -1e9 * LOG2E)
                p = jnp.exp2(s - top)
                dp = lax.dot_general(vh, doh, CONTRACT_LAST, preferred_element_type=F32)
                g = (p * (dp - delta)).astype(BF)
                dk = jnp.dot(g, qh, preferred_element_type=F32) * scale
                tk[start : start + rows, lanes] = dk.astype(BF)
                dv = jnp.dot(p.astype(BF), doh, preferred_element_type=F32)
                tv[start : start + rows, lanes] = dv.astype(BF)
                vsum += jnp.sum(dv, axis=0, keepdims=True)
                dqt += jnp.dot(jnp.transpose(kh), g, preferred_element_type=F32)
            dq = jnp.transpose(dqt) * scale
            tq[:, lanes] = dq.astype(BF)
            v1[0, h : h + 1, 0:HEAD_DIM] = jnp.sum(dq, axis=0, keepdims=True)
            v1[0, h : h + 1, 128 : 128 + HEAD_DIM] = vsum
        low[:, ds(base, 128)] = tq[...]
        low[:, ds(base + part, 128)] = tk[...]
        low[:, ds(base + 2 * part, 128)] = tv[...]
        place = ds(r * 2 * part + i * 128, 128)
        vbuf[6:7, place] = jnp.concatenate([v1[0, 0:1, 0:HEAD_DIM], v1[0, 1:2, 0:HEAD_DIM]], axis=1)
        vbuf[7:8, place] = jnp.concatenate([v1[0, 0:1, 128 : 128 + HEAD_DIM], v1[0, 1:2, 128 : 128 + HEAD_DIM]], axis=1)

        @pl.when(i == 0)
        def _():
            for copy in loads[3:]:
                copy.wait()
            step2(2)
            send_first(4, False)
            send_first(4, True)

        @pl.when(i == 2)
        def _():
            step3(2)
            step2(4)
        return carry
    lax.fori_loop(0, do.shape[1] // 128, pair, 0)

    for s in range(1, 4):
        vec_z(s).start()

    def weight_rows(t, carry):
        xt = jnp.transpose(x[:, ds(t * 256, 256)])
        for j in range(2):
            gq[j, t] = jnp.dot(xt, low[:, j * part3q : (j + 1) * part3q], preferred_element_type=F32).astype(BF)
        return carry
    lax.fori_loop(0, 4, weight_rows, 0)
    send_first(0, False)
    send_first(0, True)

    def out_rows(t, carry):
        xt = jnp.transpose(ctx[:, ds(t * 256, 256)])
        go[ds(t * 256, 256), :] = jnp.dot(xt, attn[...], preferred_element_type=F32).astype(BF)
        return carry
    lax.fori_loop(0, ctx.shape[1] // 256, out_rows, 0)
    send_first(1, False)
    send_first(1, True)

    def mate_rows(t, carry):
        mate_out[ds(t * 256, 256), :] = lax.dot_general(
            low[ds(half + t * 256, 256), :], wq[...], CONTRACT_LAST, preferred_element_type=F32)
        return carry
    lax.fori_loop(0, half // 256, mate_rows, 0)
    mate.start()
    step3(4)
    for s in range(1, 4):
        vec_z(s).wait()
    s4[...] = (vbuf[:, ds(c * 256, 256)] + v1[1]) + (v1[2] + v1[3])
    for i in range(7):
        vec_plane(i).start()
    mate.wait_recv()

    def own_rows(t, carry):
        place = ds(t * 256, 256)
        value = lax.dot_general(low[place, :], wq[...], CONTRACT_LAST, preferred_element_type=F32)
        in_half[place, :] = (value + mate_in[place, :] + one_grad[place, :]).astype(BF)
        return carry
    lax.fori_loop(0, half // 256, own_rows, 0)
    for q in range(4):
        token_copy(q, False)
    step2(0)
    step2(1)
    step3(1)
    finish(3)
    for i in range(7):
        vec_plane(i).wait()
    total[...] = ((s4[...] + v2[0]) + (v2[1] + v2[2])) + ((v2[3] + v2[4]) + (v2[5] + v2[6]))
    finish(2)
    finish(4)
    for q in range(4):
        place = pl.ds(q * half, half)
        wait_for(inp_low.at[place], recv_i.at[q])
        inp[place, :] = inp_low[place, :].astype(F32)
    step3(0)
    finish(1)
    finish(0)
    for w in range(5):
        for j in range(2):
            for i in range(2):
                if w != 3:
                    copy1(w, j, i).wait_send()
                copy3(w, j, i, True)
            if w != 3:
                copy2(w, j).wait_send()
    mate.wait_send()
    for q in range(4):
        token_copy(q, True)


def back(x, wq, qkv, do, ctx, lse, segk, segq, one_grad, vec, grads, scale):
    dma = pltpu.SemaphoreType.DMA
    vmem, anywhere = pl.BlockSpec(memory_space=pltpu.VMEM), pl.BlockSpec(memory_space=pl.ANY)
    half, width = one_grad.shape
    far = (qkv, do, ctx, grads[1], grads[0], x, wq, one_grad)
    length, part = 2 * half, width // 4
    rows_q, heads, units = wq.shape[1] // 2, do.shape[1], grads[1].shape[1] // 2
    slab, own, cut = width // 4, width // 8, units // 2
    out = [((4 * half, part), F32), ((vec.shape[0], part), F32), ((own, rows_q), F32), ((heads // 2, own), F32), ((own, units), F32), ((units, own), F32)]
    slabs = [(slab, rows_q), (heads // 2, slab), (slab, cut), (slab, cut)]
    r1, r2 = [(2, 2) + v for v in slabs], [(2,) + v for v in slabs]
    r3 = [(4, own, rows_q), (4, heads // 2, own), (4, own, cut), (4, own, cut), (4, own, cut)]
    scratch = [(v.shape, v.dtype) for v in far] + [((heads, width), BF), ((4 * half, part), BF), ((2, 4, width // 4, wq.shape[1] // 2), BF), (qkv.shape, BF)] + [((length, 128), BF)] * 4
    scratch += [(vec.shape, F32), ((half, width), F32), ((half, width), F32), ((half, width), BF)]
    scratch += [(s, BF) for s in r1 + r2 + r3] + [(r3[3][1:], F32)]
    scratch += [((4, vec.shape[0], part), F32), ((vec.shape[0], part), F32), ((7, vec.shape[0], part), F32)]
    sems = [(5, 2, 2), (5, 2, 2), (5, 2), (5, 2), (5, 2, 2), (5, 4), (4,), (4,), (4,), (4,), (7,), (7,), (1,), (1,), (8,)]
    return pl.pallas_call(
        partial(back_kernel, scale=scale),
        out_shape=[jax.ShapeDtypeStruct(s, t) for s, t in out],
        in_specs=[vmem] * 5 + [anywhere] * 9,
        out_specs=[vmem] * 6,
        scratch_shapes=[pltpu.VMEM(s, t) for s, t in scratch] + [dma(s) for s in sems],
        compiler_params=pltpu.CompilerParams(collective_id=1, has_side_effects=True, vmem_limit_bytes=VMEM_LIMIT),
        name="back",
    )(lse, segk, segq, vec, grads[3], *far, grads[2])


def part_rows(values, groups):
    if groups == 1:
        return values
    rows, cols = values.shape
    return values.reshape(4, groups, 2, rows // (8 * groups), cols).transpose(0, 2, 1, 3, 4).reshape(rows, cols)


def on_device(
    tokens, segment_ids, w_qkv, b_qv, w_out, b_out, norm1_gain, norm1_shift,
    w_up, b_up, w_down, b_down, norm2_gain, norm2_shift, out_grad,
):
    groups = lax.axis_size("rh")
    core, col = lax.axis_index("core"), lax.axis_index("col")
    part = tokens.shape[1]
    scale = 1.0 / math.sqrt(HEAD_DIM)
    wq, wo, wu, wd = w_qkv.reshape(w_qkv.shape[0], 3 * part), w_out, w_up, w_down
    if groups > 1:
        both_rows = ("rh", "core")
        wq, wu = (lax.all_gather(w, both_rows, axis=0, tiled=True) for w in (wq, wu))
        wo, wd = (lax.all_gather(w, both_rows, axis=1, tiled=True) for w in (wo, wd))
        wq, wu = (lax.dynamic_slice_in_dim(w, core * (w.shape[0] // 2), w.shape[0] // 2, 0) for w in (wq, wu))
        wo, wd = (lax.dynamic_slice_in_dim(w, core * (w.shape[1] // 2), w.shape[1] // 2, 1) for w in (wo, wd))
    index = lax.broadcasted_iota(jnp.int32, (16, part), 0)
    par = jnp.where(index < 8, jnp.pad(b_qv, ((0, 14), (0, 0))), jnp.pad(b_up.reshape(4, part), ((8, 4), (0, 0))))
    for k, vector in enumerate((b_out, norm1_gain, norm1_shift, b_down, norm2_gain, norm2_shift)):
        par = jnp.where(index == k + 2, vector[None], par)
    (params, lse, seg_col, seg_row, inverse_one, vec, x, wq, wo, wu, wd, qkv, ctx, normed_one, hidden, activated, slope, output, two_grad,
     mix) = gather(tokens, out_grad, par, segment_ids, (wq, wo, wu, wd), scale)
    x_cols, hidden_cols, mix_cols = x, hidden, mix
    if groups > 1:
        x_cols, hidden_cols, mix_cols = (part_rows(v.T, groups).T for v in (x, hidden, mix))
    output, up_wgrad, attn, ctx_grad, one_grad, vec, down_sum, down_early = middle(
        output, activated, mix_cols, mix, slope, wd, two_grad, normed_one, inverse_one, params, vec, hidden_cols, wu, wo)
    if groups > 1:
        attn = part_rows(attn.T, groups).T
    in_grad, sums, qkv_share, out_share, up_share, down_share = back(
        x_cols, wq, qkv, ctx_grad, ctx, lse, seg_col, seg_row, one_grad, vec, (attn, up_wgrad, down_sum, down_early), scale)
    if groups > 1:
        sums = lax.psum(sums, "rh")
        qkv_share, up_share = (lax.psum_scatter(g, "rh", scatter_dimension=0, tiled=True) for g in (qkv_share, up_share))
        out_share, down_share = (lax.psum_scatter(g, "rh", scatter_dimension=1, tiled=True) for g in (out_share, down_share))
    return (
        output,
        in_grad,
        qkv_share.reshape(qkv_share.shape[0], 3, part),
        sums[6:8],
        out_share,
        sums[0],
        sums[1],
        sums[2],
        up_share,
        sums[8:12].reshape(-1),
        down_share,
        sums[3],
        sums[4],
        sums[5],
    )


def solution(mesh):
    dp, row, col = (mesh.shape[name] for name in ("dp", "row", "col"))
    fine = Mesh(mesh.devices.reshape(dp, row // 2, 2, col), ("dp", "rh", "core", "col"))
    row, every = ("rh", "core"), ("dp", "rh", "core")
    return jax.shard_map(
        on_device,
        mesh=fine,
        in_specs=(
            P(every, "col"), P(every, None), P(row, None, "col"), P(None, "col"), P("col", row), P("col"), P("col"), P("col"),
            P(row, "col"), P("col"), P("col", row), P("col"), P("col"), P("col"), P(every, "col"),
        ),
        out_specs=(
            P(every, "col"), P(every, "col"), P(every, None, "col"), P(None, "col"), P("col", every), P("col"), P("col"),
            P("col"), P(every, "col"), P("col"), P("col", every), P("col"), P("col"), P("col"),
        ),
        check_vma=False,
    )
```
